128 devices in a mesh: wall: 8 (over z_lo, y), gas: 16 (over x, z_hi, core).
Axes of the slice: x: 4, y: 4, z: 4 (z_hi: 2, z_lo: 2; z = z_hi * 2 + z_lo), core: 2. Of those that a mesh axis runs over, the one named last changes fastest.
Arguments:
- gas_state: float32 [3, 4, 1024, 8192], P(None, None, 'wall', 'gas'), may hold values from -8 to 8
- wall_flags: int32 [1024, 64], P('wall', 'gas'), may hold values from 0 to 128
- film_state: float32 [4, 1024, 8192], P(None, 'wall', 'gas'), may hold values from -12 to 12, as said below
- deposit: float32 [1024, 8192], P('wall', 'gas'), may hold values from 0.05 to 1
- owner_map: int32 [8, 16], replicated, may hold values from 0 to 15, each once within a row
Outputs:
- film_out: float32 [4, 1024, 8192], P(None, ('wall', 'gas'))
- cfl: float32 [], replicated
The draws below stay inside these ranges and needn't reach their ends.
Inputs may be any that keep to these rules, and one draw needn't show every extreme that they name: film_state[0] is positive. `owner_map`: each row is a permutation of 0 to 16 - 1.
All inputs are finite; a program needn't handle non-finite values.
Results may differ from the reference program's by a relative error of at most 0.00002.
Values sent between devices are 32-bit elements; how exact they have to be, the bound alone decides.
No kernel may reach another device: no remote copies, remote signals or barrier semaphores. Data moves between devices by JAX's collectives and lax.ppermute only.
A program may use at most 64 MiB of HBM per device.

```python
import math
import jax
import jax.numpy as jnp

LAYERS = 4
SUBSTEPS = 4
WY = 1024
WX = 8192
STRIP = 8
N_WALL = 8
N_GAS = 16


def draw_film_state(key, part):
    subkeys = jax.random.split(key, 5)
    row_share = jnp.arange(WY, dtype=jnp.float32) / max(WY - 1, 1)
    col_share = jnp.arange(WX, dtype=jnp.float32) / max(WX - 1, 1)
    rising = jnp.exp(jnp.log(3.0) * 0.5 * (row_share[:, None] + col_share[None, :]))
    roughness = jax.random.uniform(subkeys[4], (WY, WX), jnp.float32, 0.5, 1.0)
    height = jax.random.uniform(subkeys[0], (WY, WX), jnp.float32, 0.2, 1.5)
    momentum = jnp.clip(jax.random.normal(subkeys[1], (2, WY, WX), jnp.float32), -4.0, 4.0)
    film_heat = jnp.clip(jax.random.normal(subkeys[2], (WY, WX), jnp.float32), -4.0, 4.0)
    momentum = momentum * (rising * roughness)[None]
    return jnp.stack([height, momentum[0], momentum[1], film_heat]).astype(jnp.float32)


def place_ends(result, own_key, least, high):
    place = [jax.random.randint(jax.random.fold_in(own_key, axis), (), 0, length) for axis, length in enumerate(result.shape)]
    main_axis = result.shape.index(max(result.shape))
    next_to = place[:main_axis] + [(place[main_axis] + 1) % result.shape[main_axis]] + place[main_axis + 1:]
    return result.at[tuple(place)].set(least).at[tuple(next_to)].set(high)


def level_of(own_key, extent, cuts, smallest, largest):
    factor_of = 1.0
    for dim, shards_of in cuts:
        heights = jax.random.uniform(jax.random.fold_in(jax.random.fold_in(own_key, 6), dim), (shards_of,), jnp.float32, smallest / len(cuts), largest / len(cuts))
        factor_of = factor_of * jnp.repeat(jnp.exp(heights), extent[dim] // shards_of).reshape((-1,) + (1,) * (len(extent) - 1 - dim))
    return factor_of


def gaussian(stream_key, extent, scale, most, cuts=(), kind=jnp.bfloat16):
    loudness = level_of(stream_key, extent, cuts, -0.22, 0.18) if cuts else 1.0
    drawn = jax.random.normal(stream_key, extent, jnp.float32) * scale * loudness
    return jnp.minimum(jnp.maximum(drawn, -most), most).astype(kind)


def setup_inputs(seed: int = 0) -> dict:
    keys = jax.random.split(jax.random.key(seed), 6)
    gas_state = gaussian(keys[0], (3, LAYERS, WY, WX), 1.5, 8.0, ((2, 8), (3, 16)), jnp.float32)
    wall_flags = place_ends(jax.random.randint(keys[1], (WY, WX // 128), 0, 129), jax.random.fold_in(keys[1], 1), 0, 128).astype(jnp.int32)
    film_state = draw_film_state(jax.random.fold_in(keys[5], 71), 0)
    deposit = jnp.clip(jnp.exp(math.log(1.0) - 2.9957323 * jax.random.uniform(keys[3], (WY, WX), jnp.float32) ** level_of(keys[3], (WY, WX), ((0, 8), (1, 16)), -0.2, 0.2)), 0.05, 1.0)
    owner_map = jax.vmap(lambda own: jax.random.permutation(own, N_GAS))(jax.random.split(keys[4], N_WALL)).reshape((N_WALL, N_GAS)).astype(jnp.int32)
    return {"gas_state": gas_state, "wall_flags": wall_flags, "film_state": film_state, "deposit": deposit, "owner_map": owner_map}


LAYER_WEIGHTS = (0.1, 0.2, 0.3, 0.4)
KAPPA = 0.41
HEIGHT_RATIO = 20.0
SPEED_FLOOR = 0.5
PRANDTL_TURB = 0.85
PRANDTL_JUMP = 3.0
LAMINAR_SHEAR = 0.3
LAMINAR_HEAT = 0.2
FILM_SPREAD = 0.24
FILM_FLOOR = 0.3
FRICTION = 0.5
GRAVITY = 1.0
COURANT = 6.0

def reichardt(scaled_height):
    return jnp.log1p(KAPPA * scaled_height) / KAPPA + 7.8 * (1.0 - jnp.exp(-scaled_height / 11.0) - scaled_height / 11.0 * jnp.exp(-scaled_height / 3.0))

def surface_forcing(filtered, film_heat, attached, deposit):
    along, across, gas_heat = (filtered[0], filtered[1], filtered[2])
    wall_speed = jnp.sqrt(along * along + across * across + SPEED_FLOOR * SPEED_FLOOR)
    scaled_height = jnp.sqrt(HEIGHT_RATIO * wall_speed)
    scaled_speed = reichardt(scaled_height)
    factor = wall_speed / (scaled_speed * scaled_speed)
    contrast = gas_heat - film_heat
    shear_along = jnp.where(attached, factor * along, LAMINAR_SHEAR * along)
    shear_across = jnp.where(attached, factor * across, LAMINAR_SHEAR * across)
    heat_flux = jnp.where(attached, wall_speed * contrast / (PRANDTL_TURB * scaled_speed + PRANDTL_JUMP), LAMINAR_HEAT * contrast)
    return jnp.stack([shear_along, shear_across, heat_flux, deposit])

def peak_speed(film_now):
    thickness = jnp.sqrt(film_now[0] * film_now[0] + FILM_FLOOR * FILM_FLOOR)
    moving = jnp.sqrt(film_now[1] * film_now[1] + film_now[2] * film_now[2])
    return jnp.max(moving / thickness + jnp.sqrt(GRAVITY * thickness))

def advance(padded, forcing, time_step):
    centre = padded[:, 1:-1, 1:-1]
    north_side = padded[:, :-2, 1:-1]
    south_side = padded[:, 2:, 1:-1]
    west_side = padded[:, 1:-1, :-2]
    east_side = padded[:, 1:-1, 2:]
    spread = north_side + south_side + west_side + east_side - 4.0 * centre
    height = centre[0]
    thickness = jnp.sqrt(height * height + FILM_FLOOR * FILM_FLOOR)
    divergence = 0.5 * (east_side[1] - west_side[1]) + 0.5 * (south_side[2] - north_side[2])
    slope_along = 0.5 * (east_side[0] - west_side[0])
    slope_across = 0.5 * (south_side[0] - north_side[0])
    new_height = height + FILM_SPREAD * spread[0] + time_step * (forcing[3] - divergence)
    new_along = centre[1] + FILM_SPREAD * spread[1] + time_step * (forcing[0] - FRICTION * centre[1] / thickness - GRAVITY * height * slope_along)
    new_across = centre[2] + FILM_SPREAD * spread[2] + time_step * (forcing[1] - FRICTION * centre[2] / thickness - GRAVITY * height * slope_across)
    new_heat = centre[3] + FILM_SPREAD * spread[3] + time_step * forcing[2] / thickness
    return jnp.stack([new_height, new_along, new_across, new_heat])

def reference(gas_state, wall_flags, film_state, deposit, owner_map):
    sampled = LAYER_WEIGHTS[0] * gas_state[:, 0]
    for layer in range(1, LAYERS):
        sampled = sampled + LAYER_WEIGHTS[layer] * gas_state[:, layer]
    row_sum = jnp.roll(sampled, 1, 1) + sampled + jnp.roll(sampled, -1, 1)
    filtered = (jnp.roll(row_sum, 1, 2) + row_sum + jnp.roll(row_sum, -1, 2)) / 9.0
    limit = jnp.repeat(wall_flags, 128, axis=1)
    position = jnp.arange(WX, dtype=jnp.int32) % 128
    attached = position[None, :] < limit
    forcing = surface_forcing(filtered, film_state[3], attached, deposit)
    time_step = COURANT / peak_speed(film_state)
    film_now = film_state
    for substep in range(SUBSTEPS):
        film_now = advance(jnp.pad(film_now, ((0, 0), (1, 1), (1, 1)), mode='wrap'), forcing, time_step)
    cfl = time_step * peak_speed(film_now)
    inverse = jnp.argsort(owner_map, axis=1).astype(jnp.int32)
    strips = film_now.reshape(4, N_WALL, N_GAS, STRIP, WX)
    bands = jnp.arange(N_WALL, dtype=jnp.int32)
    picked = strips[:, bands[:, None], inverse]
    return (picked.reshape(4, WY, WX), cfl)
```

```python
import functools

import jax
import jax.numpy as jnp
from jax import lax
from jax.experimental import pallas as pl
from jax.experimental.pallas import tpu as pltpu
from jax.sharding import PartitionSpec as P

SUBSTEPS = 4
LAYER_WEIGHTS = (0.1, 0.2, 0.3, 0.4)
KAPPA = 0.41
HEIGHT_RATIO = 20.0
SPEED_FLOOR = 0.5
PRANDTL_TURB = 0.85
PRANDTL_JUMP = 3.0
LAMINAR_SHEAR = 0.3
LAMINAR_HEAT = 0.2
FILM_SPREAD = 0.24
FILM_FLOOR = 0.3
FRICTION = 0.5
COURANT = 6.0

ROWS = 128
COLS = 512
LANES = 128
TILES = COLS // LANES
HALO = SUBSTEPS
FIELDS = 9
STRIP = 8
RING = ROWS + 16
VMEM_LIMIT = 48 * 1024 * 1024


def lane_iota(shape):
    return lax.broadcasted_iota(jnp.int32, shape, len(shape) - 1)


def film_speed(height, along, across):
    square = height * height + FILM_FLOOR * FILM_FLOOR
    thickness = jnp.sqrt(square)
    moving = jnp.sqrt(along * along + across * across)
    return moving / thickness + jnp.sqrt(thickness)


def pack_columns(rows_of, count, left):
    lane = lane_iota((count, LANES))
    packed = jnp.zeros((count, LANES), jnp.float32)
    for field in range(FIELDS):
        shift = (4 * field) if left else (4 * field + 4)
        value = rows_of(field)
        if shift:
            value = pltpu.roll(value, shift, 1)
        packed = jnp.where((lane >= 4 * field) & (lane < 4 * field + 4), value, packed)
    return packed


def edges_kernel(
    gas, flags, film, deposit, sampled, to_north, to_south, core_pack, chip_pack, peak
):
    lane8 = lane_iota((STRIP, LANES))
    best = jnp.zeros((STRIP, LANES), jnp.float32)
    for tile in range(TILES):
        cols = slice(tile * LANES, (tile + 1) * LANES)
        for field in range(3):
            value = LAYER_WEIGHTS[0] * gas[field, 0, :, cols]
            for layer in range(1, 4):
                value = value + LAYER_WEIGHTS[layer] * gas[field, layer, :, cols]
            sampled[field, :, cols] = value
        speed = film_speed(film[0, :, cols], film[1, :, cols], film[2, :, cols])
        for row in range(0, ROWS, STRIP):
            best = jnp.maximum(best, speed[row : row + STRIP])
    peak[...] = jnp.broadcast_to(jnp.max(best, keepdims=True), (ROWS, LANES))

    def attached(rows, tile):
        count = flags[rows, tile : tile + 1]
        return jnp.where(lane_iota((count.shape[0], LANES)) < count, 1.0, 0.0)

    def value_of(field, rows, tile):
        cols = slice(tile * LANES, (tile + 1) * LANES)
        if field < 4:
            return film[field, rows, cols]
        if field < 7:
            return sampled[field - 4, rows, cols]
        if field == 7:
            return deposit[rows, cols]
        return attached(rows, tile)

    for field in range(FIELDS):
        for tile in range(TILES):
            cols = slice(tile * LANES, (tile + 1) * LANES)
            out = slice(4 * field, 4 * field + 4)
            to_north[out, cols] = value_of(field, slice(0, 4), tile)
            to_south[out, cols] = value_of(field, slice(ROWS - 4, ROWS), tile)

    even = lax.rem(lax.axis_index("gas"), 2) == 0
    every = slice(0, ROWS)
    west = pack_columns(lambda f: value_of(f, every, 0), ROWS, True)
    east = pack_columns(lambda f: value_of(f, every, TILES - 1), ROWS, False)
    core_pack[4 : 4 + ROWS, :] = jnp.where(even, east, west)
    chip_pack[4 : 4 + ROWS, :] = jnp.where(even, west, east)


def corners_kernel(from_north, from_south, core_in, chip_in, core_pack, chip_pack):
    even = lax.rem(lax.axis_index("gas"), 2) == 0
    core_pack[4 : 4 + ROWS, :] = core_in[4 : 4 + ROWS, :]
    chip_pack[4 : 4 + ROWS, :] = chip_in[4 : 4 + ROWS, :]
    for source, start in ((from_north, 0), (from_south, 4 + ROWS)):
        west = pack_columns(lambda f: source[4 * f : 4 * f + 4, 0:LANES], 4, True)
        east = pack_columns(
            lambda f: source[4 * f : 4 * f + 4, COLS - LANES : COLS], 4, False
        )
        core_pack[start : start + 4, :] = jnp.where(even, east, west)
        chip_pack[start : start + 4, :] = jnp.where(even, west, east)


def shifted_lanes(tiles):
    lane = lane_iota(tiles[0].shape)
    plus = [pltpu.roll(t, 1, 1) for t in tiles]
    minus = [pltpu.roll(t, LANES - 1, 1) for t in tiles]
    count = len(tiles)
    west = [jnp.where(lane == 0, plus[i - 1], plus[i]) for i in range(count)]
    east = [
        jnp.where(lane == LANES - 1, minus[(i + 1) % count], minus[i])
        for i in range(count)
    ]
    return west, east


def film_kernel(
    owner_map,
    film,
    sampled,
    flags,
    deposit,
    from_north,
    from_south,
    core_pack,
    chip_pack,
    peaks,
    out,
    peak,
    ring_a,
    ring_b,
    gas_ring,
    force,
):
    count = TILES + 1
    inner = slice(8, 8 + ROWS)
    even = lax.rem(lax.axis_index("gas"), 2) == 0
    wall = lax.axis_index("wall")
    step = COURANT / jnp.max(peaks[...])

    refs = [ring_a.at[f] for f in range(4)] + [gas_ring.at[f] for f in range(3)]
    refs += [force.at[3], force.at[0]]
    for field in range(FIELDS):
        ref = refs[field]
        for tile in range(TILES):
            cols = slice(tile * LANES, (tile + 1) * LANES)
            if field < 4:
                ref[tile, inner, :] = film[field, :, cols]
            elif field < 7:
                ref[tile, inner, :] = sampled[field - 4, :, cols]
            elif field == 7:
                ref[tile, inner, :] = deposit[:, cols]
            else:
                ref[tile, inner, :] = jnp.where(
                    lane_iota((ROWS, LANES)) < flags[:, tile : tile + 1], 1.0, 0.0
                )
            ref[tile, 4:8, :] = from_north[4 * field : 4 * field + 4, cols]
            ref[tile, 8 + ROWS : 12 + ROWS, :] = from_south[
                4 * field : 4 * field + 4, cols
            ]
    lane = lane_iota((ROWS + 8, LANES))
    core, chip = core_pack[...], chip_pack[...]
    east_side = jnp.where(even, core, chip)
    west_side = jnp.where(even, chip, core)
    for field in range(FIELDS):
        value = jnp.where(
            lane < LANES // 2,
            pltpu.roll(east_side, (LANES - 4 * field) % LANES, 1),
            pltpu.roll(west_side, (LANES - 4 - 4 * field) % LANES, 1),
        )
        refs[field][TILES, 4 : 12 + ROWS, :] = value

    def forcing_rows(index, carry):
        row = 4 + 8 * index
        here = pl.ds(row, STRIP)
        filtered = []
        for field in range(3):
            summed = [
                gas_ring[field, t, pl.ds(row - 1, STRIP), :]
                + gas_ring[field, t, here, :]
                + gas_ring[field, t, pl.ds(row + 1, STRIP), :]
                for t in range(count)
            ]
            west, east = shifted_lanes(summed)
            filtered.append(
                [(west[t] + summed[t] + east[t]) * (1.0 / 9.0) for t in range(count)]
            )
        for t in range(count):
            along, across = filtered[0][t], filtered[1][t]
            contrast = filtered[2][t] - ring_a[3, t, here, :]
            on_wall = force[0, t, here, :] > 0.5
            speed = jnp.sqrt(along * along + across * across + SPEED_FLOOR * SPEED_FLOOR)
            scaled = jnp.sqrt(HEIGHT_RATIO * speed)
            uplus = jnp.log(1.0 + KAPPA * scaled) * (1.0 / KAPPA) + 7.8 * (
                1.0
                - jnp.exp(scaled * (-1.0 / 11.0))
                - scaled * (1.0 / 11.0) * jnp.exp(scaled * (-1.0 / 3.0))
            )
            factor = jnp.where(on_wall, speed / (uplus * uplus), LAMINAR_SHEAR)
            heat = jnp.where(
                on_wall, speed / (PRANDTL_TURB * uplus + PRANDTL_JUMP), LAMINAR_HEAT
            )
            force[0, t, here, :] = step * (factor * along)
            force[1, t, here, :] = step * (factor * across)
            force[2, t, here, :] = step * (heat * contrast)
            force[3, t, here, :] = step * force[3, t, here, :]
        return carry

    lax.fori_loop(0, 17, forcing_rows, 0)

    half = 0.5 * step

    def advance(source, row):
        here = pl.ds(row, STRIP)
        centre, total, wests, easts, norths, souths = [], [], [], [], [], []
        for field in range(4):
            middle = [source[field, t, here, :] for t in range(count)]
            north = [source[field, t, pl.ds(row - 1, STRIP), :] for t in range(count)]
            south = [source[field, t, pl.ds(row + 1, STRIP), :] for t in range(count)]
            west, east = shifted_lanes(middle)
            centre.append(middle)
            wests.append(west)
            easts.append(east)
            norths.append(north)
            souths.append(south)
        news = []
        for t in range(count):
            spread = [
                (1.0 - 4.0 * FILM_SPREAD) * centre[f][t]
                + FILM_SPREAD
                * ((norths[f][t] + souths[f][t]) + (wests[f][t] + easts[f][t]))
                for f in range(4)
            ]
            height = centre[0][t]
            inverse = lax.rsqrt(height * height + FILM_FLOOR * FILM_FLOOR)
            drag = (FRICTION * step) * inverse
            slope = half * height
            height_new = (
                spread[0]
                + force[3, t, here, :]
                - half * ((easts[1][t] - wests[1][t]) + (souths[2][t] - norths[2][t]))
            )
            along_new = (
                spread[1]
                + force[0, t, here, :]
                - drag * centre[1][t]
                - slope * (easts[0][t] - wests[0][t])
            )
            across_new = (
                spread[2]
                + force[1, t, here, :]
                - drag * centre[2][t]
                - slope * (souths[0][t] - norths[0][t])
            )
            heat_new = spread[3] + force[2, t, here, :] * inverse
            news.append((height_new, along_new, across_new, heat_new))
        return news

    def middle_rows(source, target):
        def body(index, carry):
            row = 4 + 8 * index
            news = advance(source, row)
            for t in range(count):
                for field in range(4):
                    target[field, t, pl.ds(row, STRIP), :] = news[t][field]
            return carry

        lax.fori_loop(0, 17, body, 0)

    middle_rows(ring_a, ring_b)
    middle_rows(ring_b, ring_a)
    middle_rows(ring_a, ring_b)

    def last_rows(index, best):
        row = pl.multiple_of(8 + 8 * index, 8)
        news = advance(ring_b, row)
        place = pl.multiple_of(owner_map[wall, index] * STRIP, STRIP)
        for t in range(TILES):
            for field in range(4):
                out[field, pl.ds(place, STRIP), t * LANES : (t + 1) * LANES] = news[t][
                    field
                ]
            best = jnp.maximum(best, film_speed(*news[t][:3]))
        return best

    best = lax.fori_loop(0, 16, last_rows, jnp.zeros((STRIP, LANES), jnp.float32))
    peak[...] = jnp.broadcast_to(step * jnp.max(best, keepdims=True), (ROWS, LANES))


def vmem(count):
    return [pl.BlockSpec(memory_space=pltpu.VMEM)] * count


def shape(*dims):
    return jax.ShapeDtypeStruct(dims, jnp.float32)


def per_device(gas_state, wall_flags, film_state, deposit, owner_map):
    params = pltpu.CompilerParams(vmem_limit_bytes=VMEM_LIMIT)
    sampled, to_north, to_south, core_main, chip_main, peak = pl.pallas_call(
        edges_kernel,
        out_shape=(
            shape(3, ROWS, COLS),
            shape(4 * FIELDS, COLS),
            shape(4 * FIELDS, COLS),
            shape(ROWS + 8, LANES),
            shape(ROWS + 8, LANES),
            shape(ROWS, LANES),
        ),
        in_specs=vmem(4),
        out_specs=tuple(vmem(6)),
        compiler_params=params,
        name="edges",
    )(gas_state, wall_flags, film_state, deposit)

    walls, gases = lax.axis_size("wall"), lax.axis_size("gas")
    both = ("wall", "gas")
    peaks = lax.all_to_all(peak, both, split_axis=0, concat_axis=0, tiled=True)
    down = [(i, (i + 1) % walls) for i in range(walls)]
    up = [(j, i) for i, j in down]
    from_north = lax.ppermute(to_south, "wall", down)
    from_south = lax.ppermute(to_north, "wall", up)
    core_pack, chip_pack = pl.pallas_call(
        corners_kernel,
        out_shape=(shape(ROWS + 8, LANES), shape(ROWS + 8, LANES)),
        in_specs=vmem(4),
        out_specs=tuple(vmem(2)),
        compiler_params=params,
        name="corners",
    )(from_north, from_south, core_main, chip_main)
    partner = [(i, i ^ 1) for i in range(gases)]
    outer = [(i, (i + 1) % gases if i % 2 else (i - 1) % gases) for i in range(gases)]
    core_pack = lax.ppermute(core_pack, "gas", partner)
    chip_pack = lax.ppermute(chip_pack, "gas", outer)

    ring = (4, TILES + 1, RING, LANES)
    film, local = pl.pallas_call(
        film_kernel,
        out_shape=(shape(4, ROWS, COLS), shape(ROWS, LANES)),
        in_specs=[pl.BlockSpec(memory_space=pltpu.SMEM)] + vmem(9),
        out_specs=tuple(vmem(2)),
        scratch_shapes=[
            pltpu.VMEM(ring, jnp.float32),
            pltpu.VMEM(ring, jnp.float32),
            pltpu.VMEM((3,) + ring[1:], jnp.float32),
            pltpu.VMEM(ring, jnp.float32),
        ],
        compiler_params=params,
        name="film",
    )(
        owner_map,
        film_state,
        sampled,
        wall_flags,
        deposit,
        from_north,
        from_south,
        core_pack,
        chip_pack,
        peaks,
    )
    film_out = lax.all_to_all(film, "gas", split_axis=1, concat_axis=2, tiled=True)
    cfl = jnp.max(lax.all_to_all(local, both, split_axis=0, concat_axis=0, tiled=True))
    return film_out, cfl


def solution(mesh):
    return jax.shard_map(
        per_device,
        mesh=mesh,
        in_specs=(
            P(None, None, "wall", "gas"),
            P("wall", "gas"),
            P(None, "wall", "gas"),
            P("wall", "gas"),
            P(),
        ),
        out_specs=(P(None, ("wall", "gas"), None), P()),
        check_vma=False,
    )
```

```python
import jax
import jax.numpy as jnp
from jax import lax
from jax.experimental import pallas as pl
from jax.experimental.pallas import tpu as pltpu
from jax.sharding import PartitionSpec as P


LAYER_WEIGHTS = (0.1, 0.2, 0.3, 0.4)
KAPPA = 0.41
HEIGHT_RATIO = 20.0
SPEED_FLOOR = 0.5
PRANDTL_TURB = 0.85
PRANDTL_JUMP = 3.0
LAMINAR_SHEAR = 0.3
LAMINAR_HEAT = 0.2
FILM_SPREAD = 0.24
FILM_FLOOR = 0.3
FRICTION = 0.5
COURANT = 6.0

ROWS = 128
COLS = 512
LANES = 128
TILES = COLS // LANES
FIELDS = 9
STRIP = 8
RING = ROWS + 24
VMEM_LIMIT = 48 * 1024 * 1024


def lane_iota(shape):
    return lax.broadcasted_iota(jnp.int32, shape, len(shape) - 1)


def film_speed(height, along, across):
    square = height * height + FILM_FLOOR * FILM_FLOOR
    thickness = jnp.sqrt(square)
    moving = jnp.sqrt(along * along + across * across)
    return moving / thickness + jnp.sqrt(thickness)


def pack_columns(rows_of, count, left):
    lane = lane_iota((count, LANES))
    packed = jnp.zeros((count, LANES), jnp.float32)
    for field in range(FIELDS):
        shift = (4 * field) if left else (4 * field + 4)
        value = rows_of(field)
        if shift:
            value = pltpu.roll(value, shift, 1)
        packed = jnp.where((lane >= 4 * field) & (lane < 4 * field + 4), value, packed)
    return packed


def edges_kernel(
    gas, flags, film, deposit, sampled, to_north, to_south, core_pack, chip_pack, peak
):
    lane8 = lane_iota((STRIP, LANES))
    best = jnp.zeros((STRIP, LANES), jnp.float32)
    for tile in range(TILES):
        cols = slice(tile * LANES, (tile + 1) * LANES)
        for field in range(3):
            value = LAYER_WEIGHTS[0] * gas[field, 0, :, cols]
            for layer in range(1, 4):
                value = value + LAYER_WEIGHTS[layer] * gas[field, layer, :, cols]
            sampled[field, :, cols] = value
        speed = film_speed(film[0, :, cols], film[1, :, cols], film[2, :, cols])
        for row in range(0, ROWS, STRIP):
            best = jnp.maximum(best, speed[row : row + STRIP])
    peak[...] = jnp.broadcast_to(jnp.max(best, keepdims=True), (ROWS, LANES))

    def attached(rows, tile):
        count = flags[rows, tile : tile + 1]
        return jnp.where(lane_iota((count.shape[0], LANES)) < count, 1.0, 0.0)

    def value_of(field, rows, tile):
        cols = slice(tile * LANES, (tile + 1) * LANES)
        if field < 4:
            return film[field, rows, cols]
        if field < 7:
            return sampled[field - 4, rows, cols]
        if field == 7:
            return deposit[rows, cols]
        return attached(rows, tile)

    for field in range(FIELDS):
        for tile in range(TILES):
            cols = slice(tile * LANES, (tile + 1) * LANES)
            out = slice(4 * field, 4 * field + 4)
            to_north[out, cols] = value_of(field, slice(0, 4), tile)
            to_south[out, cols] = value_of(field, slice(ROWS - 4, ROWS), tile)

    even = lax.rem(lax.axis_index("gas"), 2) == 0
    every = slice(0, ROWS)
    west = pack_columns(lambda f: value_of(f, every, 0), ROWS, True)
    east = pack_columns(lambda f: value_of(f, every, TILES - 1), ROWS, False)
    core_pack[4 : 4 + ROWS, :] = jnp.where(even, east, west)
    chip_pack[4 : 4 + ROWS, :] = jnp.where(even, west, east)


def corners_kernel(from_north, from_south, core_in, chip_in, core_pack, chip_pack):
    even = lax.rem(lax.axis_index("gas"), 2) == 0
    core_pack[4 : 4 + ROWS, :] = core_in[4 : 4 + ROWS, :]
    chip_pack[4 : 4 + ROWS, :] = chip_in[4 : 4 + ROWS, :]
    for source, start in ((from_north, 0), (from_south, 4 + ROWS)):
        west = pack_columns(lambda f: source[4 * f : 4 * f + 4, 0:LANES], 4, True)
        east = pack_columns(
            lambda f: source[4 * f : 4 * f + 4, COLS - LANES : COLS], 4, False
        )
        core_pack[start : start + 4, :] = jnp.where(even, east, west)
        chip_pack[start : start + 4, :] = jnp.where(even, west, east)


def shifted_lanes(tiles):
    lane = lane_iota(tiles[0].shape)
    plus = [pltpu.roll(t, 1, 1) for t in tiles]
    minus = [pltpu.roll(t, LANES - 1, 1) for t in tiles]
    count = len(tiles)
    west = [jnp.where(lane == 0, plus[i - 1], plus[i]) for i in range(count)]
    east = [
        jnp.where(lane == LANES - 1, minus[(i + 1) % count], minus[i])
        for i in range(count)
    ]
    return west, east


def film_kernel(
    owner_map,
    film,
    sampled,
    flags,
    deposit,
    from_north,
    from_south,
    core_pack,
    chip_pack,
    peaks,
    out,
    ring_a,
    ring_b,
    gas_ring,
    force,
):
    count = TILES + 1
    inner = slice(8, 8 + ROWS)
    even = lax.rem(lax.axis_index("gas"), 2) == 0
    wall = lax.axis_index("wall")
    step = COURANT / jnp.max(peaks[...])

    refs = [ring_a.at[f] for f in range(4)] + [gas_ring.at[f] for f in range(3)]
    refs += [force.at[3], force.at[0]]
    for field in range(FIELDS):
        ref = refs[field]
        for tile in range(TILES):
            cols = slice(tile * LANES, (tile + 1) * LANES)
            if field < 4:
                ref[tile, inner, :] = film[field, :, cols]
            elif field < 7:
                ref[tile, inner, :] = sampled[field - 4, :, cols]
            elif field == 7:
                ref[tile, inner, :] = deposit[:, cols]
            else:
                ref[tile, inner, :] = jnp.where(
                    lane_iota((ROWS, LANES)) < flags[:, tile : tile + 1], 1.0, 0.0
                )
            ref[tile, 4:8, :] = from_north[4 * field : 4 * field + 4, cols]
            ref[tile, 8 + ROWS : 12 + ROWS, :] = from_south[
                4 * field : 4 * field + 4, cols
            ]
    lane = lane_iota((ROWS + 8, LANES))
    core, chip = core_pack[...], chip_pack[...]
    east_side = jnp.where(even, core, chip)
    west_side = jnp.where(even, chip, core)
    for field in range(FIELDS):
        value = jnp.where(
            lane < LANES // 2,
            pltpu.roll(east_side, (LANES - 4 * field) % LANES, 1),
            pltpu.roll(west_side, (LANES - 4 - 4 * field) % LANES, 1),
        )
        refs[field][TILES, 4 : 12 + ROWS, :] = value

    def forcing_rows(index, carry):
        row = 4 + 8 * index
        here = pl.ds(row, STRIP)
        filtered = []
        for field in range(3):
            summed = [
                gas_ring[field, t, pl.ds(row - 1, STRIP), :]
                + gas_ring[field, t, here, :]
                + gas_ring[field, t, pl.ds(row + 1, STRIP), :]
                for t in range(count)
            ]
            west, east = shifted_lanes(summed)
            filtered.append(
                [(west[t] + summed[t] + east[t]) * (1.0 / 9.0) for t in range(count)]
            )
        for t in range(count):
            along, across = filtered[0][t], filtered[1][t]
            contrast = filtered[2][t] - ring_a[3, t, here, :]
            on_wall = force[0, t, here, :] > 0.5
            speed = jnp.sqrt(along * along + across * across + SPEED_FLOOR * SPEED_FLOOR)
            scaled = jnp.sqrt(HEIGHT_RATIO * speed)
            uplus = jnp.log(1.0 + KAPPA * scaled) * (1.0 / KAPPA) + 7.8 * (
                1.0
                - jnp.exp(scaled * (-1.0 / 11.0))
                - scaled * (1.0 / 11.0) * jnp.exp(scaled * (-1.0 / 3.0))
            )
            factor = jnp.where(on_wall, speed / (uplus * uplus), LAMINAR_SHEAR)
            heat = jnp.where(
                on_wall, speed / (PRANDTL_TURB * uplus + PRANDTL_JUMP), LAMINAR_HEAT
            )
            force[0, t, here, :] = step * (factor * along)
            force[1, t, here, :] = step * (factor * across)
            force[2, t, here, :] = step * (heat * contrast)
            force[3, t, here, :] = step * force[3, t, here, :]
        return carry

    grouped(3, 18, forcing_rows, 0)

    half = 0.5 * step

    def advance(source, row):
        here = pl.ds(row, STRIP)
        centre, wests, easts, norths, souths = [], [], [], [], []
        for field in range(4):
            middle = [source[field, t, here, :] for t in range(count)]
            north = [source[field, t, pl.ds(row - 1, STRIP), :] for t in range(count)]
            south = [source[field, t, pl.ds(row + 1, STRIP), :] for t in range(count)]
            west, east = shifted_lanes(middle)
            centre.append(middle)
            wests.append(west)
            easts.append(east)
            norths.append(north)
            souths.append(south)
        news = []
        for t in range(count):
            spread = [
                (1.0 - 4.0 * FILM_SPREAD) * centre[f][t]
                + FILM_SPREAD
                * ((norths[f][t] + souths[f][t]) + (wests[f][t] + easts[f][t]))
                for f in range(4)
            ]
            height = centre[0][t]
            inverse = lax.rsqrt(height * height + FILM_FLOOR * FILM_FLOOR)
            drag = (FRICTION * step) * inverse
            slope = half * height
            height_new = (
                spread[0]
                + force[3, t, here, :]
                - half * ((easts[1][t] - wests[1][t]) + (souths[2][t] - norths[2][t]))
            )
            along_new = (
                spread[1]
                + force[0, t, here, :]
                - drag * centre[1][t]
                - slope * (easts[0][t] - wests[0][t])
            )
            across_new = (
                spread[2]
                + force[1, t, here, :]
                - drag * centre[2][t]
                - slope * (souths[0][t] - norths[0][t])
            )
            heat_new = spread[3] + force[2, t, here, :] * inverse
            news.append((height_new, along_new, across_new, heat_new))
        return news

    def middle_rows(source, target):
        def body(index, carry):
            row = 4 + 8 * index
            news = advance(source, row)
            for t in range(count):
                for field in range(4):
                    target[field, t, pl.ds(row, STRIP), :] = news[t][field]
            return carry

        grouped(6, 18, body, 0)

    middle_rows(ring_a, ring_b)
    middle_rows(ring_b, ring_a)
    middle_rows(ring_a, ring_b)

    def last_rows(index, best):
        row = pl.multiple_of(8 + 8 * index, 8)
        news = advance(ring_b, row)
        place = owner_map[wall, index]
        for t in range(TILES):
            for field in range(4):
                out[place, field * TILES + t] = news[t][field]
            best = jnp.maximum(best, film_speed(*news[t][:3]))
        return best

    best = grouped(4, 16, last_rows, jnp.zeros((STRIP, LANES), jnp.float32))
    top = jnp.broadcast_to(step * jnp.max(best, keepdims=True), (STRIP, LANES))
    for owner in range(ROWS // STRIP):
        out[owner, 4 * TILES] = top


def band_peak_kernel(pieces, peak):
    best = pieces[0, 0]
    for source in range(1, pieces.shape[0]):
        best = jnp.maximum(best, pieces[source, 0])
    peak[...] = best


def strips_kernel(pieces, out):
    for source in range(pieces.shape[0]):
        for t in range(TILES):
            start = source * COLS + t * LANES
            out[0, :, start : start + LANES] = pieces[source, t]


def grouped(unroll, total, body, carry):
    whole = total // unroll

    def many(index, carry):
        for k in range(unroll):
            carry = body(index * unroll + k, carry)
        return carry

    carry = lax.fori_loop(0, whole, many, carry)
    for index in range(whole * unroll, total):
        carry = body(index, carry)
    return carry


def vmem(count):
    return [pl.BlockSpec(memory_space=pltpu.VMEM)] * count


def shape(*dims):
    return jax.ShapeDtypeStruct(dims, jnp.float32)


def coupling_step(gas_state, wall_flags, film_state, deposit, owner_map):
    params = pltpu.CompilerParams(vmem_limit_bytes=VMEM_LIMIT)
    sampled, to_north, to_south, core_main, chip_main, peak = pl.pallas_call(
        edges_kernel,
        out_shape=(
            shape(3, ROWS, COLS),
            shape(4 * FIELDS, COLS),
            shape(4 * FIELDS, COLS),
            shape(ROWS + 8, LANES),
            shape(ROWS + 8, LANES),
            shape(ROWS, LANES),
        ),
        in_specs=vmem(4),
        out_specs=tuple(vmem(6)),
        compiler_params=params,
        name="edges",
    )(gas_state, wall_flags, film_state, deposit)

    walls, gases = lax.axis_size("wall"), lax.axis_size("gas")
    both = ("wall", "gas")
    peaks = lax.all_to_all(peak, both, split_axis=0, concat_axis=0, tiled=True)
    down = [(i, (i + 1) % walls) for i in range(walls)]
    up = [(j, i) for i, j in down]
    from_north = lax.ppermute(to_south, "wall", down)
    from_south = lax.ppermute(to_north, "wall", up)
    core_pack, chip_pack = pl.pallas_call(
        corners_kernel,
        out_shape=(shape(ROWS + 8, LANES), shape(ROWS + 8, LANES)),
        in_specs=vmem(4),
        out_specs=tuple(vmem(2)),
        compiler_params=params,
        name="corners",
    )(from_north, from_south, core_main, chip_main)
    partner = [(i, i ^ 1) for i in range(gases)]
    outer = [(i, (i + 1) % gases if i % 2 else (i - 1) % gases) for i in range(gases)]
    core_pack = lax.ppermute(core_pack, "gas", partner)
    chip_pack = lax.ppermute(chip_pack, "gas", outer)

    ring = (4, TILES + 1, RING, LANES)
    pieces = pl.pallas_call(
        film_kernel,
        out_shape=shape(gases, 4 * TILES + 1, STRIP, LANES),
        in_specs=[pl.BlockSpec(memory_space=pltpu.SMEM)] + vmem(9),
        out_specs=vmem(1)[0],
        scratch_shapes=[
            pltpu.VMEM(ring, jnp.float32),
            pltpu.VMEM(ring, jnp.float32),
            pltpu.VMEM((3,) + ring[1:], jnp.float32),
            pltpu.VMEM(ring, jnp.float32),
        ],
        compiler_params=params,
        name="film",
    )(
        owner_map,
        film_state,
        sampled,
        wall_flags,
        deposit,
        from_north,
        from_south,
        core_pack,
        chip_pack,
        peaks,
    )
    pieces = lax.all_to_all(pieces, "gas", split_axis=0, concat_axis=0, tiled=True)
    band_peak = pl.pallas_call(
        band_peak_kernel,
        out_shape=shape(STRIP, LANES),
        grid=(1,),
        in_specs=[
            pl.BlockSpec((gases, 1, STRIP, LANES), lambda i: (0, 4 * TILES, 0, 0))
        ],
        out_specs=pl.BlockSpec((STRIP, LANES), lambda i: (0, 0)),
        name="band_peak",
    )(pieces)
    cfl = jnp.max(
        lax.all_to_all(band_peak, "wall", split_axis=0, concat_axis=0, tiled=True)
    )
    film_out = pl.pallas_call(
        strips_kernel,
        out_shape=shape(4, STRIP, gases * COLS),
        grid=(4,),
        in_specs=[pl.BlockSpec((gases, TILES, STRIP, LANES), lambda i: (0, i, 0, 0))],
        out_specs=pl.BlockSpec((1, STRIP, gases * COLS), lambda i: (i, 0, 0)),
        cost_estimate=pl.CostEstimate(
            flops=0, bytes_accessed=2 << 20, transcendentals=0
        ),
        name="strips",
    )(pieces)
    return film_out, cfl


def solution(mesh):
    return jax.shard_map(
        coupling_step,
        mesh=mesh,
        in_specs=(
            P(None, None, "wall", "gas"),
            P("wall", "gas"),
            P(None, "wall", "gas"),
            P("wall", "gas"),
            P(),
        ),
        out_specs=(P(None, ("wall", "gas"), None), P()),
        check_vma=False,
    )
```

```python
import jax
import jax.numpy as jnp
from jax import lax
from jax.experimental import pallas as pl
from jax.experimental.pallas import tpu as pltpu
from jax.sharding import PartitionSpec as P


LAYER_WEIGHTS = (0.1, 0.2, 0.3, 0.4)
KAPPA = 0.41
HEIGHT_RATIO = 20.0
SPEED_FLOOR = 0.5
PRANDTL_TURB = 0.85
PRANDTL_JUMP = 3.0
LAMINAR_SHEAR = 0.3
LAMINAR_HEAT = 0.2
FILM_SPREAD = 0.24
FILM_FLOOR = 0.3
FRICTION = 0.5
COURANT = 6.0

ROWS = 128
COLS = 512
LANES = 128
TILES = COLS // LANES
FIELDS = 9
STRIP = 8
RING = ROWS + 24
VMEM_LIMIT = 24 << 20


def lane_iota(shape):
    return lax.broadcasted_iota(jnp.int32, shape, len(shape) - 1)


def film_speed(height, along, across):
    square = height * height + FILM_FLOOR * FILM_FLOOR
    thickness = jnp.sqrt(square)
    moving = jnp.sqrt(along * along + across * across)
    return moving / thickness + jnp.sqrt(thickness)


def pack_columns(rows_of, count, left):
    lane = lane_iota((count, LANES))
    packed = jnp.zeros((count, LANES), jnp.float32)
    for field in range(FIELDS):
        shift = (4 * field) if left else (4 * field + 4)
        value = rows_of(field)
        if shift:
            value = pltpu.roll(value, shift, 1)
        packed = jnp.where((lane >= 4 * field) & (lane < 4 * field + 4), value, packed)
    return packed


def sample(gas, field, rows, cols):
    value = LAYER_WEIGHTS[0] * gas[field, 0, rows, cols]
    for layer in range(1, 4):
        value = value + LAYER_WEIGHTS[layer] * gas[field, layer, rows, cols]
    return value


def flag_columns(flags_by_row):
    flags = flags_by_row.astype(jnp.float32)
    return jnp.transpose(jnp.concatenate([flags, flags], axis=0))


def attached_rows(columns, rows, tile):
    count = columns[rows, tile : tile + 1]
    lane = lane_iota((count.shape[0], LANES)).astype(jnp.float32)
    return jnp.where(lane < count, 1.0, 0.0)


def edges_kernel(
    gas_hbm,
    flags_hbm,
    film_hbm,
    deposit_hbm,
    sampled,
    to_north,
    to_south,
    core_pack,
    chip_pack,
    peak,
    film,
    gas,
    deposit,
    flags,
    sems,
):
    copies = [
        pltpu.make_async_copy(film_hbm, film, sems.at[0]),
        pltpu.make_async_copy(gas_hbm.at[0], gas.at[0], sems.at[1]),
        pltpu.make_async_copy(gas_hbm.at[1], gas.at[1], sems.at[2]),
        pltpu.make_async_copy(gas_hbm.at[2], gas.at[2], sems.at[3]),
        pltpu.make_async_copy(flags_hbm, flags, sems.at[4]),
        pltpu.make_async_copy(deposit_hbm, deposit, sems.at[5]),
    ]
    for copy in copies:
        copy.start()
    tiles = [slice(tile * LANES, (tile + 1) * LANES) for tile in range(TILES)]
    copies[0].wait()
    best = jnp.zeros((STRIP, LANES), jnp.float32)
    for cols in tiles:
        speed = film_speed(film[0, :, cols], film[1, :, cols], film[2, :, cols])
        for row in range(0, ROWS, STRIP):
            best = jnp.maximum(best, speed[row : row + STRIP])
    peak[...] = jnp.broadcast_to(jnp.max(best, keepdims=True), (ROWS, LANES))
    every = slice(0, ROWS)
    for field in range(3):
        copies[1 + field].wait()
        for cols in tiles:
            sampled[field, :, cols] = sample(gas, field, every, cols)
    copies[4].wait()
    copies[5].wait()
    columns = flag_columns(flags[...])

    def value_of(field, rows, tile):
        if field < 4:
            return film[field, rows, tiles[tile]]
        if field < 7:
            return sampled[field - 4, rows, tiles[tile]]
        if field == 7:
            return deposit[rows, tiles[tile]]
        return attached_rows(columns, rows, tile)

    for field in range(FIELDS):
        for tile, cols in enumerate(tiles):
            target = slice(4 * field, 4 * field + 4)
            to_north[target, cols] = value_of(field, slice(0, 4), tile)
            to_south[target, cols] = value_of(field, slice(ROWS - 4, ROWS), tile)

    even = lax.rem(lax.axis_index("gas"), 2) == 0
    west = pack_columns(lambda f: value_of(f, every, 0), ROWS, True)
    east = pack_columns(lambda f: value_of(f, every, TILES - 1), ROWS, False)
    core_pack[4 : 4 + ROWS, :] = jnp.where(even, east, west)
    chip_pack[4 : 4 + ROWS, :] = jnp.where(even, west, east)


def corners_kernel(from_north, from_south, core_in, chip_in, core_pack, chip_pack):
    even = lax.rem(lax.axis_index("gas"), 2) == 0
    core_pack[4 : 4 + ROWS, :] = core_in[4 : 4 + ROWS, :]
    chip_pack[4 : 4 + ROWS, :] = chip_in[4 : 4 + ROWS, :]
    for source, start in ((from_north, 0), (from_south, 4 + ROWS)):
        west = pack_columns(lambda f: source[4 * f : 4 * f + 4, 0:LANES], 4, True)
        east = pack_columns(
            lambda f: source[4 * f : 4 * f + 4, COLS - LANES : COLS], 4, False
        )
        core_pack[start : start + 4, :] = jnp.where(even, east, west)
        chip_pack[start : start + 4, :] = jnp.where(even, west, east)


def shifted_lanes(tiles):
    lane = lane_iota(tiles[0].shape)
    plus = [pltpu.roll(t, 1, 1) for t in tiles]
    minus = [pltpu.roll(t, LANES - 1, 1) for t in tiles]
    count = len(tiles)
    west = [jnp.where(lane == 0, plus[i - 1], plus[i]) for i in range(count)]
    east = [
        jnp.where(lane == LANES - 1, minus[(i + 1) % count], minus[i])
        for i in range(count)
    ]
    return west, east


def wall_forcing(filtered, film_heat, attached):
    along, across, gas_heat = filtered
    contrast = gas_heat - film_heat
    on_wall = attached > 0.5
    square = along * along + across * across + SPEED_FLOOR * SPEED_FLOOR
    speed = square * lax.rsqrt(square)
    height = HEIGHT_RATIO * speed
    scaled = height * lax.rsqrt(height)
    uplus = jnp.log(1.0 + KAPPA * scaled) * (1.0 / KAPPA) + 7.8 * (
        1.0
        - jnp.exp(scaled * (-1.0 / 11.0))
        - scaled * (1.0 / 11.0) * jnp.exp(scaled * (-1.0 / 3.0))
    )
    factor = jnp.where(on_wall, speed / (uplus * uplus), LAMINAR_SHEAR)
    heat = jnp.where(
        on_wall, speed / (PRANDTL_TURB * uplus + PRANDTL_JUMP), LAMINAR_HEAT
    )
    return factor * along, factor * across, heat * contrast


def inside_kernel(
    sampled,
    film_hbm,
    flags_hbm,
    deposit_hbm,
    from_north,
    from_south,
    ring,
    force,
    seam,
    gas_ring,
    attached,
    film,
    flags,
    deposit,
    sems,
):
    pairs = (
        (flags_hbm, flags),
        (film_hbm, film),
        (deposit_hbm, deposit),
    )
    copies = [
        pltpu.make_async_copy(source, target, sems.at[index])
        for index, (source, target) in enumerate(pairs)
    ]
    for copy in copies:
        copy.start()
    for copy in copies:
        copy.wait()
    inner = slice(8, 8 + ROWS)
    columns = flag_columns(flags[...])
    refs = [ring.at[f] for f in range(4)] + [gas_ring.at[f] for f in range(3)]
    refs += [force.at[3], attached]
    for field in range(FIELDS):
        ref = refs[field]
        for tile in range(TILES):
            cols = slice(tile * LANES, (tile + 1) * LANES)
            if field < 4:
                ref[tile, inner, :] = film[field, :, cols]
            elif field < 7:
                ref[tile, inner, :] = sampled[field - 4, :, cols]
            elif field == 7:
                ref[tile, inner, :] = deposit[:, cols]
            else:
                ref[tile, inner, :] = attached_rows(columns, slice(0, ROWS), tile)
            ref[tile, 4:8, :] = from_north[4 * field : 4 * field + 4, cols]
            ref[tile, 8 + ROWS : 12 + ROWS, :] = from_south[
                4 * field : 4 * field + 4, cols
            ]
    every = slice(4, 12 + ROWS)
    lane = lane_iota((ROWS + 8, LANES))
    for index, ref in enumerate(refs[4:7] + [refs[3], attached]):
        seam[index, every, :] = jnp.where(
            lane < LANES // 4,
            ref[0, every, :],
            pltpu.roll(ref[TILES - 1, every, :], LANES // 2, 1),
        )

    def forcing_rows(index, carry):
        row = 4 + 8 * index
        here = pl.ds(row, STRIP)
        filtered = []
        for field in range(3):
            summed = [
                gas_ring[field, t, pl.ds(row - 1, STRIP), :]
                + gas_ring[field, t, here, :]
                + gas_ring[field, t, pl.ds(row + 1, STRIP), :]
                for t in range(TILES)
            ]
            west, east = shifted_lanes(summed)
            filtered.append(
                [(west[t] + summed[t] + east[t]) * (1.0 / 9.0) for t in range(TILES)]
            )
        for t in range(TILES):
            result = wall_forcing(
                [filtered[f][t] for f in range(3)],
                ring[3, t, here, :],
                attached[t, here, :],
            )
            for field in range(3):
                force[field, t, here, :] = result[field]
        return carry

    grouped(3, 18, forcing_rows, 0)


def film_kernel(
    owner_map,
    ring,
    force_in,
    seam_in,
    core_pack,
    chip_pack,
    peaks,
    out,
    halo,
    seam,
    ring_a,
    ring_b,
    force,
):
    count = TILES + 1
    even = lax.rem(lax.axis_index("gas"), 2) == 0
    wall = lax.axis_index("wall")
    step = COURANT / jnp.max(peaks[...])

    every = slice(4, 12 + ROWS)
    lane = lane_iota((ROWS + 8, LANES))
    core, chip = core_pack[...], chip_pack[...]
    east_side = jnp.where(even, core, chip)
    west_side = jnp.where(even, chip, core)
    for field in (0, 1, 2, 3, 7):
        value = jnp.where(
            lane < LANES // 2,
            pltpu.roll(east_side, (LANES - 4 * field) % LANES, 1),
            pltpu.roll(west_side, (LANES - 4 - 4 * field) % LANES, 1),
        )
        if field == 7:
            force[3, TILES, every, :] = step * value
        else:
            halo[field, every, :] = value
    for index, field in enumerate((4, 5, 6, 3, 8)):
        east = pltpu.roll(east_side, (LANES // 2 - 4 * field) % LANES, 1)
        west = pltpu.roll(west_side, (LANES - 4 - 4 * field) % LANES, 1)
        value = jnp.where(
            (lane >= LANES // 2) & (lane < LANES // 2 + 4), east, seam_in[index, every, :]
        )
        seam[index, every, :] = jnp.where(lane >= LANES - 4, west, value)

    def seam_rows(index, carry):
        row = 4 + 8 * index
        here = pl.ds(row, STRIP)
        lanes = lane_iota((STRIP, LANES))
        filtered = []
        for field in range(3):
            summed = (
                seam[field, pl.ds(row - 1, STRIP), :]
                + seam[field, here, :]
                + seam[field, pl.ds(row + 1, STRIP), :]
            )
            west, east = pltpu.roll(summed, 1, 1), pltpu.roll(summed, LANES - 1, 1)
            filtered.append((west + summed + east) * (1.0 / 9.0))
        result = wall_forcing(filtered, seam[3, here, :], seam[4, here, :])
        for field in range(3):
            first = step * result[field]
            last = pltpu.roll(first, LANES // 2, 1)
            force[field, TILES, here, :] = jnp.where(lanes < LANES // 2, last, first)
            for t in range(TILES):
                value = step * force_in[field, t, here, :]
                if t == 0:
                    value = jnp.where(lanes == 0, first, value)
                if t == TILES - 1:
                    value = jnp.where(lanes == LANES - 1, last, value)
                force[field, t, here, :] = value
        for t in range(TILES):
            force[3, t, here, :] = step * force_in[3, t, here, :]
        return carry

    grouped(6, 18, seam_rows, 0)

    half = 0.5 * step

    def advance(load, row):
        here = pl.ds(row, STRIP)
        centre, wests, easts, norths, souths = [], [], [], [], []
        for field in range(4):
            middle = [load(field, t, here) for t in range(count)]
            north = [load(field, t, pl.ds(row - 1, STRIP)) for t in range(count)]
            south = [load(field, t, pl.ds(row + 1, STRIP)) for t in range(count)]
            west, east = shifted_lanes(middle)
            centre.append(middle)
            wests.append(west)
            easts.append(east)
            norths.append(north)
            souths.append(south)
        news = []
        for t in range(count):
            spread = [
                (1.0 - 4.0 * FILM_SPREAD) * centre[f][t]
                + FILM_SPREAD
                * ((norths[f][t] + souths[f][t]) + (wests[f][t] + easts[f][t]))
                for f in range(4)
            ]
            height = centre[0][t]
            inverse = lax.rsqrt(height * height + FILM_FLOOR * FILM_FLOOR)
            drag = (FRICTION * step) * inverse
            slope = half * height
            height_new = (
                spread[0]
                + force[3, t, here, :]
                - half * ((easts[1][t] - wests[1][t]) + (souths[2][t] - norths[2][t]))
            )
            along_new = (
                spread[1]
                + force[0, t, here, :]
                - drag * centre[1][t]
                - slope * (easts[0][t] - wests[0][t])
            )
            across_new = (
                spread[2]
                + force[1, t, here, :]
                - drag * centre[2][t]
                - slope * (souths[0][t] - norths[0][t])
            )
            heat_new = spread[3] + force[2, t, here, :] * inverse
            news.append((height_new, along_new, across_new, heat_new))
        return news

    def middle_rows(source, target):
        def body(index, carry):
            row = 4 + 8 * index
            news = advance(source, row)
            for t in range(count):
                for field in range(4):
                    target[field, t, pl.ds(row, STRIP), :] = news[t][field]
            return carry

        grouped(6, 18, body, 0)

    def first_load(field, t, rows):
        return ring[field, t, rows, :] if t < TILES else halo[field, rows, :]

    def load_from(source):
        return lambda field, t, rows: source[field, t, rows, :]

    middle_rows(first_load, ring_a)
    middle_rows(load_from(ring_a), ring_b)
    middle_rows(load_from(ring_b), ring_a)

    def last_rows(index, best):
        row = pl.multiple_of(8 + 8 * index, 8)
        news = advance(load_from(ring_a), row)
        place = owner_map[wall, index]
        for t in range(TILES):
            for field in range(4):
                out[place, field * TILES + t] = news[t][field]
            best = jnp.maximum(best, film_speed(*news[t][:3]))
        return best

    best = grouped(4, 16, last_rows, jnp.zeros((STRIP, LANES), jnp.float32))
    top = jnp.broadcast_to(step * jnp.max(best, keepdims=True), (STRIP, LANES))
    for owner in range(ROWS // STRIP):
        out[owner, 4 * TILES] = top


def band_peak_kernel(pieces, peak):
    best = pieces[0, 4 * TILES]
    for source in range(1, pieces.shape[0]):
        best = jnp.maximum(best, pieces[source, 4 * TILES])
    peak[...] = best


def strips_kernel(pieces, out):
    first = pl.program_id(0) * TILES
    for source in range(pieces.shape[0]):
        for t in range(TILES):
            start = source * COLS + t * LANES
            out[0, :, start : start + LANES] = pieces[source, first + t]


def grouped(unroll, total, body, carry):
    whole = total // unroll

    def many(index, carry):
        for k in range(unroll):
            carry = body(index * unroll + k, carry)
        return carry

    carry = lax.fori_loop(0, whole, many, carry)
    for index in range(whole * unroll, total):
        carry = body(index, carry)
    return carry


def in_hbm(*arrays):
    return [pltpu.with_memory_space_constraint(a, pltpu.HBM) for a in arrays]


def vmem(count):
    return [pl.BlockSpec(memory_space=pltpu.VMEM)] * count


def shape(*dims):
    return jax.ShapeDtypeStruct(dims, jnp.float32)


def coupling_step(gas_state, wall_flags, film_state, deposit, owner_map):
    params = pltpu.CompilerParams(vmem_limit_bytes=VMEM_LIMIT)
    tail = pltpu.CompilerParams(vmem_limit_bytes=8 << 20)
    flags = jnp.transpose(wall_flags)
    sampled, to_north, to_south, core_main, chip_main, peak = pl.pallas_call(
        edges_kernel,
        out_shape=(
            shape(3, ROWS, COLS),
            shape(4 * FIELDS, COLS),
            shape(4 * FIELDS, COLS),
            shape(ROWS + 8, LANES),
            shape(ROWS + 8, LANES),
            shape(ROWS, LANES),
        ),
        in_specs=[pl.BlockSpec(memory_space=pltpu.HBM)] * 4,
        out_specs=tuple(vmem(6)),
        scratch_shapes=[
            pltpu.VMEM((4, ROWS, COLS), jnp.float32),
            pltpu.VMEM((3, 4, ROWS, COLS), jnp.float32),
            pltpu.VMEM((ROWS, COLS), jnp.float32),
            pltpu.VMEM((TILES, ROWS), jnp.int32),
            pltpu.SemaphoreType.DMA((6,)),
        ],
        compiler_params=pltpu.CompilerParams(vmem_limit_bytes=VMEM_LIMIT),
        name="edges",
    )(*in_hbm(gas_state, flags, film_state, deposit))

    walls, gases = lax.axis_size("wall"), lax.axis_size("gas")
    both = ("wall", "gas")
    peaks = lax.all_to_all(peak, both, split_axis=0, concat_axis=0, tiled=True)
    down = [(i, (i + 1) % walls) for i in range(walls)]
    up = [(j, i) for i, j in down]
    from_north = lax.ppermute(to_south, "wall", down)
    from_south = lax.ppermute(to_north, "wall", up)
    core_pack, chip_pack = pl.pallas_call(
        corners_kernel,
        out_shape=(shape(ROWS + 8, LANES), shape(ROWS + 8, LANES)),
        in_specs=vmem(4),
        out_specs=tuple(vmem(2)),
        compiler_params=params,
        name="corners",
    )(from_north, from_south, core_main, chip_main)
    partner = [(i, i ^ 1) for i in range(gases)]
    outer = [(i, (i + 1) % gases if i % 2 else (i - 1) % gases) for i in range(gases)]
    core_pack = lax.ppermute(core_pack, "gas", partner)
    chip_pack = lax.ppermute(chip_pack, "gas", outer)

    inner = (4, TILES, RING, LANES)
    ring, force, seam = pl.pallas_call(
        inside_kernel,
        out_shape=(shape(*inner), shape(*inner), shape(5, RING, LANES)),
        in_specs=vmem(1) + [pl.BlockSpec(memory_space=pltpu.HBM)] * 3 + vmem(2),
        out_specs=tuple(vmem(3)),
        scratch_shapes=[
            pltpu.VMEM((3,) + inner[1:], jnp.float32),
            pltpu.VMEM(inner[1:], jnp.float32),
            pltpu.VMEM((4, ROWS, COLS), jnp.float32),
            pltpu.VMEM((TILES, ROWS), jnp.int32),
            pltpu.VMEM((ROWS, COLS), jnp.float32),
            pltpu.SemaphoreType.DMA((3,)),
        ],
        compiler_params=pltpu.CompilerParams(vmem_limit_bytes=24 << 20),
        cost_estimate=pl.CostEstimate(
            flops=20 << 20, bytes_accessed=8 << 20, transcendentals=1 << 19
        ),
        name="inside",
    )(sampled, *in_hbm(film_state, flags, deposit), from_north, from_south)
    outer_ring = (4, TILES + 1, RING, LANES)
    pieces = pl.pallas_call(
        film_kernel,
        out_shape=shape(gases, 4 * TILES + 1, STRIP, LANES),
        in_specs=[pl.BlockSpec(memory_space=pltpu.SMEM)] + vmem(6),
        out_specs=vmem(1)[0],
        scratch_shapes=[
            pltpu.VMEM((4, RING, LANES), jnp.float32),
            pltpu.VMEM((5, RING, LANES), jnp.float32),
            pltpu.VMEM(outer_ring, jnp.float32),
            pltpu.VMEM(outer_ring, jnp.float32),
            pltpu.VMEM(outer_ring, jnp.float32),
        ],
        compiler_params=pltpu.CompilerParams(vmem_limit_bytes=24 << 20),
        name="film",
    )(owner_map, ring, force, seam, core_pack, chip_pack, peaks)
    pieces = lax.all_to_all(pieces, "gas", split_axis=0, concat_axis=0, tiled=True)
    band_peak = pl.pallas_call(
        band_peak_kernel,
        out_shape=shape(STRIP, LANES),
        in_specs=vmem(1),
        out_specs=vmem(1)[0],
        compiler_params=tail,
        name="band_peak",
    )(pieces)
    cfl = jnp.max(
        lax.all_to_all(band_peak, "wall", split_axis=0, concat_axis=0, tiled=True)
    )
    film_out = pl.pallas_call(
        strips_kernel,
        out_shape=shape(4, STRIP, gases * COLS),
        grid=(4,),
        in_specs=vmem(1),
        compiler_params=tail,
        out_specs=pl.BlockSpec((1, STRIP, gases * COLS), lambda i: (i, 0, 0)),
        cost_estimate=pl.CostEstimate(
            flops=0, bytes_accessed=2 << 20, transcendentals=0
        ),
        name="strips",
    )(pieces)
    return film_out, cfl


def solution(mesh):
    return jax.shard_map(
        coupling_step,
        mesh=mesh,
        in_specs=(
            P(None, None, "wall", "gas"),
            P("wall", "gas"),
            P(None, "wall", "gas"),
            P("wall", "gas"),
            P(),
        ),
        out_specs=(P(None, ("wall", "gas"), None), P()),
        check_vma=False,
    )
```

```python
import jax
import jax.numpy as jnp
from jax import lax
from jax.experimental import pallas as pl
from jax.experimental.pallas import tpu as pltpu
from jax.sharding import PartitionSpec as P


LAYER_WEIGHTS = (0.1, 0.2, 0.3, 0.4)
KAPPA = 0.41
HEIGHT_RATIO = 20.0
SPEED_FLOOR = 0.5
PRANDTL_TURB = 0.85
PRANDTL_JUMP = 3.0
LAMINAR_SHEAR = 0.3
LAMINAR_HEAT = 0.2
FILM_SPREAD = 0.24
FILM_FLOOR = 0.3
FRICTION = 0.5
COURANT = 6.0

ROWS = 128
COLS = 512
LANES = 128
TILES = COLS // LANES
FIELDS = 9
STRIP = 8
RING = ROWS + 16
AHEAD = 8
VMEM_LIMIT = 24 << 20


def lane_iota(shape):
    return lax.broadcasted_iota(jnp.int32, shape, len(shape) - 1)


def film_speed(height, along, across):
    square = height * height + FILM_FLOOR * FILM_FLOOR
    thickness = jnp.sqrt(square)
    moving = jnp.sqrt(along * along + across * across)
    return moving / thickness + jnp.sqrt(thickness)


def pack_columns(rows_of, count, left):
    lane = lane_iota((count, LANES))
    packed = jnp.zeros((count, LANES), jnp.float32)
    for field in range(FIELDS):
        shift = (4 * field) if left else (4 * field + 4)
        value = rows_of(field)
        if shift:
            value = pltpu.roll(value, shift, 1)
        packed = jnp.where((lane >= 4 * field) & (lane < 4 * field + 4), value, packed)
    return packed


def sample(gas, field, rows, cols):
    value = LAYER_WEIGHTS[0] * gas[field, 0, rows, cols]
    for layer in range(1, 4):
        value = value + LAYER_WEIGHTS[layer] * gas[field, layer, rows, cols]
    return value


def flag_columns(flags_by_row):
    flags = flags_by_row.astype(jnp.float32)
    return jnp.transpose(jnp.concatenate([flags, flags], axis=0))


def attached_rows(columns, rows, tile):
    count = columns[rows, tile : tile + 1]
    lane = lane_iota((count.shape[0], LANES)).astype(jnp.float32)
    return jnp.where(lane < count, 1.0, 0.0)


def edges_kernel(
    gas_hbm,
    flags_hbm,
    film_hbm,
    deposit_hbm,
    gas_ring,
    to_north,
    to_south,
    core_pack,
    chip_pack,
    peak,
    film,
    gas,
    deposit,
    flags,
    sems,
):
    copies = [
        pltpu.make_async_copy(film_hbm, film, sems.at[0]),
        pltpu.make_async_copy(flags_hbm, flags, sems.at[1]),
        pltpu.make_async_copy(deposit_hbm, deposit, sems.at[2]),
        pltpu.make_async_copy(gas_hbm.at[0], gas.at[0], sems.at[3]),
        pltpu.make_async_copy(gas_hbm.at[1], gas.at[1], sems.at[4]),
        pltpu.make_async_copy(gas_hbm.at[2], gas.at[2], sems.at[5]),
    ]
    for copy in copies:
        copy.start()
    tiles = [slice(tile * LANES, (tile + 1) * LANES) for tile in range(TILES)]
    every = slice(0, ROWS)
    even = lax.rem(lax.axis_index("gas"), 2) == 0
    lane = lane_iota((ROWS, LANES))

    def send(field, value_of):
        target = slice(4 * field, 4 * field + 4)
        for tile, cols in enumerate(tiles):
            to_north[target, cols] = value_of(slice(0, 4), tile)
            to_south[target, cols] = value_of(slice(ROWS - 4, ROWS), tile)
        west = value_of(every, 0)
        if field:
            west = pltpu.roll(west, 4 * field, 1)
        east = pltpu.roll(value_of(every, TILES - 1), 4 * field + 4, 1)
        here = (lane >= 4 * field) & (lane < 4 * field + 4)
        for pack, value in (
            (core_pack, jnp.where(even, east, west)),
            (chip_pack, jnp.where(even, west, east)),
        ):
            old = pack[4 : 4 + ROWS, :] if field else jnp.zeros_like(value)
            pack[4 : 4 + ROWS, :] = jnp.where(here, value, old)

    copies[0].wait()
    best = jnp.zeros((STRIP, LANES), jnp.float32)
    for cols in tiles:
        speed = film_speed(film[0, :, cols], film[1, :, cols], film[2, :, cols])
        for row in range(0, ROWS, STRIP):
            best = jnp.maximum(best, speed[row : row + STRIP])
    peak[...] = jnp.broadcast_to(jnp.max(best, keepdims=True), (ROWS, LANES))
    for field in range(4):
        send(field, lambda rows, tile, f=field: film[f, rows, tiles[tile]])
    copies[1].wait()
    columns = flag_columns(flags[...])
    send(8, lambda rows, tile: attached_rows(columns, rows, tile))
    copies[2].wait()
    send(7, lambda rows, tile: deposit[rows, tiles[tile]])
    for field in range(3):
        copies[3 + field].wait()
        for tile, cols in enumerate(tiles):
            gas_ring[field, tile, 16 : 16 + ROWS, :] = sample(gas, field, every, cols)
        send(
            4 + field,
            lambda rows, tile, f=field: gas_ring[
                f, tile, 16 + rows.start : 16 + rows.stop, :
            ],
        )


def corners_kernel(from_north, from_south, core_in, chip_in, core_pack, chip_pack):
    even = lax.rem(lax.axis_index("gas"), 2) == 0
    core_pack[4 : 4 + ROWS, :] = core_in[4 : 4 + ROWS, :]
    chip_pack[4 : 4 + ROWS, :] = chip_in[4 : 4 + ROWS, :]
    for source, start in ((from_north, 0), (from_south, 4 + ROWS)):
        west = pack_columns(lambda f: source[4 * f : 4 * f + 4, 0:LANES], 4, True)
        east = pack_columns(
            lambda f: source[4 * f : 4 * f + 4, COLS - LANES : COLS], 4, False
        )
        core_pack[start : start + 4, :] = jnp.where(even, east, west)
        chip_pack[start : start + 4, :] = jnp.where(even, west, east)


def shifted_lanes(tiles):
    lane = lane_iota(tiles[0].shape)
    plus = [pltpu.roll(t, 1, 1) for t in tiles]
    minus = [pltpu.roll(t, LANES - 1, 1) for t in tiles]
    count = len(tiles)
    west = [jnp.where(lane == 0, plus[i - 1], plus[i]) for i in range(count)]
    east = [
        jnp.where(lane == LANES - 1, minus[(i + 1) % count], minus[i])
        for i in range(count)
    ]
    return west, east


def wall_forcing(filtered, film_heat, attached):
    along, across, gas_heat = filtered
    contrast = gas_heat - film_heat
    on_wall = attached > 0.5
    square = along * along + across * across + SPEED_FLOOR * SPEED_FLOOR
    speed = square * lax.rsqrt(square)
    height = HEIGHT_RATIO * speed
    scaled = height * lax.rsqrt(height)
    uplus = jnp.log(1.0 + KAPPA * scaled) * (1.0 / KAPPA) + 7.8 * (
        1.0
        - jnp.exp(scaled * (-1.0 / 11.0))
        - scaled * (1.0 / 11.0) * jnp.exp(scaled * (-1.0 / 3.0))
    )
    factor = jnp.where(on_wall, speed / (uplus * uplus), LAMINAR_SHEAR)
    heat = jnp.where(
        on_wall, speed / (PRANDTL_TURB * uplus + PRANDTL_JUMP), LAMINAR_HEAT
    )
    return factor * along, factor * across, heat * contrast


def inside_kernel(
    gas_in,
    film_hbm,
    flags_hbm,
    deposit_hbm,
    from_north,
    from_south,
    ring,
    spray,
    seam,
    force,
    attached,
    flags,
    sems,
):
    del gas_in
    tiles = [slice(tile * LANES, (tile + 1) * LANES) for tile in range(TILES)]
    inner = slice(8, 8 + ROWS)
    flags_copy = pltpu.make_async_copy(flags_hbm, flags, sems.at[5, 0])
    flags_copy.start()
    arriving = {}
    for field in (3, 0, 1, 2, 4):
        arriving[field] = []
        for tile, cols in enumerate(tiles):
            if field < 4:
                source, target = film_hbm.at[field, :, cols], ring.at[field, tile, inner]
            else:
                source, target = deposit_hbm.at[:, cols], spray.at[tile, inner]
            copy = pltpu.make_async_copy(source, target, sems.at[field, tile])
            copy.start()
            arriving[field].append(copy)

    refs = [ring.at[f] for f in range(4)]
    refs += [force.at[f, :, pl.ds(AHEAD, RING)] for f in range(3)]
    refs += [spray, attached]
    for field, ref in enumerate(refs):
        target = slice(4 * field, 4 * field + 4)
        for tile, cols in enumerate(tiles):
            ref[tile, 4:8, :] = from_north[target, cols]
            ref[tile, 8 + ROWS : 12 + ROWS, :] = from_south[target, cols]
    flags_copy.wait()
    columns = flag_columns(flags[...])
    for tile in range(TILES):
        attached[tile, inner, :] = attached_rows(columns, slice(0, ROWS), tile)
    every = slice(4, 12 + ROWS)
    lane = lane_iota((ROWS + 8, LANES))

    def ends(ref, shift):
        first, last = ref[0, every, :], ref[TILES - 1, every, :]
        first = pltpu.roll(first, shift, 1) if shift else first
        last = pltpu.roll(last, LANES // 2 + shift, 1)
        return jnp.where(lane < shift + LANES // 4, first, last)

    for index in range(2):
        left = ends(refs[4 + 2 * index], 0)
        right = ends(refs[5] if index == 0 else attached, LANES // 4)
        inside = (lane < 8) | ((lane >= 48) & (lane < 72))
        seam[index, every, :] = jnp.where(inside, left, right)
    for copy in arriving[3]:
        copy.wait()

    def forcing_rows(index, carry):
        row = 4 + 8 * index
        here = pl.ds(row, STRIP)
        filtered = []
        for field in range(3):
            summed = [
                force[field, t, pl.ds(row + AHEAD - 1, STRIP), :]
                + force[field, t, pl.ds(row + AHEAD, STRIP), :]
                + force[field, t, pl.ds(row + AHEAD + 1, STRIP), :]
                for t in range(TILES)
            ]
            west, east = shifted_lanes(summed)
            filtered.append(
                [(west[t] + summed[t] + east[t]) * (1.0 / 9.0) for t in range(TILES)]
            )
        for t in range(TILES):
            result = wall_forcing(
                [filtered[f][t] for f in range(3)],
                ring[3, t, here, :],
                attached[t, here, :],
            )
            for field in range(3):
                force[field, t, here, :] = result[field]
        return carry

    grouped(4, 17, forcing_rows, 0)
    for field in (0, 1, 2, 4):
        for copy in arriving[field]:
            copy.wait()


def film_kernel(
    owner_map,
    ring,
    spray,
    seam_in,
    force_in,
    core_pack,
    chip_pack,
    peaks,
    out,
    halo,
    seam,
    ring_a,
    ring_b,
    force,
):
    count = TILES + 1
    even = lax.rem(lax.axis_index("gas"), 2) == 0
    wall = lax.axis_index("wall")
    step = COURANT / jnp.max(peaks[...])

    every = slice(4, 12 + ROWS)
    lane = lane_iota((ROWS + 8, LANES))
    core, chip = core_pack[...], chip_pack[...]
    east_side = jnp.where(even, core, chip)
    west_side = jnp.where(even, chip, core)
    for field in (0, 1, 2, 3, 7):
        value = jnp.where(
            lane < LANES // 2,
            pltpu.roll(east_side, (LANES - 4 * field) % LANES, 1),
            pltpu.roll(west_side, (LANES - 4 - 4 * field) % LANES, 1),
        )
        if field == 7:
            force[3, TILES, every, :] = step * value
        else:
            halo[field, every, :] = value
    film_ends = jnp.where(
        lane < LANES // 4,
        ring[3, 0, every, :],
        pltpu.roll(ring[3, TILES - 1, every, :], LANES // 2, 1),
    )
    first, second = seam_in[0, every, :], seam_in[1, every, :]
    quarter = LANES - LANES // 4
    own = (
        first,
        pltpu.roll(first, quarter, 1),
        second,
        film_ends,
        pltpu.roll(second, quarter, 1),
    )
    for index, field in enumerate((4, 5, 6, 3, 8)):
        east = pltpu.roll(east_side, (LANES // 2 - 4 * field) % LANES, 1)
        west = pltpu.roll(west_side, (LANES - 4 - 4 * field) % LANES, 1)
        value = jnp.where(
            (lane >= LANES // 2) & (lane < LANES // 2 + 4), east, own[index]
        )
        seam[index, every, :] = jnp.where(lane >= LANES - 4, west, value)

    def seam_rows(index, carry):
        row = 4 + 8 * index
        here = pl.ds(row, STRIP)
        lanes = lane_iota((STRIP, LANES))
        filtered = []
        for field in range(3):
            summed = (
                seam[field, pl.ds(row - 1, STRIP), :]
                + seam[field, here, :]
                + seam[field, pl.ds(row + 1, STRIP), :]
            )
            west, east = pltpu.roll(summed, 1, 1), pltpu.roll(summed, LANES - 1, 1)
            filtered.append((west + summed + east) * (1.0 / 9.0))
        result = wall_forcing(filtered, seam[3, here, :], seam[4, here, :])
        for field in range(3):
            first = step * result[field]
            last = pltpu.roll(first, LANES // 2, 1)
            force[field, TILES, here, :] = jnp.where(lanes < LANES // 2, last, first)
            for t in range(TILES):
                value = step * force_in[field, t, here, :]
                if t == 0:
                    value = jnp.where(lanes == 0, first, value)
                if t == TILES - 1:
                    value = jnp.where(lanes == LANES - 1, last, value)
                force[field, t, here, :] = value
        for t in range(TILES):
            force[3, t, here, :] = step * spray[t, here, :]
        return carry

    grouped(6, 17, seam_rows, 0)

    half = 0.5 * step

    def advance(load, row):
        here = pl.ds(row, STRIP)
        centre, wests, easts, norths, souths = [], [], [], [], []
        for field in range(4):
            middle = [load(field, t, here) for t in range(count)]
            north = [load(field, t, pl.ds(row - 1, STRIP)) for t in range(count)]
            south = [load(field, t, pl.ds(row + 1, STRIP)) for t in range(count)]
            west, east = shifted_lanes(middle)
            centre.append(middle)
            wests.append(west)
            easts.append(east)
            norths.append(north)
            souths.append(south)
        news = []
        for t in range(count):
            spread = [
                (1.0 - 4.0 * FILM_SPREAD) * centre[f][t]
                + FILM_SPREAD
                * ((norths[f][t] + souths[f][t]) + (wests[f][t] + easts[f][t]))
                for f in range(4)
            ]
            height = centre[0][t]
            inverse = lax.rsqrt(height * height + FILM_FLOOR * FILM_FLOOR)
            drag = (FRICTION * step) * inverse
            slope = half * height
            height_new = (
                spread[0]
                + force[3, t, here, :]
                - half * ((easts[1][t] - wests[1][t]) + (souths[2][t] - norths[2][t]))
            )
            along_new = (
                spread[1]
                + force[0, t, here, :]
                - drag * centre[1][t]
                - slope * (easts[0][t] - wests[0][t])
            )
            across_new = (
                spread[2]
                + force[1, t, here, :]
                - drag * centre[2][t]
                - slope * (souths[0][t] - norths[0][t])
            )
            heat_new = spread[3] + force[2, t, here, :] * inverse
            news.append((height_new, along_new, across_new, heat_new))
        return news

    def middle_rows(source, target):
        def body(index, carry):
            row = 4 + 8 * index
            news = advance(source, row)
            for t in range(count):
                for field in range(4):
                    target[field, t, pl.ds(row, STRIP), :] = news[t][field]
            return carry

        grouped(6, 17, body, 0)

    def first_load(field, t, rows):
        return ring[field, t, rows, :] if t < TILES else halo[field, rows, :]

    def load_from(source):
        return lambda field, t, rows: source[field, t, rows, :]

    middle_rows(first_load, ring_a)
    middle_rows(load_from(ring_a), ring_b)
    middle_rows(load_from(ring_b), ring_a)

    def last_rows(index, best):
        row = pl.multiple_of(8 + 8 * index, 8)
        news = advance(load_from(ring_a), row)
        place = owner_map[wall, index]
        for t in range(TILES):
            for field in range(4):
                out[place, field * TILES + t] = news[t][field]
            best = jnp.maximum(best, film_speed(*news[t][:3]))
        return best

    best = grouped(4, 16, last_rows, jnp.zeros((STRIP, LANES), jnp.float32))
    top = jnp.broadcast_to(step * jnp.max(best, keepdims=True), (STRIP, LANES))
    for owner in range(ROWS // STRIP):
        out[owner, 4 * TILES] = top


def band_peak_kernel(pieces, peak):
    best = pieces[0, 4 * TILES]
    for source in range(1, pieces.shape[0]):
        best = jnp.maximum(best, pieces[source, 4 * TILES])
    peak[...] = best


def strips_kernel(pieces, out):
    first = pl.program_id(0) * TILES
    for source in range(pieces.shape[0]):
        for t in range(TILES):
            start = source * COLS + t * LANES
            out[0, :, start : start + LANES] = pieces[source, first + t]


def grouped(unroll, total, body, carry):
    whole = total // unroll

    def many(index, carry):
        for k in range(unroll):
            carry = body(index * unroll + k, carry)
        return carry

    carry = lax.fori_loop(0, whole, many, carry)
    for index in range(whole * unroll, total):
        carry = body(index, carry)
    return carry


def in_hbm(*arrays):
    return [pltpu.with_memory_space_constraint(a, pltpu.HBM) for a in arrays]


def vmem(count):
    return [pl.BlockSpec(memory_space=pltpu.VMEM)] * count


def shape(*dims):
    return jax.ShapeDtypeStruct(dims, jnp.float32)


def coupling_step(gas_state, wall_flags, film_state, deposit, owner_map):
    params = pltpu.CompilerParams(vmem_limit_bytes=VMEM_LIMIT)
    tail = pltpu.CompilerParams(vmem_limit_bytes=8 << 20)
    flags = jnp.transpose(wall_flags)
    gas_ring, to_north, to_south, core_main, chip_main, peak = pl.pallas_call(
        edges_kernel,
        out_shape=(
            shape(3, TILES, RING + AHEAD, LANES),
            shape(4 * FIELDS, COLS),
            shape(4 * FIELDS, COLS),
            shape(ROWS + 8, LANES),
            shape(ROWS + 8, LANES),
            shape(ROWS, LANES),
        ),
        in_specs=[pl.BlockSpec(memory_space=pltpu.HBM)] * 4,
        out_specs=tuple(vmem(6)),
        scratch_shapes=[
            pltpu.VMEM((4, ROWS, COLS), jnp.float32),
            pltpu.VMEM((3, 4, ROWS, COLS), jnp.float32),
            pltpu.VMEM((ROWS, COLS), jnp.float32),
            pltpu.VMEM((TILES, ROWS), jnp.int32),
            pltpu.SemaphoreType.DMA((6,)),
        ],
        compiler_params=pltpu.CompilerParams(vmem_limit_bytes=VMEM_LIMIT),
        name="edges",
    )(*in_hbm(gas_state, flags, film_state, deposit))

    walls, gases = lax.axis_size("wall"), lax.axis_size("gas")
    both = ("wall", "gas")
    peaks = lax.all_to_all(peak, both, split_axis=0, concat_axis=0, tiled=True)
    down = [(i, (i + 1) % walls) for i in range(walls)]
    up = [(j, i) for i, j in down]
    from_north = lax.ppermute(to_south, "wall", down)
    from_south = lax.ppermute(to_north, "wall", up)
    core_pack, chip_pack = pl.pallas_call(
        corners_kernel,
        out_shape=(shape(ROWS + 8, LANES), shape(ROWS + 8, LANES)),
        in_specs=vmem(4),
        out_specs=tuple(vmem(2)),
        compiler_params=params,
        name="corners",
    )(from_north, from_south, core_main, chip_main)
    partner = [(i, i ^ 1) for i in range(gases)]
    outer = [(i, (i + 1) % gases if i % 2 else (i - 1) % gases) for i in range(gases)]
    core_pack = lax.ppermute(core_pack, "gas", partner)
    chip_pack = lax.ppermute(chip_pack, "gas", outer)

    inner = (4, TILES, RING, LANES)
    ring, spray, seam, force = pl.pallas_call(
        inside_kernel,
        out_shape=(
            shape(*inner),
            shape(*inner[1:]),
            shape(2, RING, LANES),
            shape(3, TILES, RING + AHEAD, LANES),
        ),
        in_specs=vmem(1) + [pl.BlockSpec(memory_space=pltpu.HBM)] * 3 + vmem(2),
        out_specs=tuple(vmem(4)),
        input_output_aliases={0: 3},
        scratch_shapes=[
            pltpu.VMEM(inner[1:], jnp.float32),
            pltpu.VMEM((TILES, ROWS), jnp.int32),
            pltpu.SemaphoreType.DMA((6, TILES)),
        ],
        compiler_params=pltpu.CompilerParams(vmem_limit_bytes=24 << 20),
        cost_estimate=pl.CostEstimate(
            flops=20 << 20, bytes_accessed=8 << 20, transcendentals=1 << 19
        ),
        name="inside",
    )(gas_ring, *in_hbm(film_state, flags, deposit), from_north, from_south)
    outer_ring = (4, TILES + 1, RING, LANES)
    pieces = pl.pallas_call(
        film_kernel,
        out_shape=shape(gases, 4 * TILES + 1, STRIP, LANES),
        in_specs=[pl.BlockSpec(memory_space=pltpu.SMEM)] + vmem(7),
        out_specs=vmem(1)[0],
        scratch_shapes=[
            pltpu.VMEM((4, RING, LANES), jnp.float32),
            pltpu.VMEM((5, RING, LANES), jnp.float32),
            pltpu.VMEM(outer_ring, jnp.float32),
            pltpu.VMEM(outer_ring, jnp.float32),
            pltpu.VMEM(outer_ring, jnp.float32),
        ],
        compiler_params=pltpu.CompilerParams(vmem_limit_bytes=24 << 20),
        name="film",
    )(owner_map, ring, spray, seam, force, core_pack, chip_pack, peaks)
    pieces = lax.all_to_all(pieces, "gas", split_axis=0, concat_axis=0, tiled=True)
    band_peak = pl.pallas_call(
        band_peak_kernel,
        out_shape=shape(STRIP, LANES),
        in_specs=vmem(1),
        out_specs=vmem(1)[0],
        compiler_params=tail,
        name="band_peak",
    )(pieces)
    cfl = jnp.max(
        lax.all_to_all(band_peak, "wall", split_axis=0, concat_axis=0, tiled=True)
    )
    film_out = pl.pallas_call(
        strips_kernel,
        out_shape=shape(4, STRIP, gases * COLS),
        grid=(4,),
        in_specs=vmem(1),
        compiler_params=tail,
        out_specs=pl.BlockSpec((1, STRIP, gases * COLS), lambda i: (i, 0, 0)),
        cost_estimate=pl.CostEstimate(
            flops=0, bytes_accessed=2 << 20, transcendentals=0
        ),
        name="strips",
    )(pieces)
    return film_out, cfl


def solution(mesh):
    return jax.shard_map(
        coupling_step,
        mesh=mesh,
        in_specs=(
            P(None, None, "wall", "gas"),
            P("wall", "gas"),
            P(None, "wall", "gas"),
            P("wall", "gas"),
            P(),
        ),
        out_specs=(P(None, ("wall", "gas"), None), P()),
        check_vma=False,
    )
```

```python
import jax
import jax.numpy as jnp
from jax import lax
from jax.experimental import pallas as pl
from jax.experimental.pallas import tpu as pltpu
from jax.sharding import PartitionSpec as P


LAYER_WEIGHTS = (0.1, 0.2, 0.3, 0.4)
KAPPA = 0.41
HEIGHT_RATIO = 20.0
SPEED_FLOOR = 0.5
PRANDTL_TURB = 0.85
PRANDTL_JUMP = 3.0
LAMINAR_SHEAR = 0.3
LAMINAR_HEAT = 0.2
FILM_SPREAD = 0.24
FILM_FLOOR = 0.3
FRICTION = 0.5
COURANT = 6.0

ROWS = 128
COLS = 512
LANES = 128
TILES = COLS // LANES
FIELDS = 9
STRIP = 8
RING = ROWS + 16
WIDE = COLS + LANES
AHEAD = 8
VMEM_LIMIT = 24 << 20


def lane_iota(shape):
    return lax.broadcasted_iota(jnp.int32, shape, len(shape) - 1)


def film_speed(height, along, across):
    square = height * height + FILM_FLOOR * FILM_FLOOR
    thickness = jnp.sqrt(square)
    moving = jnp.sqrt(along * along + across * across)
    return moving / thickness + jnp.sqrt(thickness)


def halo_tile(east, west, field):
    lane = lane_iota(east.shape)
    return jnp.where(
        lane < LANES // 2,
        pltpu.roll(east, (LANES - 4 * field) % LANES, 1),
        pltpu.roll(west, (LANES - 4 - 4 * field) % LANES, 1),
    )


def sides(core, chip):
    even = lax.rem(lax.axis_index("gas"), 2) == 0
    return jnp.where(even, core, chip), jnp.where(even, chip, core)


def sample(gas, field, rows, cols):
    value = LAYER_WEIGHTS[0] * gas[field, 0, rows, cols]
    for layer in range(1, 4):
        value = value + LAYER_WEIGHTS[layer] * gas[field, layer, rows, cols]
    return value


def flag_columns(flags_by_row):
    flags = flags_by_row.astype(jnp.float32)
    return jnp.transpose(jnp.concatenate([flags, flags], axis=0))


def attached_rows(columns, rows, tile):
    count = columns[rows, tile : tile + 1]
    lane = lane_iota((count.shape[0], LANES)).astype(jnp.float32)
    return jnp.where(lane < count, 1.0, 0.0)


def edges_kernel(
    gas_hbm,
    flags_hbm,
    film_hbm,
    deposit_hbm,
    gas_ring,
    to_north,
    to_south,
    core_pack,
    chip_pack,
    peak,
    film,
    gas,
    deposit,
    flags,
    sems,
):
    copies = [
        pltpu.make_async_copy(film_hbm, film, sems.at[0]),
        pltpu.make_async_copy(flags_hbm, flags, sems.at[1]),
        pltpu.make_async_copy(deposit_hbm, deposit, sems.at[2]),
        pltpu.make_async_copy(gas_hbm.at[0], gas.at[0], sems.at[3]),
        pltpu.make_async_copy(gas_hbm.at[1], gas.at[1], sems.at[4]),
        pltpu.make_async_copy(gas_hbm.at[2], gas.at[2], sems.at[5]),
    ]
    for copy in copies:
        copy.start()
    tiles = [slice(tile * LANES, (tile + 1) * LANES) for tile in range(TILES)]
    every = slice(0, ROWS)
    even = lax.rem(lax.axis_index("gas"), 2) == 0
    lane = lane_iota((ROWS, LANES))

    def send(field, value_of):
        target = slice(4 * field, 4 * field + 4)
        for tile, cols in enumerate(tiles):
            to_north[target, cols] = value_of(slice(0, 4), tile)
            to_south[target, cols] = value_of(slice(ROWS - 4, ROWS), tile)
        west = value_of(every, 0)
        if field:
            west = pltpu.roll(west, 4 * field, 1)
        east = pltpu.roll(value_of(every, TILES - 1), 4 * field + 4, 1)
        here = (lane >= 4 * field) & (lane < 4 * field + 4)
        for pack, value in (
            (core_pack, jnp.where(even, east, west)),
            (chip_pack, jnp.where(even, west, east)),
        ):
            old = pack[...] if field else jnp.zeros_like(value)
            pack[...] = jnp.where(here, value, old)

    copies[0].wait()
    best = jnp.zeros((STRIP, LANES), jnp.float32)
    for cols in tiles:
        speed = film_speed(film[0, :, cols], film[1, :, cols], film[2, :, cols])
        for row in range(0, ROWS, STRIP):
            best = jnp.maximum(best, speed[row : row + STRIP])
    peak[...] = jnp.broadcast_to(jnp.max(best, keepdims=True), (ROWS, LANES))
    for field in range(4):
        send(field, lambda rows, tile, f=field: film[f, rows, tiles[tile]])
    copies[1].wait()
    columns = flag_columns(flags[...])
    send(8, lambda rows, tile: attached_rows(columns, rows, tile))
    copies[2].wait()
    send(7, lambda rows, tile: deposit[rows, tiles[tile]])
    for field in range(3):
        copies[3 + field].wait()
        for tile, cols in enumerate(tiles):
            gas_ring[field, tile, AHEAD : AHEAD + ROWS, :] = sample(gas, field, every, cols)
        send(
            4 + field,
            lambda rows, tile, f=field: gas_ring[
                f, tile, AHEAD + rows.start : AHEAD + rows.stop, :
            ],
        )


def corners_kernel(core, chip, north_in, south_in, to_north, to_south):
    for rows, source, target in (
        (slice(0, 8), north_in, to_north),
        (slice(ROWS - 8, ROWS), south_in, to_south),
    ):
        target[:, 0:COLS] = source[:, 0:COLS]
        east, west = sides(core[rows, :], chip[rows, :])
        for field in range(FIELDS):
            value = halo_tile(east, west, field)
            value = value[0:4] if rows.start == 0 else value[4:8]
            target[4 * field : 4 * field + 4, COLS:WIDE] = value


def shifted_lanes(tiles):
    lane = lane_iota(tiles[0].shape)
    plus = [pltpu.roll(t, 1, 1) for t in tiles]
    minus = [pltpu.roll(t, LANES - 1, 1) for t in tiles]
    count = len(tiles)
    west = [jnp.where(lane == 0, plus[i - 1], plus[i]) for i in range(count)]
    east = [
        jnp.where(lane == LANES - 1, minus[(i + 1) % count], minus[i])
        for i in range(count)
    ]
    return west, east


def wall_forcing(filtered, film_heat, attached):
    along, across, gas_heat = filtered
    contrast = gas_heat - film_heat
    on_wall = attached > 0.5
    square = along * along + across * across + SPEED_FLOOR * SPEED_FLOOR
    speed = square * lax.rsqrt(square)
    height = HEIGHT_RATIO * speed
    scaled = height * lax.rsqrt(height)
    uplus = jnp.log(1.0 + KAPPA * scaled) * (1.0 / KAPPA) + 7.8 * (
        1.0
        - jnp.exp(scaled * (-1.0 / 11.0))
        - scaled * (1.0 / 11.0) * jnp.exp(scaled * (-1.0 / 3.0))
    )
    factor = jnp.where(on_wall, speed / (uplus * uplus), LAMINAR_SHEAR)
    heat = jnp.where(
        on_wall, speed / (PRANDTL_TURB * uplus + PRANDTL_JUMP), LAMINAR_HEAT
    )
    return factor * along, factor * across, heat * contrast


def inside_kernel(
    gas_in,
    film_hbm,
    flags_hbm,
    deposit_hbm,
    core,
    chip,
    ring,
    spray,
    force,
    attached,
    flags,
    sems,
):
    del gas_in
    count = TILES + 1
    inner = slice(8, 8 + ROWS)
    flags_copy = pltpu.make_async_copy(flags_hbm, flags, sems.at[5, 0])
    flags_copy.start()
    arriving = {}
    for field in (3, 0, 1, 2, 4):
        arriving[field] = []
        for tile in range(TILES):
            cols = slice(tile * LANES, (tile + 1) * LANES)
            if field < 4:
                source, target = film_hbm.at[field, :, cols], ring.at[field, tile, inner]
            else:
                source, target = deposit_hbm.at[:, cols], spray.at[tile]
            copy = pltpu.make_async_copy(source, target, sems.at[field, tile])
            copy.start()
            arriving[field].append(copy)

    east, west = sides(core[...], chip[...])
    for field in range(4):
        ring[field, TILES, inner, :] = halo_tile(east, west, field)
    for field in range(3):
        force[field, TILES, AHEAD : AHEAD + ROWS, :] = halo_tile(east, west, 4 + field)
    spray[TILES] = halo_tile(east, west, 7)
    attached[TILES, 0:ROWS, :] = halo_tile(east, west, 8)
    flags_copy.wait()
    columns = flag_columns(flags[...])
    for tile in range(TILES):
        attached[tile, 0:ROWS, :] = attached_rows(columns, slice(0, ROWS), tile)
    for copy in arriving[3]:
        copy.wait()

    def forcing_rows(index, carry):
        row = 1 + 8 * index
        here = pl.ds(row, STRIP)
        filtered = []
        for field in range(3):
            summed = [
                force[field, t, pl.ds(row + AHEAD - 1, STRIP), :]
                + force[field, t, pl.ds(row + AHEAD, STRIP), :]
                + force[field, t, pl.ds(row + AHEAD + 1, STRIP), :]
                for t in range(count)
            ]
            west, east = shifted_lanes(summed)
            filtered.append(
                [(west[t] + summed[t] + east[t]) * (1.0 / 9.0) for t in range(count)]
            )
        for t in range(count):
            result = wall_forcing(
                [filtered[f][t] for f in range(3)],
                ring[3, t, pl.ds(row + 8, STRIP), :],
                attached[t, here, :],
            )
            for field in range(3):
                force[field, t, here, :] = result[field]
        return carry

    grouped(4, 16, forcing_rows, 0)
    for field in (0, 1, 2, 4):
        for copy in arriving[field]:
            copy.wait()


def film_kernel(
    owner_map,
    ring_in,
    spray,
    force_in,
    to_north,
    to_south,
    from_north,
    from_south,
    peaks,
    out,
    ring,
    stack,
    ring_a,
    ring_b,
    force,
):
    del ring_in
    count = TILES + 1
    wall = lax.axis_index("wall")
    step = COURANT / jnp.max(peaks[...])
    inner = slice(8, 8 + ROWS)
    above, below = slice(4, 8), slice(8 + ROWS, 12 + ROWS)

    for tile in range(count):
        cols = slice(tile * LANES, (tile + 1) * LANES)
        for field in range(4):
            source = slice(4 * field, 4 * field + 4)
            ring[field, tile, above, :] = from_north[source, cols]
            ring[field, tile, below, :] = from_south[source, cols]
        force[3, tile, above, :] = step * from_north[28:32, cols]
        force[3, tile, inner, :] = step * spray[tile]
        force[3, tile, below, :] = step * from_south[28:32, cols]
        for index, field in enumerate((4, 5, 6, 3, 8)):
            source = slice(4 * field, 4 * field + 4)
            stack[index, tile, 0:4, :] = from_north[source, cols]
            stack[index, tile, 4:8, :] = to_north[source, cols]
            stack[index, tile, 8:12, :] = to_south[source, cols]
            stack[index, tile, 12:16, :] = from_south[source, cols]

    def scale_rows(index, carry):
        row = 1 + 8 * index
        for field in range(3):
            for t in range(count):
                force[field, t, pl.ds(row + 8, STRIP), :] = (
                    step * force_in[field, t, pl.ds(row, STRIP), :]
                )
        return carry

    grouped(4, 16, scale_rows, 0)
    for start, first, target in ((1, 0, 5), (8, 3, 135)):
        filtered = []
        for field in range(3):
            summed = [
                stack[field, t, start - 1 : start - 1 + STRIP, :]
                + stack[field, t, start : start + STRIP, :]
                + stack[field, t, start + 1 : start + 1 + STRIP, :]
                for t in range(count)
            ]
            west, east = shifted_lanes(summed)
            filtered.append(
                [(west[t] + summed[t] + east[t]) * (1.0 / 9.0) for t in range(count)]
            )
        for t in range(count):
            rows = slice(start, start + STRIP)
            result = wall_forcing(
                [filtered[f][t] for f in range(3)], stack[3, t, rows, :], stack[4, t, rows, :]
            )
            for field in range(3):
                force[field, t, target : target + 4, :] = (
                    step * result[field][first : first + 4]
                )

    half = 0.5 * step

    def advance(load, row):
        here = pl.ds(row, STRIP)
        centre, wests, easts, norths, souths = [], [], [], [], []
        for field in range(4):
            middle = [load(field, t, here) for t in range(count)]
            north = [load(field, t, pl.ds(row - 1, STRIP)) for t in range(count)]
            south = [load(field, t, pl.ds(row + 1, STRIP)) for t in range(count)]
            west, east = shifted_lanes(middle)
            centre.append(middle)
            wests.append(west)
            easts.append(east)
            norths.append(north)
            souths.append(south)
        news = []
        for t in range(count):
            spread = [
                (1.0 - 4.0 * FILM_SPREAD) * centre[f][t]
                + FILM_SPREAD
                * ((norths[f][t] + souths[f][t]) + (wests[f][t] + easts[f][t]))
                for f in range(4)
            ]
            height = centre[0][t]
            inverse = lax.rsqrt(height * height + FILM_FLOOR * FILM_FLOOR)
            drag = (FRICTION * step) * inverse
            slope = half * height
            height_new = (
                spread[0]
                + force[3, t, here, :]
                - half * ((easts[1][t] - wests[1][t]) + (souths[2][t] - norths[2][t]))
            )
            along_new = (
                spread[1]
                + force[0, t, here, :]
                - drag * centre[1][t]
                - slope * (easts[0][t] - wests[0][t])
            )
            across_new = (
                spread[2]
                + force[1, t, here, :]
                - drag * centre[2][t]
                - slope * (souths[0][t] - norths[0][t])
            )
            heat_new = spread[3] + force[2, t, here, :] * inverse
            news.append((height_new, along_new, across_new, heat_new))
        return news

    def middle_rows(source, target):
        def body(index, carry):
            row = 4 + 8 * index
            news = advance(source, row)
            for t in range(count):
                for field in range(4):
                    target[field, t, pl.ds(row, STRIP), :] = news[t][field]
            return carry

        grouped(6, 17, body, 0)

    def load_from(source):
        return lambda field, t, rows: source[field, t, rows, :]

    middle_rows(load_from(ring), ring_a)
    middle_rows(load_from(ring_a), ring_b)
    middle_rows(load_from(ring_b), ring_a)

    def last_rows(index, best):
        row = pl.multiple_of(8 + 8 * index, 8)
        news = advance(load_from(ring_a), row)
        place = owner_map[wall, index]
        for t in range(TILES):
            for field in range(4):
                out[place, field * TILES + t] = news[t][field]
            best = jnp.maximum(best, film_speed(*news[t][:3]))
        return best

    best = grouped(4, 16, last_rows, jnp.zeros((STRIP, LANES), jnp.float32))
    top = jnp.broadcast_to(step * jnp.max(best, keepdims=True), (STRIP, LANES))
    for owner in range(ROWS // STRIP):
        out[owner, 4 * TILES] = top


def band_peak_kernel(pieces, peak):
    best = pieces[0, 4 * TILES]
    for source in range(1, pieces.shape[0]):
        best = jnp.maximum(best, pieces[source, 4 * TILES])
    peak[...] = best


def strips_kernel(pieces, out):
    first = pl.program_id(0) * TILES
    for source in range(pieces.shape[0]):
        for t in range(TILES):
            start = source * COLS + t * LANES
            out[0, :, start : start + LANES] = pieces[source, first + t]


def grouped(unroll, total, body, carry):
    whole = total // unroll

    def many(index, carry):
        for k in range(unroll):
            carry = body(index * unroll + k, carry)
        return carry

    carry = lax.fori_loop(0, whole, many, carry)
    for index in range(whole * unroll, total):
        carry = body(index, carry)
    return carry


def in_hbm(*arrays):
    return [pltpu.with_memory_space_constraint(a, pltpu.HBM) for a in arrays]


def vmem(count):
    return [pl.BlockSpec(memory_space=pltpu.VMEM)] * count


def shape(*dims):
    return jax.ShapeDtypeStruct(dims, jnp.float32)


def coupling_step(gas_state, wall_flags, film_state, deposit, owner_map):
    params = pltpu.CompilerParams(vmem_limit_bytes=VMEM_LIMIT)
    tail = pltpu.CompilerParams(vmem_limit_bytes=8 << 20)
    flags = jnp.transpose(wall_flags)
    gas_ring, north_main, south_main, core_pack, chip_pack, peak = pl.pallas_call(
        edges_kernel,
        out_shape=(
            shape(3, TILES + 1, RING, LANES),
            shape(4 * FIELDS, WIDE),
            shape(4 * FIELDS, WIDE),
            shape(ROWS, LANES),
            shape(ROWS, LANES),
            shape(ROWS, LANES),
        ),
        in_specs=[pl.BlockSpec(memory_space=pltpu.HBM)] * 4,
        out_specs=tuple(vmem(6)),
        scratch_shapes=[
            pltpu.VMEM((4, ROWS, COLS), jnp.float32),
            pltpu.VMEM((3, 4, ROWS, COLS), jnp.float32),
            pltpu.VMEM((ROWS, COLS), jnp.float32),
            pltpu.VMEM((TILES, ROWS), jnp.int32),
            pltpu.SemaphoreType.DMA((6,)),
        ],
        compiler_params=pltpu.CompilerParams(vmem_limit_bytes=VMEM_LIMIT),
        name="edges",
    )(*in_hbm(gas_state, flags, film_state, deposit))

    walls, gases = lax.axis_size("wall"), lax.axis_size("gas")
    partner = [(i, i ^ 1) for i in range(gases)]
    outer = [(i, (i + 1) % gases if i % 2 else (i - 1) % gases) for i in range(gases)]
    chip_side = lax.ppermute(chip_pack, "gas", outer)
    core_side = lax.ppermute(core_pack, "gas", partner)
    both = ("wall", "gas")
    peaks = lax.all_to_all(peak, both, split_axis=0, concat_axis=0, tiled=True)
    to_north, to_south = pl.pallas_call(
        corners_kernel,
        out_shape=(shape(4 * FIELDS, WIDE), shape(4 * FIELDS, WIDE)),
        in_specs=vmem(4),
        out_specs=tuple(vmem(2)),
        compiler_params=params,
        name="corners",
    )(core_side, chip_side, north_main, south_main)
    down = [(i, (i + 1) % walls) for i in range(walls)]
    up = [(j, i) for i, j in down]
    from_north = lax.ppermute(to_south, "wall", down)
    from_south = lax.ppermute(to_north, "wall", up)

    ring_shape = (4, TILES + 1, RING, LANES)
    ring, spray, force = pl.pallas_call(
        inside_kernel,
        out_shape=(
            shape(*ring_shape),
            shape(TILES + 1, ROWS, LANES),
            shape(3, *ring_shape[1:]),
        ),
        in_specs=vmem(1) + [pl.BlockSpec(memory_space=pltpu.HBM)] * 3 + vmem(2),
        out_specs=tuple(vmem(3)),
        input_output_aliases={0: 2},
        scratch_shapes=[
            pltpu.VMEM(ring_shape[1:], jnp.float32),
            pltpu.VMEM((TILES, ROWS), jnp.int32),
            pltpu.SemaphoreType.DMA((6, TILES)),
        ],
        compiler_params=params,
        cost_estimate=pl.CostEstimate(
            flops=20 << 20, bytes_accessed=8 << 20, transcendentals=1 << 19
        ),
        name="inside",
    )(gas_ring, *in_hbm(film_state, flags, deposit), core_side, chip_side)
    pieces, _ = pl.pallas_call(
        film_kernel,
        out_shape=(shape(gases, 4 * TILES + 1, STRIP, LANES), shape(*ring_shape)),
        in_specs=[pl.BlockSpec(memory_space=pltpu.SMEM)] + vmem(8),
        out_specs=tuple(vmem(2)),
        input_output_aliases={1: 1},
        scratch_shapes=[
            pltpu.VMEM((5, TILES + 1, 24, LANES), jnp.float32),
            pltpu.VMEM(ring_shape, jnp.float32),
            pltpu.VMEM(ring_shape, jnp.float32),
            pltpu.VMEM(ring_shape, jnp.float32),
        ],
        compiler_params=params,
        name="film",
    )(
        owner_map,
        ring,
        spray,
        force,
        to_north,
        to_south,
        from_north,
        from_south,
        peaks,
    )
    pieces = lax.all_to_all(pieces, "gas", split_axis=0, concat_axis=0, tiled=True)
    band_peak = pl.pallas_call(
        band_peak_kernel,
        out_shape=shape(STRIP, LANES),
        in_specs=vmem(1),
        out_specs=vmem(1)[0],
        compiler_params=tail,
        name="band_peak",
    )(pieces)
    cfl = jnp.max(
        lax.all_to_all(band_peak, "wall", split_axis=0, concat_axis=0, tiled=True)
    )
    film_out = pl.pallas_call(
        strips_kernel,
        out_shape=shape(4, STRIP, gases * COLS),
        grid=(4,),
        in_specs=vmem(1),
        compiler_params=tail,
        out_specs=pl.BlockSpec((1, STRIP, gases * COLS), lambda i: (i, 0, 0)),
        cost_estimate=pl.CostEstimate(
            flops=0, bytes_accessed=2 << 20, transcendentals=0
        ),
        name="strips",
    )(pieces)
    return film_out, cfl


def solution(mesh):
    return jax.shard_map(
        coupling_step,
        mesh=mesh,
        in_specs=(
            P(None, None, "wall", "gas"),
            P("wall", "gas"),
            P(None, "wall", "gas"),
            P("wall", "gas"),
            P(),
        ),
        out_specs=(P(None, ("wall", "gas"), None), P()),
        check_vma=False,
    )
```

```python
import jax
import jax.numpy as jnp
from jax import lax
from jax.experimental import pallas as pl
from jax.experimental.pallas import tpu as pltpu
from jax.sharding import PartitionSpec as P


LAYER_WEIGHTS = (0.1, 0.2, 0.3, 0.4)
KAPPA = 0.41
HEIGHT_RATIO = 20.0
SPEED_FLOOR = 0.5
PRANDTL_TURB = 0.85
PRANDTL_JUMP = 3.0
LAMINAR_SHEAR = 0.3
LAMINAR_HEAT = 0.2
FILM_SPREAD = 0.24
FILM_FLOOR = 0.3
FRICTION = 0.5
COURANT = 6.0

ROWS = 128
COLS = 512
LANES = 128
TILES = COLS // LANES
FIELDS = 9
STRIP = 8
RING = ROWS + 16
WIDE = COLS + LANES
AHEAD = 8
VMEM_LIMIT = 24 << 20


def lane_iota(shape):
    return lax.broadcasted_iota(jnp.int32, shape, len(shape) - 1)


def film_speed(height, along, across):
    square = height * height + FILM_FLOOR * FILM_FLOOR
    thickness = jnp.sqrt(square)
    moving = jnp.sqrt(along * along + across * across)
    return moving / thickness + jnp.sqrt(thickness)


def halo_tile(east, west, field):
    lane = lane_iota(east.shape)
    return jnp.where(
        lane < LANES // 2,
        pltpu.roll(east, (LANES - 4 * field) % LANES, 1),
        pltpu.roll(west, (LANES - 4 - 4 * field) % LANES, 1),
    )


def sides(core, chip):
    even = lax.rem(lax.axis_index("gas"), 2) == 0
    return jnp.where(even, core, chip), jnp.where(even, chip, core)


def sample(gas, field, rows, cols):
    value = LAYER_WEIGHTS[0] * gas[field, 0, rows, cols]
    for layer in range(1, 4):
        value = value + LAYER_WEIGHTS[layer] * gas[field, layer, rows, cols]
    return value


def flag_columns(flags_by_row):
    flags = flags_by_row.astype(jnp.float32)
    return jnp.transpose(jnp.concatenate([flags, flags], axis=0))


def attached_rows(columns, rows, tile):
    count = columns[rows, tile : tile + 1]
    lane = lane_iota((count.shape[0], LANES)).astype(jnp.float32)
    return jnp.where(lane < count, 1.0, 0.0)


def edges_kernel(
    gas_hbm,
    flags_hbm,
    film_hbm,
    deposit_hbm,
    gas_ring,
    to_north,
    to_south,
    core_pack,
    chip_pack,
    peak,
    film,
    gas,
    deposit,
    flags,
    sems,
):
    copies = [
        pltpu.make_async_copy(film_hbm, film, sems.at[0]),
        pltpu.make_async_copy(flags_hbm, flags, sems.at[1]),
        pltpu.make_async_copy(deposit_hbm, deposit, sems.at[2]),
        pltpu.make_async_copy(gas_hbm.at[0], gas.at[0], sems.at[3]),
        pltpu.make_async_copy(gas_hbm.at[1], gas.at[1], sems.at[4]),
        pltpu.make_async_copy(gas_hbm.at[2], gas.at[2], sems.at[5]),
    ]
    for copy in copies:
        copy.start()
    tiles = [slice(tile * LANES, (tile + 1) * LANES) for tile in range(TILES)]
    every = slice(0, ROWS)
    even = lax.rem(lax.axis_index("gas"), 2) == 0
    lane = lane_iota((ROWS, LANES))

    def send(field, value_of):
        target = slice(4 * field, 4 * field + 4)
        for tile, cols in enumerate(tiles):
            to_north[target, cols] = value_of(slice(0, 4), tile)
            to_south[target, cols] = value_of(slice(ROWS - 4, ROWS), tile)
        west = value_of(every, 0)
        if field:
            west = pltpu.roll(west, 4 * field, 1)
        east = pltpu.roll(value_of(every, TILES - 1), 4 * field + 4, 1)
        here = (lane >= 4 * field) & (lane < 4 * field + 4)
        for pack, value in (
            (core_pack, jnp.where(even, east, west)),
            (chip_pack, jnp.where(even, west, east)),
        ):
            old = pack[...] if field else jnp.zeros_like(value)
            pack[...] = jnp.where(here, value, old)

    copies[0].wait()
    best = jnp.zeros((STRIP, LANES), jnp.float32)
    for cols in tiles:
        speed = film_speed(film[0, :, cols], film[1, :, cols], film[2, :, cols])
        for row in range(0, ROWS, STRIP):
            best = jnp.maximum(best, speed[row : row + STRIP])
    peak[...] = jnp.broadcast_to(jnp.max(best, keepdims=True), (ROWS, LANES))
    for field in range(4):
        send(field, lambda rows, tile, f=field: film[f, rows, tiles[tile]])
    copies[1].wait()
    columns = flag_columns(flags[...])
    send(8, lambda rows, tile: attached_rows(columns, rows, tile))
    copies[2].wait()
    send(7, lambda rows, tile: deposit[rows, tiles[tile]])
    for field in range(3):
        copies[3 + field].wait()
        for tile, cols in enumerate(tiles):
            gas_ring[field, tile, AHEAD : AHEAD + ROWS, :] = sample(gas, field, every, cols)
        send(
            4 + field,
            lambda rows, tile, f=field: gas_ring[
                f, tile, AHEAD + rows.start : AHEAD + rows.stop, :
            ],
        )


def even_wall():
    return lax.rem(lax.axis_index("wall"), 2) == 0


def corners_kernel(core, chip, north_in, south_in, near, far):
    even = even_wall()
    north, south = north_in[:, 0:COLS], south_in[:, 0:COLS]
    near[:, 0:COLS] = jnp.where(even, south, north)
    far[:, 0:COLS] = jnp.where(even, north, south)
    top, bottom = slice(0, 8), slice(ROWS - 8, ROWS)
    upper = sides(core[top, :], chip[top, :])
    lower = sides(core[bottom, :], chip[bottom, :])
    for field in range(FIELDS):
        target = slice(4 * field, 4 * field + 4)
        north = halo_tile(*upper, field)[0:4]
        south = halo_tile(*lower, field)[4:8]
        near[target, COLS:WIDE] = jnp.where(even, south, north)
        far[target, COLS:WIDE] = jnp.where(even, north, south)


def shifted_lanes(tiles):
    lane = lane_iota(tiles[0].shape)
    plus = [pltpu.roll(t, 1, 1) for t in tiles]
    minus = [pltpu.roll(t, LANES - 1, 1) for t in tiles]
    count = len(tiles)
    west = [jnp.where(lane == 0, plus[i - 1], plus[i]) for i in range(count)]
    east = [
        jnp.where(lane == LANES - 1, minus[(i + 1) % count], minus[i])
        for i in range(count)
    ]
    return west, east


def wall_forcing(filtered, film_heat, attached):
    along, across, gas_heat = filtered
    contrast = gas_heat - film_heat
    on_wall = attached > 0.5
    square = along * along + across * across + SPEED_FLOOR * SPEED_FLOOR
    speed = square * lax.rsqrt(square)
    height = HEIGHT_RATIO * speed
    scaled = height * lax.rsqrt(height)
    uplus = jnp.log(1.0 + KAPPA * scaled) * (1.0 / KAPPA) + 7.8 * (
        1.0
        - jnp.exp(scaled * (-1.0 / 11.0))
        - scaled * (1.0 / 11.0) * jnp.exp(scaled * (-1.0 / 3.0))
    )
    factor = jnp.where(on_wall, speed / (uplus * uplus), LAMINAR_SHEAR)
    heat = jnp.where(
        on_wall, speed / (PRANDTL_TURB * uplus + PRANDTL_JUMP), LAMINAR_HEAT
    )
    return factor * along, factor * across, heat * contrast


def inside_kernel(
    gas_in,
    film_hbm,
    flags_hbm,
    deposit_hbm,
    core,
    chip,
    ring,
    spray,
    force,
    attached,
    flags,
    sems,
):
    del gas_in
    count = TILES + 1
    inner = slice(8, 8 + ROWS)
    flags_copy = pltpu.make_async_copy(flags_hbm, flags, sems.at[5, 0])
    flags_copy.start()
    arriving = {}
    for field in (3, 0, 1, 2, 4):
        arriving[field] = []
        for tile in range(TILES):
            cols = slice(tile * LANES, (tile + 1) * LANES)
            if field < 4:
                source, target = film_hbm.at[field, :, cols], ring.at[field, tile, inner]
            else:
                source, target = deposit_hbm.at[:, cols], spray.at[tile]
            copy = pltpu.make_async_copy(source, target, sems.at[field, tile])
            copy.start()
            arriving[field].append(copy)

    east, west = sides(core[...], chip[...])
    for field in range(4):
        ring[field, TILES, inner, :] = halo_tile(east, west, field)
    for field in range(3):
        force[field, TILES, AHEAD : AHEAD + ROWS, :] = halo_tile(east, west, 4 + field)
    spray[TILES] = halo_tile(east, west, 7)
    attached[TILES, 0:ROWS, :] = halo_tile(east, west, 8)
    flags_copy.wait()
    columns = flag_columns(flags[...])
    for tile in range(TILES):
        attached[tile, 0:ROWS, :] = attached_rows(columns, slice(0, ROWS), tile)
    for copy in arriving[3]:
        copy.wait()

    def forcing_rows(index, carry):
        row = 1 + 8 * index
        here = pl.ds(row, STRIP)
        filtered = []
        for field in range(3):
            summed = [
                force[field, t, pl.ds(row + AHEAD - 1, STRIP), :]
                + force[field, t, pl.ds(row + AHEAD, STRIP), :]
                + force[field, t, pl.ds(row + AHEAD + 1, STRIP), :]
                for t in range(count)
            ]
            west, east = shifted_lanes(summed)
            filtered.append(
                [(west[t] + summed[t] + east[t]) * (1.0 / 9.0) for t in range(count)]
            )
        for t in range(count):
            result = wall_forcing(
                [filtered[f][t] for f in range(3)],
                ring[3, t, pl.ds(row + 8, STRIP), :],
                attached[t, here, :],
            )
            for field in range(3):
                force[field, t, here, :] = result[field]
        return carry

    grouped(4, 16, forcing_rows, 0)
    for field in (0, 1, 2, 4):
        for copy in arriving[field]:
            copy.wait()


def film_kernel(
    owner_map,
    ring_in,
    spray,
    force_in,
    near_sent,
    far_sent,
    near,
    far,
    peaks,
    out,
    ring,
    stack,
    ring_a,
    ring_b,
    force,
):
    del ring_in
    count = TILES + 1
    wall = lax.axis_index("wall")
    step = COURANT / jnp.max(peaks[...])
    inner = slice(8, 8 + ROWS)
    above, below = slice(4, 8), slice(8 + ROWS, 12 + ROWS)

    even = even_wall()

    def pair(field, cols, close, distant):
        rows = slice(4 * field, 4 * field + 4)
        one, two = close[rows, cols], distant[rows, cols]
        return jnp.where(even, two, one), jnp.where(even, one, two)

    for tile in range(count):
        cols = slice(tile * LANES, (tile + 1) * LANES)
        arrived = [pair(field, cols, near, far) for field in range(FIELDS)]
        for field in range(4):
            ring[field, tile, above, :], ring[field, tile, below, :] = arrived[field]
        force[3, tile, above, :] = step * arrived[7][0]
        force[3, tile, inner, :] = step * spray[tile]
        force[3, tile, below, :] = step * arrived[7][1]
        for index, field in enumerate((4, 5, 6, 3, 8)):
            own = pair(field, cols, near_sent, far_sent)
            stack[index, tile, 0:4, :] = arrived[field][0]
            stack[index, tile, 4:8, :] = own[0]
            stack[index, tile, 8:12, :] = own[1]
            stack[index, tile, 12:16, :] = arrived[field][1]

    def scale_rows(index, carry):
        row = 1 + 8 * index
        for field in range(3):
            for t in range(count):
                force[field, t, pl.ds(row + 8, STRIP), :] = (
                    step * force_in[field, t, pl.ds(row, STRIP), :]
                )
        return carry

    grouped(4, 16, scale_rows, 0)
    for start, first, target in ((1, 0, 5), (8, 3, 135)):
        filtered = []
        for field in range(3):
            summed = [
                stack[field, t, start - 1 : start - 1 + STRIP, :]
                + stack[field, t, start : start + STRIP, :]
                + stack[field, t, start + 1 : start + 1 + STRIP, :]
                for t in range(count)
            ]
            west, east = shifted_lanes(summed)
            filtered.append(
                [(west[t] + summed[t] + east[t]) * (1.0 / 9.0) for t in range(count)]
            )
        for t in range(count):
            rows = slice(start, start + STRIP)
            result = wall_forcing(
                [filtered[f][t] for f in range(3)], stack[3, t, rows, :], stack[4, t, rows, :]
            )
            for field in range(3):
                force[field, t, target : target + 4, :] = (
                    step * result[field][first : first + 4]
                )

    half = 0.5 * step

    def advance(load, row):
        here = pl.ds(row, STRIP)
        centre, wests, easts, norths, souths = [], [], [], [], []
        for field in range(4):
            middle = [load(field, t, here) for t in range(count)]
            north = [load(field, t, pl.ds(row - 1, STRIP)) for t in range(count)]
            south = [load(field, t, pl.ds(row + 1, STRIP)) for t in range(count)]
            west, east = shifted_lanes(middle)
            centre.append(middle)
            wests.append(west)
            easts.append(east)
            norths.append(north)
            souths.append(south)
        news = []
        for t in range(count):
            spread = [
                (1.0 - 4.0 * FILM_SPREAD) * centre[f][t]
                + FILM_SPREAD
                * ((norths[f][t] + souths[f][t]) + (wests[f][t] + easts[f][t]))
                for f in range(4)
            ]
            height = centre[0][t]
            inverse = lax.rsqrt(height * height + FILM_FLOOR * FILM_FLOOR)
            drag = (FRICTION * step) * inverse
            slope = half * height
            height_new = (
                spread[0]
                + force[3, t, here, :]
                - half * ((easts[1][t] - wests[1][t]) + (souths[2][t] - norths[2][t]))
            )
            along_new = (
                spread[1]
                + force[0, t, here, :]
                - drag * centre[1][t]
                - slope * (easts[0][t] - wests[0][t])
            )
            across_new = (
                spread[2]
                + force[1, t, here, :]
                - drag * centre[2][t]
                - slope * (souths[0][t] - norths[0][t])
            )
            heat_new = spread[3] + force[2, t, here, :] * inverse
            news.append((height_new, along_new, across_new, heat_new))
        return news

    def middle_rows(source, target):
        def body(index, carry):
            row = 4 + 8 * index
            news = advance(source, row)
            for t in range(count):
                for field in range(4):
                    target[field, t, pl.ds(row, STRIP), :] = news[t][field]
            return carry

        grouped(6, 17, body, 0)

    def load_from(source):
        return lambda field, t, rows: source[field, t, rows, :]

    middle_rows(load_from(ring), ring_a)
    middle_rows(load_from(ring_a), ring_b)
    middle_rows(load_from(ring_b), ring_a)

    def last_rows(index, best):
        row = pl.multiple_of(8 + 8 * index, 8)
        news = advance(load_from(ring_a), row)
        place = owner_map[wall, index]
        for t in range(TILES):
            for field in range(4):
                out[place, field * TILES + t] = news[t][field]
            best = jnp.maximum(best, film_speed(*news[t][:3]))
        return best

    best = grouped(4, 16, last_rows, jnp.zeros((STRIP, LANES), jnp.float32))
    top = jnp.broadcast_to(step * jnp.max(best, keepdims=True), (STRIP, LANES))
    for owner in range(ROWS // STRIP):
        out[owner, 4 * TILES] = top


def band_peak_kernel(pieces, peak):
    best = pieces[0, 4 * TILES]
    for source in range(1, pieces.shape[0]):
        best = jnp.maximum(best, pieces[source, 4 * TILES])
    peak[...] = best


def strips_kernel(pieces, out):
    first = pl.program_id(0) * TILES
    for source in range(pieces.shape[0]):
        for t in range(TILES):
            start = source * COLS + t * LANES
            out[0, :, start : start + LANES] = pieces[source, first + t]


def grouped(unroll, total, body, carry):
    whole = total // unroll

    def many(index, carry):
        for k in range(unroll):
            carry = body(index * unroll + k, carry)
        return carry

    carry = lax.fori_loop(0, whole, many, carry)
    for index in range(whole * unroll, total):
        carry = body(index, carry)
    return carry


def in_hbm(*arrays):
    return [pltpu.with_memory_space_constraint(a, pltpu.HBM) for a in arrays]


def vmem(count):
    return [pl.BlockSpec(memory_space=pltpu.VMEM)] * count


def shape(*dims):
    return jax.ShapeDtypeStruct(dims, jnp.float32)


def coupling_step(gas_state, wall_flags, film_state, deposit, owner_map):
    params = pltpu.CompilerParams(vmem_limit_bytes=VMEM_LIMIT)
    tail = pltpu.CompilerParams(vmem_limit_bytes=8 << 20)
    flags = jnp.transpose(wall_flags)
    gas_ring, north_main, south_main, core_pack, chip_pack, peak = pl.pallas_call(
        edges_kernel,
        out_shape=(
            shape(3, TILES + 1, RING, LANES),
            shape(4 * FIELDS, WIDE),
            shape(4 * FIELDS, WIDE),
            shape(ROWS, LANES),
            shape(ROWS, LANES),
            shape(ROWS, LANES),
        ),
        in_specs=[pl.BlockSpec(memory_space=pltpu.HBM)] * 4,
        out_specs=tuple(vmem(6)),
        scratch_shapes=[
            pltpu.VMEM((4, ROWS, COLS), jnp.float32),
            pltpu.VMEM((3, 4, ROWS, COLS), jnp.float32),
            pltpu.VMEM((ROWS, COLS), jnp.float32),
            pltpu.VMEM((TILES, ROWS), jnp.int32),
            pltpu.SemaphoreType.DMA((6,)),
        ],
        compiler_params=pltpu.CompilerParams(vmem_limit_bytes=VMEM_LIMIT),
        name="edges",
    )(*in_hbm(gas_state, flags, film_state, deposit))

    walls, gases = lax.axis_size("wall"), lax.axis_size("gas")
    partner = [(i, i ^ 1) for i in range(gases)]
    outer = [(i, (i + 1) % gases if i % 2 else (i - 1) % gases) for i in range(gases)]
    chip_side = lax.ppermute(chip_pack, "gas", outer)
    core_side = lax.ppermute(core_pack, "gas", partner)
    both = ("wall", "gas")
    peaks = lax.all_to_all(peak, both, split_axis=0, concat_axis=0, tiled=True)
    near, far = pl.pallas_call(
        corners_kernel,
        out_shape=(shape(4 * FIELDS, WIDE), shape(4 * FIELDS, WIDE)),
        in_specs=vmem(4),
        out_specs=tuple(vmem(2)),
        compiler_params=params,
        name="corners",
    )(core_side, chip_side, north_main, south_main)
    close = [(i, i ^ 1) for i in range(walls)]
    distant = [(i, (i + 1) % walls if i % 2 else (i - 1) % walls) for i in range(walls)]
    from_near = lax.ppermute(near, "wall", close)
    from_far = lax.ppermute(far, "wall", distant)

    ring_shape = (4, TILES + 1, RING, LANES)
    ring, spray, force = pl.pallas_call(
        inside_kernel,
        out_shape=(
            shape(*ring_shape),
            shape(TILES + 1, ROWS, LANES),
            shape(3, *ring_shape[1:]),
        ),
        in_specs=vmem(1) + [pl.BlockSpec(memory_space=pltpu.HBM)] * 3 + vmem(2),
        out_specs=tuple(vmem(3)),
        input_output_aliases={0: 2},
        scratch_shapes=[
            pltpu.VMEM(ring_shape[1:], jnp.float32),
            pltpu.VMEM((TILES, ROWS), jnp.int32),
            pltpu.SemaphoreType.DMA((6, TILES)),
        ],
        compiler_params=params,
        cost_estimate=pl.CostEstimate(
            flops=20 << 20, bytes_accessed=8 << 20, transcendentals=1 << 19
        ),
        name="inside",
    )(gas_ring, *in_hbm(film_state, flags, deposit), core_side, chip_side)
    pieces, _ = pl.pallas_call(
        film_kernel,
        out_shape=(shape(gases, 4 * TILES + 1, STRIP, LANES), shape(*ring_shape)),
        in_specs=[pl.BlockSpec(memory_space=pltpu.SMEM)] + vmem(8),
        out_specs=tuple(vmem(2)),
        input_output_aliases={1: 1},
        scratch_shapes=[
            pltpu.VMEM((5, TILES + 1, 24, LANES), jnp.float32),
            pltpu.VMEM(ring_shape, jnp.float32),
            pltpu.VMEM(ring_shape, jnp.float32),
            pltpu.VMEM(ring_shape, jnp.float32),
        ],
        compiler_params=params,
        name="film",
    )(
        owner_map,
        ring,
        spray,
        force,
        near,
        far,
        from_near,
        from_far,
        peaks,
    )
    pieces = lax.all_to_all(pieces, "gas", split_axis=0, concat_axis=0, tiled=True)
    band_peak = pl.pallas_call(
        band_peak_kernel,
        out_shape=shape(STRIP, LANES),
        in_specs=vmem(1),
        out_specs=vmem(1)[0],
        compiler_params=tail,
        name="band_peak",
    )(pieces)
    cfl = jnp.max(
        lax.all_to_all(band_peak, "wall", split_axis=0, concat_axis=0, tiled=True)
    )
    film_out = pl.pallas_call(
        strips_kernel,
        out_shape=shape(4, STRIP, gases * COLS),
        grid=(4,),
        in_specs=vmem(1),
        compiler_params=tail,
        out_specs=pl.BlockSpec((1, STRIP, gases * COLS), lambda i: (i, 0, 0)),
        cost_estimate=pl.CostEstimate(
            flops=0, bytes_accessed=2 << 20, transcendentals=0
        ),
        name="strips",
    )(pieces)
    return film_out, cfl


def solution(mesh):
    return jax.shard_map(
        coupling_step,
        mesh=mesh,
        in_specs=(
            P(None, None, "wall", "gas"),
            P("wall", "gas"),
            P(None, "wall", "gas"),
            P("wall", "gas"),
            P(),
        ),
        out_specs=(P(None, ("wall", "gas"), None), P()),
        check_vma=False,
    )
```

```python
import jax
import jax.numpy as jnp
from jax import lax
from jax.experimental import pallas as pl
from jax.experimental.pallas import tpu as pltpu
from jax.sharding import PartitionSpec as P


LAYER_WEIGHTS = (0.1, 0.2, 0.3, 0.4)
KAPPA = 0.41
HEIGHT_RATIO = 20.0
SPEED_FLOOR = 0.5
PRANDTL_TURB = 0.85
PRANDTL_JUMP = 3.0
LAMINAR_SHEAR = 0.3
LAMINAR_HEAT = 0.2
FILM_SPREAD = 0.24
FILM_FLOOR = 0.3
FRICTION = 0.5
COURANT = 6.0

ROWS = 128
COLS = 512
LANES = 128
TILES = COLS // LANES
FIELDS = 9
STRIP = 8
RING = ROWS + 16
WIDE = COLS + LANES
AHEAD = 8
VMEM_LIMIT = 24 << 20


def lane_iota(shape):
    return lax.broadcasted_iota(jnp.int32, shape, len(shape) - 1)


def film_speed(height, along, across):
    square = height * height + FILM_FLOOR * FILM_FLOOR
    thickness = jnp.sqrt(square)
    moving = jnp.sqrt(along * along + across * across)
    return moving / thickness + jnp.sqrt(thickness)


def halo_tile(east, west, field):
    lane = lane_iota(east.shape)
    return jnp.where(
        lane < LANES // 2,
        pltpu.roll(east, (LANES - 4 * field) % LANES, 1),
        pltpu.roll(west, (LANES - 4 - 4 * field) % LANES, 1),
    )


def sides(core, chip):
    even = lax.rem(lax.axis_index("gas"), 2) == 0
    return jnp.where(even, core, chip), jnp.where(even, chip, core)


def sample(gas, field, rows, cols):
    value = LAYER_WEIGHTS[0] * gas[field, 0, rows, cols]
    for layer in range(1, 4):
        value = value + LAYER_WEIGHTS[layer] * gas[field, layer, rows, cols]
    return value


def flag_columns(flags_by_row):
    flags = flags_by_row.astype(jnp.float32)
    return jnp.transpose(jnp.concatenate([flags, flags], axis=0))


def attached_rows(columns, rows, tile):
    count = columns[rows, tile : tile + 1]
    lane = lane_iota((count.shape[0], LANES)).astype(jnp.float32)
    return jnp.where(lane < count, 1.0, 0.0)


def edges_kernel(
    gas_hbm,
    flags_hbm,
    film_hbm,
    deposit_hbm,
    gas_ring,
    to_north,
    to_south,
    core_pack,
    chip_pack,
    peak,
    film,
    gas,
    deposit,
    flags,
    sems,
):
    copies = [
        pltpu.make_async_copy(film_hbm, film, sems.at[0]),
        pltpu.make_async_copy(flags_hbm, flags, sems.at[1]),
        pltpu.make_async_copy(deposit_hbm, deposit, sems.at[2]),
        pltpu.make_async_copy(gas_hbm.at[0], gas.at[0], sems.at[3]),
        pltpu.make_async_copy(gas_hbm.at[1], gas.at[1], sems.at[4]),
        pltpu.make_async_copy(gas_hbm.at[2], gas.at[2], sems.at[5]),
    ]
    for copy in copies:
        copy.start()
    tiles = [slice(tile * LANES, (tile + 1) * LANES) for tile in range(TILES)]
    every = slice(0, ROWS)
    even = lax.rem(lax.axis_index("gas"), 2) == 0
    lane = lane_iota((ROWS, LANES))

    def send(field, value_of):
        target = slice(4 * field, 4 * field + 4)
        for tile, cols in enumerate(tiles):
            to_north[target, cols] = value_of(slice(0, 4), tile)
            to_south[target, cols] = value_of(slice(ROWS - 4, ROWS), tile)
        west = value_of(every, 0)
        if field:
            west = pltpu.roll(west, 4 * field, 1)
        east = pltpu.roll(value_of(every, TILES - 1), 4 * field + 4, 1)
        here = (lane >= 4 * field) & (lane < 4 * field + 4)
        for pack, value in (
            (core_pack, jnp.where(even, east, west)),
            (chip_pack, jnp.where(even, west, east)),
        ):
            old = pack[...] if field else jnp.zeros_like(value)
            pack[...] = jnp.where(here, value, old)

    copies[0].wait()
    best = jnp.zeros((STRIP, LANES), jnp.float32)
    for cols in tiles:
        speed = film_speed(film[0, :, cols], film[1, :, cols], film[2, :, cols])
        for row in range(0, ROWS, STRIP):
            best = jnp.maximum(best, speed[row : row + STRIP])
    peak[...] = jnp.broadcast_to(jnp.max(best, keepdims=True), (ROWS, LANES))
    for field in range(4):
        send(field, lambda rows, tile, f=field: film[f, rows, tiles[tile]])
    copies[1].wait()
    columns = flag_columns(flags[...])
    send(8, lambda rows, tile: attached_rows(columns, rows, tile))
    copies[2].wait()
    send(7, lambda rows, tile: deposit[rows, tiles[tile]])
    for field in range(3):
        copies[3 + field].wait()
        for tile, cols in enumerate(tiles):
            gas_ring[field, tile, AHEAD : AHEAD + ROWS, :] = sample(gas, field, every, cols)
        send(
            4 + field,
            lambda rows, tile, f=field: gas_ring[
                f, tile, AHEAD + rows.start : AHEAD + rows.stop, :
            ],
        )


def even_wall():
    return lax.rem(lax.axis_index("wall"), 2) == 0


def corners_kernel(core, chip, north_in, south_in, near, far):
    even = even_wall()
    north, south = north_in[:, 0:COLS], south_in[:, 0:COLS]
    near[:, 0:COLS] = jnp.where(even, south, north)
    far[:, 0:COLS] = jnp.where(even, north, south)
    top, bottom = slice(0, 8), slice(ROWS - 8, ROWS)
    upper = sides(core[top, :], chip[top, :])
    lower = sides(core[bottom, :], chip[bottom, :])
    for field in range(FIELDS):
        target = slice(4 * field, 4 * field + 4)
        north = halo_tile(*upper, field)[0:4]
        south = halo_tile(*lower, field)[4:8]
        near[target, COLS:WIDE] = jnp.where(even, south, north)
        far[target, COLS:WIDE] = jnp.where(even, north, south)


def shifted_lanes(tiles):
    lane = lane_iota(tiles[0].shape)
    plus = [pltpu.roll(t, 1, 1) for t in tiles]
    minus = [pltpu.roll(t, LANES - 1, 1) for t in tiles]
    count = len(tiles)
    west = [jnp.where(lane == 0, plus[i - 1], plus[i]) for i in range(count)]
    east = [
        jnp.where(lane == LANES - 1, minus[(i + 1) % count], minus[i])
        for i in range(count)
    ]
    return west, east


def wall_forcing(filtered, film_heat, attached):
    along, across, gas_heat = filtered
    contrast = gas_heat - film_heat
    on_wall = attached > 0.5
    square = along * along + across * across + SPEED_FLOOR * SPEED_FLOOR
    speed = square * lax.rsqrt(square)
    height = HEIGHT_RATIO * speed
    scaled = height * lax.rsqrt(height)
    uplus = jnp.log(1.0 + KAPPA * scaled) * (1.0 / KAPPA) + 7.8 * (
        1.0
        - jnp.exp(scaled * (-1.0 / 11.0))
        - scaled * (1.0 / 11.0) * jnp.exp(scaled * (-1.0 / 3.0))
    )
    factor = jnp.where(on_wall, speed / (uplus * uplus), LAMINAR_SHEAR)
    heat = jnp.where(
        on_wall, speed / (PRANDTL_TURB * uplus + PRANDTL_JUMP), LAMINAR_HEAT
    )
    return factor * along, factor * across, heat * contrast


def inside_kernel(
    gas_in,
    film_hbm,
    flags_hbm,
    deposit_hbm,
    core,
    chip,
    ring,
    spray,
    force,
    attached,
    flags,
    sems,
):
    del gas_in
    count = TILES + 1
    inner = slice(8, 8 + ROWS)
    flags_copy = pltpu.make_async_copy(flags_hbm, flags, sems.at[5, 0])
    flags_copy.start()
    arriving = {}
    for field in (3, 0, 1, 2, 4):
        arriving[field] = []
        for tile in range(TILES):
            cols = slice(tile * LANES, (tile + 1) * LANES)
            if field < 4:
                source, target = film_hbm.at[field, :, cols], ring.at[field, tile, inner]
            else:
                source, target = deposit_hbm.at[:, cols], spray.at[tile]
            copy = pltpu.make_async_copy(source, target, sems.at[field, tile])
            copy.start()
            arriving[field].append(copy)

    east, west = sides(core[...], chip[...])
    for field in range(4):
        ring[field, TILES, inner, :] = halo_tile(east, west, field)
    for field in range(3):
        force[field, TILES, AHEAD : AHEAD + ROWS, :] = halo_tile(east, west, 4 + field)
    spray[TILES] = halo_tile(east, west, 7)
    attached[TILES, 0:ROWS, :] = halo_tile(east, west, 8)
    flags_copy.wait()
    columns = flag_columns(flags[...])
    for tile in range(TILES):
        attached[tile, 0:ROWS, :] = attached_rows(columns, slice(0, ROWS), tile)
    for copy in arriving[3]:
        copy.wait()

    def forcing_rows(index, carry):
        row = 1 + 8 * index
        here = pl.ds(row, STRIP)
        filtered = []
        for field in range(3):
            summed = [
                force[field, t, pl.ds(row + AHEAD - 1, STRIP), :]
                + force[field, t, pl.ds(row + AHEAD, STRIP), :]
                + force[field, t, pl.ds(row + AHEAD + 1, STRIP), :]
                for t in range(count)
            ]
            west, east = shifted_lanes(summed)
            filtered.append(
                [(west[t] + summed[t] + east[t]) * (1.0 / 9.0) for t in range(count)]
            )
        for t in range(count):
            result = wall_forcing(
                [filtered[f][t] for f in range(3)],
                ring[3, t, pl.ds(row + 8, STRIP), :],
                attached[t, here, :],
            )
            for field in range(3):
                force[field, t, here, :] = result[field]
        return carry

    grouped(4, 16, forcing_rows, 0)
    for field in (0, 1, 2, 4):
        for copy in arriving[field]:
            copy.wait()


def film_kernel(
    owner_map,
    ring_in,
    spray,
    force_in,
    near_sent,
    far_sent,
    near,
    far,
    peaks,
    out,
    ring,
    stack,
    ring_a,
    ring_b,
    force,
):
    del ring_in
    count = TILES + 1
    wall = lax.axis_index("wall")
    step = COURANT / jnp.max(peaks[...])
    inner = slice(8, 8 + ROWS)
    above, below = slice(4, 8), slice(8 + ROWS, 12 + ROWS)

    even = even_wall()

    def pair(field, cols, close, distant):
        rows = slice(4 * field, 4 * field + 4)
        one, two = close[rows, cols], distant[rows, cols]
        return jnp.where(even, two, one), jnp.where(even, one, two)

    for tile in range(count):
        cols = slice(tile * LANES, (tile + 1) * LANES)
        arrived = [pair(field, cols, near, far) for field in range(FIELDS)]
        for field in range(4):
            ring[field, tile, above, :], ring[field, tile, below, :] = arrived[field]
        force[3, tile, above, :] = step * arrived[7][0]
        force[3, tile, inner, :] = step * spray[tile]
        force[3, tile, below, :] = step * arrived[7][1]
        for index, field in enumerate((4, 5, 6, 3, 8)):
            own = pair(field, cols, near_sent, far_sent)
            stack[index, tile, 0:4, :] = arrived[field][0]
            stack[index, tile, 4:8, :] = own[0]
            stack[index, tile, 8:12, :] = own[1]
            stack[index, tile, 12:16, :] = arrived[field][1]

    def scale_rows(index, carry):
        row = 1 + 8 * index
        for field in range(3):
            for t in range(count):
                force[field, t, pl.ds(row + 8, STRIP), :] = (
                    step * force_in[field, t, pl.ds(row, STRIP), :]
                )
        return carry

    grouped(4, 16, scale_rows, 0)
    for start, first, target in ((1, 0, 5), (8, 3, 135)):
        filtered = []
        for field in range(3):
            summed = [
                stack[field, t, start - 1 : start - 1 + STRIP, :]
                + stack[field, t, start : start + STRIP, :]
                + stack[field, t, start + 1 : start + 1 + STRIP, :]
                for t in range(count)
            ]
            west, east = shifted_lanes(summed)
            filtered.append(
                [(west[t] + summed[t] + east[t]) * (1.0 / 9.0) for t in range(count)]
            )
        for t in range(count):
            rows = slice(start, start + STRIP)
            result = wall_forcing(
                [filtered[f][t] for f in range(3)], stack[3, t, rows, :], stack[4, t, rows, :]
            )
            for field in range(3):
                force[field, t, target : target + 4, :] = (
                    step * result[field][first : first + 4]
                )

    half = 0.5 * step

    def advance(load, row):
        here = pl.ds(row, STRIP)
        centre, wests, easts, norths, souths = [], [], [], [], []
        for field in range(4):
            middle = [load(field, t, here) for t in range(count)]
            north = [load(field, t, pl.ds(row - 1, STRIP)) for t in range(count)]
            south = [load(field, t, pl.ds(row + 1, STRIP)) for t in range(count)]
            west, east = shifted_lanes(middle)
            centre.append(middle)
            wests.append(west)
            easts.append(east)
            norths.append(north)
            souths.append(south)
        news = []
        keep = 1.0 - 4.0 * FILM_SPREAD
        for t in range(count):
            mixed = [
                FILM_SPREAD
                * ((norths[f][t] + souths[f][t]) + (wests[f][t] + easts[f][t]))
                for f in range(4)
            ]
            height = centre[0][t]
            inverse = lax.rsqrt(height * height + FILM_FLOOR * FILM_FLOOR)
            keep_moving = keep - (FRICTION * step) * inverse
            slope = half * height
            height_new = (
                keep * height
                + mixed[0]
                + force[3, t, here, :]
                - half * ((easts[1][t] - wests[1][t]) + (souths[2][t] - norths[2][t]))
            )
            along_new = (
                keep_moving * centre[1][t]
                + mixed[1]
                + force[0, t, here, :]
                - slope * (easts[0][t] - wests[0][t])
            )
            across_new = (
                keep_moving * centre[2][t]
                + mixed[2]
                + force[1, t, here, :]
                - slope * (souths[0][t] - norths[0][t])
            )
            heat_new = (
                keep * centre[3][t] + mixed[3] + force[2, t, here, :] * inverse
            )
            news.append((height_new, along_new, across_new, heat_new))
        return news

    def middle_rows(source, target):
        def body(index, carry):
            row = 4 + 8 * index
            news = advance(source, row)
            for t in range(count):
                for field in range(4):
                    target[field, t, pl.ds(row, STRIP), :] = news[t][field]
            return carry

        grouped(17, 17, body, 0)

    def load_from(source):
        return lambda field, t, rows: source[field, t, rows, :]

    middle_rows(load_from(ring), ring_a)
    middle_rows(load_from(ring_a), ring_b)
    middle_rows(load_from(ring_b), ring_a)

    def last_rows(index, best):
        row = pl.multiple_of(8 + 8 * index, 8)
        news = advance(load_from(ring_a), row)
        place = owner_map[wall, index]
        for t in range(TILES):
            for field in range(4):
                out[place, field * TILES + t] = news[t][field]
            best = jnp.maximum(best, film_speed(*news[t][:3]))
        return best

    best = grouped(16, 16, last_rows, jnp.zeros((STRIP, LANES), jnp.float32))
    top = jnp.broadcast_to(step * jnp.max(best, keepdims=True), (STRIP, LANES))
    for owner in range(ROWS // STRIP):
        out[owner, 4 * TILES] = top


def band_peak_kernel(pieces, peak):
    best = pieces[0, 4 * TILES]
    for source in range(1, pieces.shape[0]):
        best = jnp.maximum(best, pieces[source, 4 * TILES])
    peak[...] = best


def strips_kernel(pieces, out):
    first = pl.program_id(0) * TILES
    for source in range(pieces.shape[0]):
        for t in range(TILES):
            start = source * COLS + t * LANES
            out[0, :, start : start + LANES] = pieces[source, first + t]


def grouped(unroll, total, body, carry):
    whole = total // unroll

    def many(index, carry):
        for k in range(unroll):
            carry = body(index * unroll + k, carry)
        return carry

    carry = lax.fori_loop(0, whole, many, carry)
    for index in range(whole * unroll, total):
        carry = body(index, carry)
    return carry


def in_hbm(*arrays):
    return [pltpu.with_memory_space_constraint(a, pltpu.HBM) for a in arrays]


def vmem(count):
    return [pl.BlockSpec(memory_space=pltpu.VMEM)] * count


def shape(*dims):
    return jax.ShapeDtypeStruct(dims, jnp.float32)


def coupling_step(gas_state, wall_flags, film_state, deposit, owner_map):
    params = pltpu.CompilerParams(vmem_limit_bytes=VMEM_LIMIT)
    tail = pltpu.CompilerParams(vmem_limit_bytes=8 << 20)
    flags = jnp.transpose(wall_flags)
    gas_ring, north_main, south_main, core_pack, chip_pack, peak = pl.pallas_call(
        edges_kernel,
        out_shape=(
            shape(3, TILES + 1, RING, LANES),
            shape(4 * FIELDS, WIDE),
            shape(4 * FIELDS, WIDE),
            shape(ROWS, LANES),
            shape(ROWS, LANES),
            shape(ROWS, LANES),
        ),
        in_specs=[pl.BlockSpec(memory_space=pltpu.HBM)] * 4,
        out_specs=tuple(vmem(6)),
        scratch_shapes=[
            pltpu.VMEM((4, ROWS, COLS), jnp.float32),
            pltpu.VMEM((3, 4, ROWS, COLS), jnp.float32),
            pltpu.VMEM((ROWS, COLS), jnp.float32),
            pltpu.VMEM((TILES, ROWS), jnp.int32),
            pltpu.SemaphoreType.DMA((6,)),
        ],
        compiler_params=pltpu.CompilerParams(vmem_limit_bytes=VMEM_LIMIT),
        name="edges",
    )(*in_hbm(gas_state, flags, film_state, deposit))

    walls, gases = lax.axis_size("wall"), lax.axis_size("gas")
    partner = [(i, i ^ 1) for i in range(gases)]
    outer = [(i, (i + 1) % gases if i % 2 else (i - 1) % gases) for i in range(gases)]
    chip_side = lax.ppermute(chip_pack, "gas", outer)
    core_side = lax.ppermute(core_pack, "gas", partner)
    both = ("wall", "gas")
    peaks = lax.all_to_all(peak, both, split_axis=0, concat_axis=0, tiled=True)
    near, far = pl.pallas_call(
        corners_kernel,
        out_shape=(shape(4 * FIELDS, WIDE), shape(4 * FIELDS, WIDE)),
        in_specs=vmem(4),
        out_specs=tuple(vmem(2)),
        compiler_params=params,
        name="corners",
    )(core_side, chip_side, north_main, south_main)
    close = [(i, i ^ 1) for i in range(walls)]
    distant = [(i, (i + 1) % walls if i % 2 else (i - 1) % walls) for i in range(walls)]
    from_near = lax.ppermute(near, "wall", close)
    from_far = lax.ppermute(far, "wall", distant)

    ring_shape = (4, TILES + 1, RING, LANES)
    ring, spray, force = pl.pallas_call(
        inside_kernel,
        out_shape=(
            shape(*ring_shape),
            shape(TILES + 1, ROWS, LANES),
            shape(3, *ring_shape[1:]),
        ),
        in_specs=vmem(1) + [pl.BlockSpec(memory_space=pltpu.HBM)] * 3 + vmem(2),
        out_specs=tuple(vmem(3)),
        input_output_aliases={0: 2},
        scratch_shapes=[
            pltpu.VMEM(ring_shape[1:], jnp.float32),
            pltpu.VMEM((TILES, ROWS), jnp.int32),
            pltpu.SemaphoreType.DMA((6, TILES)),
        ],
        compiler_params=params,
        cost_estimate=pl.CostEstimate(
            flops=20 << 20, bytes_accessed=8 << 20, transcendentals=1 << 19
        ),
        name="inside",
    )(gas_ring, *in_hbm(film_state, flags, deposit), core_side, chip_side)
    pieces, _ = pl.pallas_call(
        film_kernel,
        out_shape=(shape(gases, 4 * TILES + 1, STRIP, LANES), shape(*ring_shape)),
        in_specs=[pl.BlockSpec(memory_space=pltpu.SMEM)] + vmem(8),
        out_specs=tuple(vmem(2)),
        input_output_aliases={1: 1},
        scratch_shapes=[
            pltpu.VMEM((5, TILES + 1, 24, LANES), jnp.float32),
            pltpu.VMEM(ring_shape, jnp.float32),
            pltpu.VMEM(ring_shape, jnp.float32),
            pltpu.VMEM(ring_shape, jnp.float32),
        ],
        compiler_params=params,
        name="film",
    )(
        owner_map,
        ring,
        spray,
        force,
        near,
        far,
        from_near,
        from_far,
        peaks,
    )
    pieces = lax.all_to_all(pieces, "gas", split_axis=0, concat_axis=0, tiled=True)
    band_peak = pl.pallas_call(
        band_peak_kernel,
        out_shape=shape(STRIP, LANES),
        in_specs=vmem(1),
        out_specs=vmem(1)[0],
        compiler_params=tail,
        name="band_peak",
    )(pieces)
    cfl = jnp.max(
        lax.all_to_all(band_peak, "wall", split_axis=0, concat_axis=0, tiled=True)
    )
    film_out = pl.pallas_call(
        strips_kernel,
        out_shape=shape(4, STRIP, gases * COLS),
        grid=(4,),
        in_specs=vmem(1),
        compiler_params=tail,
        out_specs=pl.BlockSpec((1, STRIP, gases * COLS), lambda i: (i, 0, 0)),
        cost_estimate=pl.CostEstimate(
            flops=0, bytes_accessed=2 << 20, transcendentals=0
        ),
        name="strips",
    )(pieces)
    return film_out, cfl


def solution(mesh):
    return jax.shard_map(
        coupling_step,
        mesh=mesh,
        in_specs=(
            P(None, None, "wall", "gas"),
            P("wall", "gas"),
            P(None, "wall", "gas"),
            P("wall", "gas"),
            P(),
        ),
        out_specs=(P(None, ("wall", "gas"), None), P()),
        check_vma=False,
    )
```

```python
import jax
import jax.numpy as jnp
from jax import lax
from jax.experimental import pallas as pl
from jax.experimental.pallas import tpu as pltpu
from jax.sharding import PartitionSpec as P


LAYER_WEIGHTS = (0.1, 0.2, 0.3, 0.4)
KAPPA = 0.41
HEIGHT_RATIO = 20.0
SPEED_FLOOR = 0.5
PRANDTL_TURB = 0.85
PRANDTL_JUMP = 3.0
LAMINAR_SHEAR = 0.3
LAMINAR_HEAT = 0.2
FILM_SPREAD = 0.24
FILM_FLOOR = 0.3
FRICTION = 0.5
COURANT = 6.0

ROWS = 128
COLS = 512
LANES = 128
TILES = COLS // LANES
FIELDS = 9
STRIP = 8
RING = ROWS + 16
WIDE = COLS + LANES
AHEAD = 8
VMEM_LIMIT = 24 << 20


def lane_iota(shape):
    return lax.broadcasted_iota(jnp.int32, shape, len(shape) - 1)


def film_speed(height, along, across):
    square = height * height + FILM_FLOOR * FILM_FLOOR
    inverse = lax.rsqrt(square)
    thickness = square * inverse
    moving = jnp.sqrt(along * along + across * across)
    return moving * inverse + thickness * lax.rsqrt(thickness)


def halo_tile(east, west, field):
    lane = lane_iota(east.shape)
    return jnp.where(
        lane < LANES // 2,
        pltpu.roll(east, (LANES - 4 * field) % LANES, 1),
        pltpu.roll(west, (LANES - 4 - 4 * field) % LANES, 1),
    )


def sides(core, chip):
    even = lax.rem(lax.axis_index("gas"), 2) == 0
    return jnp.where(even, core, chip), jnp.where(even, chip, core)


def sample(gas, field, rows, cols):
    value = LAYER_WEIGHTS[0] * gas[field, 0, rows, cols]
    for layer in range(1, 4):
        value = value + LAYER_WEIGHTS[layer] * gas[field, layer, rows, cols]
    return value


def flag_columns(flags_by_row):
    flags = flags_by_row.astype(jnp.float32)
    return jnp.transpose(jnp.concatenate([flags, flags], axis=0))


def attached_rows(columns, rows, tile):
    count = columns[rows, tile : tile + 1]
    lane = lane_iota((count.shape[0], LANES)).astype(jnp.float32)
    return jnp.where(lane < count, 1.0, 0.0)


def edges_kernel(
    gas_hbm,
    flags_hbm,
    film_hbm,
    deposit_hbm,
    gas_ring,
    to_north,
    to_south,
    core_pack,
    chip_pack,
    peak,
    film,
    gas,
    deposit,
    flags,
    sems,
):
    pairs = [(flags_hbm, flags), (deposit_hbm, deposit)]
    pairs += [(film_hbm.at[field], film.at[field]) for field in range(4)]
    pairs += [(gas_hbm.at[field], gas.at[field]) for field in range(3)]
    copies = [
        pltpu.make_async_copy(source, target, sems.at[index])
        for index, (source, target) in enumerate(pairs)
    ]
    for copy in copies:
        copy.start()
    tiles = [slice(tile * LANES, (tile + 1) * LANES) for tile in range(TILES)]
    every = slice(0, ROWS)
    even = lax.rem(lax.axis_index("gas"), 2) == 0
    lane = lane_iota((ROWS, LANES))

    def send(field, value_of, fresh=False):
        target = slice(4 * field, 4 * field + 4)
        for tile, cols in enumerate(tiles):
            to_north[target, cols] = value_of(slice(0, 4), tile)
            to_south[target, cols] = value_of(slice(ROWS - 4, ROWS), tile)
        west = value_of(every, 0)
        if field:
            west = pltpu.roll(west, 4 * field, 1)
        east = pltpu.roll(value_of(every, TILES - 1), 4 * field + 4, 1)
        here = (lane >= 4 * field) & (lane < 4 * field + 4)
        for pack, value in (
            (core_pack, jnp.where(even, east, west)),
            (chip_pack, jnp.where(even, west, east)),
        ):
            old = jnp.zeros_like(value) if fresh else pack[...]
            pack[...] = jnp.where(here, value, old)

    copies[0].wait()
    columns = flag_columns(flags[...])
    send(8, lambda rows, tile: attached_rows(columns, rows, tile), True)
    copies[1].wait()
    send(7, lambda rows, tile: deposit[rows, tiles[tile]])
    for field in range(4):
        copies[2 + field].wait()
        send(field, lambda rows, tile, f=field: film[f, rows, tiles[tile]])
        if field == 2:
            best = jnp.zeros((STRIP, LANES), jnp.float32)
            for cols in tiles:
                speed = film_speed(film[0, :, cols], film[1, :, cols], film[2, :, cols])
                for row in range(0, ROWS, STRIP):
                    best = jnp.maximum(best, speed[row : row + STRIP])
            peak[...] = jnp.broadcast_to(jnp.max(best, keepdims=True), (ROWS, LANES))
    for field in range(3):
        copies[6 + field].wait()
        for tile, cols in enumerate(tiles):
            gas_ring[field, tile, AHEAD : AHEAD + ROWS, :] = sample(
                gas, field, every, cols
            )
        send(
            4 + field,
            lambda rows, tile, f=field: gas_ring[
                f, tile, AHEAD + rows.start : AHEAD + rows.stop, :
            ],
        )


def even_wall():
    return lax.rem(lax.axis_index("wall"), 2) == 0


def corners_kernel(core, chip, north_in, south_in, near, far):
    even = even_wall()
    north, south = north_in[:, 0:COLS], south_in[:, 0:COLS]
    near[:, 0:COLS] = jnp.where(even, south, north)
    far[:, 0:COLS] = jnp.where(even, north, south)
    top, bottom = slice(0, 8), slice(ROWS - 8, ROWS)
    upper = sides(core[top, :], chip[top, :])
    lower = sides(core[bottom, :], chip[bottom, :])
    for field in range(FIELDS):
        target = slice(4 * field, 4 * field + 4)
        north = halo_tile(*upper, field)[0:4]
        south = halo_tile(*lower, field)[4:8]
        near[target, COLS:WIDE] = jnp.where(even, south, north)
        far[target, COLS:WIDE] = jnp.where(even, north, south)


def shifted_lanes(tiles):
    lane = lane_iota(tiles[0].shape)
    plus = [pltpu.roll(t, 1, 1) for t in tiles]
    minus = [pltpu.roll(t, LANES - 1, 1) for t in tiles]
    count = len(tiles)
    west = [jnp.where(lane == 0, plus[i - 1], plus[i]) for i in range(count)]
    east = [
        jnp.where(lane == LANES - 1, minus[(i + 1) % count], minus[i])
        for i in range(count)
    ]
    return west, east


def wall_forcing(filtered, film_heat, attached):
    along, across, gas_heat = filtered
    contrast = gas_heat - film_heat
    on_wall = attached > 0.5
    square = along * along + across * across + SPEED_FLOOR * SPEED_FLOOR
    speed = square * lax.rsqrt(square)
    height = HEIGHT_RATIO * speed
    scaled = height * lax.rsqrt(height)
    uplus = jnp.log(1.0 + KAPPA * scaled) * (1.0 / KAPPA) + 7.8 * (
        1.0
        - jnp.exp(scaled * (-1.0 / 11.0))
        - scaled * (1.0 / 11.0) * jnp.exp(scaled * (-1.0 / 3.0))
    )
    factor = jnp.where(on_wall, speed / (uplus * uplus), LAMINAR_SHEAR)
    heat = jnp.where(
        on_wall, speed / (PRANDTL_TURB * uplus + PRANDTL_JUMP), LAMINAR_HEAT
    )
    return factor * along, factor * across, heat * contrast


def inside_kernel(
    gas_in,
    film_hbm,
    flags_hbm,
    deposit_hbm,
    core,
    chip,
    ring,
    spray,
    force,
    attached,
    flags,
    sems,
):
    del gas_in
    count = TILES + 1
    inner = slice(8, 8 + ROWS)
    flags_copy = pltpu.make_async_copy(flags_hbm, flags, sems.at[5, 0])
    flags_copy.start()
    arriving = {}
    for field in (3, 0, 1, 2, 4):
        arriving[field] = []
        for tile in range(TILES):
            cols = slice(tile * LANES, (tile + 1) * LANES)
            if field < 4:
                source, target = film_hbm.at[field, :, cols], ring.at[field, tile, inner]
            else:
                source, target = deposit_hbm.at[:, cols], spray.at[tile]
            copy = pltpu.make_async_copy(source, target, sems.at[field, tile])
            copy.start()
            arriving[field].append(copy)

    east, west = sides(core[...], chip[...])
    for field in range(4):
        ring[field, TILES, inner, :] = halo_tile(east, west, field)
    for field in range(3):
        force[field, TILES, AHEAD : AHEAD + ROWS, :] = halo_tile(east, west, 4 + field)
    spray[TILES] = halo_tile(east, west, 7)
    attached[TILES, 0:ROWS, :] = halo_tile(east, west, 8)
    flags_copy.wait()
    columns = flag_columns(flags[...])
    for tile in range(TILES):
        attached[tile, 0:ROWS, :] = attached_rows(columns, slice(0, ROWS), tile)
    for copy in arriving[3]:
        copy.wait()

    def forcing_rows(index, carry):
        row = 1 + 8 * index
        here = pl.ds(row, STRIP)
        filtered = []
        for field in range(3):
            summed = [
                force[field, t, pl.ds(row + AHEAD - 1, STRIP), :]
                + force[field, t, pl.ds(row + AHEAD, STRIP), :]
                + force[field, t, pl.ds(row + AHEAD + 1, STRIP), :]
                for t in range(count)
            ]
            west, east = shifted_lanes(summed)
            filtered.append(
                [(west[t] + summed[t] + east[t]) * (1.0 / 9.0) for t in range(count)]
            )
        for t in range(count):
            result = wall_forcing(
                [filtered[f][t] for f in range(3)],
                ring[3, t, pl.ds(row + 8, STRIP), :],
                attached[t, here, :],
            )
            for field in range(3):
                force[field, t, here, :] = result[field]
        return carry

    grouped(4, 16, forcing_rows, 0)
    for field in (0, 1, 2, 4):
        for copy in arriving[field]:
            copy.wait()


def film_kernel(
    owner_map,
    ring_in,
    spray,
    force_in,
    near_sent,
    far_sent,
    near,
    far,
    peaks,
    out,
    ring,
    stack,
    ring_a,
    ring_b,
    force,
):
    del ring_in
    count = TILES + 1
    wall = lax.axis_index("wall")
    step = COURANT / jnp.max(peaks[...])
    inner = slice(8, 8 + ROWS)
    above, below = slice(4, 8), slice(8 + ROWS, 12 + ROWS)

    even = even_wall()

    def pair(field, cols, close, distant):
        rows = slice(4 * field, 4 * field + 4)
        one, two = close[rows, cols], distant[rows, cols]
        return jnp.where(even, two, one), jnp.where(even, one, two)

    for tile in range(count):
        cols = slice(tile * LANES, (tile + 1) * LANES)
        arrived = [pair(field, cols, near, far) for field in range(FIELDS)]
        for field in range(4):
            ring[field, tile, above, :], ring[field, tile, below, :] = arrived[field]
        force[3, tile, above, :] = step * arrived[7][0]
        force[3, tile, inner, :] = step * spray[tile]
        force[3, tile, below, :] = step * arrived[7][1]
        for index, field in enumerate((4, 5, 6, 3, 8)):
            own = pair(field, cols, near_sent, far_sent)
            stack[index, tile, 0:4, :] = arrived[field][0]
            stack[index, tile, 4:8, :] = own[0]
            stack[index, tile, 8:12, :] = own[1]
            stack[index, tile, 12:16, :] = arrived[field][1]

    def scale_rows(index, carry):
        row = 1 + 8 * index
        for field in range(3):
            for t in range(count):
                force[field, t, pl.ds(row + 8, STRIP), :] = (
                    step * force_in[field, t, pl.ds(row, STRIP), :]
                )
        return carry

    grouped(4, 16, scale_rows, 0)
    for start, first, target in ((1, 0, 5), (8, 3, 135)):
        filtered = []
        for field in range(3):
            summed = [
                stack[field, t, start - 1 : start - 1 + STRIP, :]
                + stack[field, t, start : start + STRIP, :]
                + stack[field, t, start + 1 : start + 1 + STRIP, :]
                for t in range(count)
            ]
            west, east = shifted_lanes(summed)
            filtered.append(
                [(west[t] + summed[t] + east[t]) * (1.0 / 9.0) for t in range(count)]
            )
        for t in range(count):
            rows = slice(start, start + STRIP)
            result = wall_forcing(
                [filtered[f][t] for f in range(3)], stack[3, t, rows, :], stack[4, t, rows, :]
            )
            for field in range(3):
                force[field, t, target : target + 4, :] = (
                    step * result[field][first : first + 4]
                )

    half = 0.5 * step

    def advance(load, row):
        here = pl.ds(row, STRIP)
        centre, wests, easts, norths, souths = [], [], [], [], []
        for field in range(4):
            middle = [load(field, t, here) for t in range(count)]
            north = [load(field, t, pl.ds(row - 1, STRIP)) for t in range(count)]
            south = [load(field, t, pl.ds(row + 1, STRIP)) for t in range(count)]
            west, east = shifted_lanes(middle)
            centre.append(middle)
            wests.append(west)
            easts.append(east)
            norths.append(north)
            souths.append(south)
        news = []
        keep = 1.0 - 4.0 * FILM_SPREAD
        for t in range(count):
            mixed = [
                FILM_SPREAD
                * ((norths[f][t] + souths[f][t]) + (wests[f][t] + easts[f][t]))
                for f in range(4)
            ]
            height = centre[0][t]
            inverse = lax.rsqrt(height * height + FILM_FLOOR * FILM_FLOOR)
            keep_moving = keep - (FRICTION * step) * inverse
            slope = half * height
            height_new = (
                keep * height
                + mixed[0]
                + force[3, t, here, :]
                - half * ((easts[1][t] - wests[1][t]) + (souths[2][t] - norths[2][t]))
            )
            along_new = (
                keep_moving * centre[1][t]
                + mixed[1]
                + force[0, t, here, :]
                - slope * (easts[0][t] - wests[0][t])
            )
            across_new = (
                keep_moving * centre[2][t]
                + mixed[2]
                + force[1, t, here, :]
                - slope * (souths[0][t] - norths[0][t])
            )
            heat_new = (
                keep * centre[3][t] + mixed[3] + force[2, t, here, :] * inverse
            )
            news.append((height_new, along_new, across_new, heat_new))
        return news

    def middle_rows(source, target):
        def body(index, carry):
            row = 4 + 8 * index
            news = advance(source, row)
            for t in range(count):
                for field in range(4):
                    target[field, t, pl.ds(row, STRIP), :] = news[t][field]
            return carry

        grouped(17, 17, body, 0)

    def load_from(source):
        return lambda field, t, rows: source[field, t, rows, :]

    middle_rows(load_from(ring), ring_a)
    middle_rows(load_from(ring_a), ring_b)
    middle_rows(load_from(ring_b), ring_a)

    def last_rows(index, best):
        row = pl.multiple_of(8 + 8 * index, 8)
        news = advance(load_from(ring_a), row)
        place = owner_map[wall, index]
        for t in range(TILES):
            for field in range(4):
                out[place, field * TILES + t] = news[t][field]
            best = jnp.maximum(best, film_speed(*news[t][:3]))
        return best

    best = grouped(16, 16, last_rows, jnp.zeros((STRIP, LANES), jnp.float32))
    top = jnp.broadcast_to(step * jnp.max(best, keepdims=True), (STRIP, LANES))
    for owner in range(ROWS // STRIP):
        out[owner, 4 * TILES] = top


def band_peak_kernel(pieces, peak):
    best = pieces[0, 4 * TILES]
    for source in range(1, pieces.shape[0]):
        best = jnp.maximum(best, pieces[source, 4 * TILES])
    peak[...] = best


def strips_kernel(pieces, out):
    first = pl.program_id(0) * TILES
    for source in range(pieces.shape[0]):
        for t in range(TILES):
            start = source * COLS + t * LANES
            out[0, :, start : start + LANES] = pieces[source, first + t]


def grouped(unroll, total, body, carry):
    whole = total // unroll

    def many(index, carry):
        for k in range(unroll):
            carry = body(index * unroll + k, carry)
        return carry

    carry = lax.fori_loop(0, whole, many, carry)
    for index in range(whole * unroll, total):
        carry = body(index, carry)
    return carry


def in_hbm(*arrays):
    return [pltpu.with_memory_space_constraint(a, pltpu.HBM) for a in arrays]


def vmem(count):
    return [pl.BlockSpec(memory_space=pltpu.VMEM)] * count


def shape(*dims):
    return jax.ShapeDtypeStruct(dims, jnp.float32)


def coupling_step(gas_state, wall_flags, film_state, deposit, owner_map):
    params = pltpu.CompilerParams(vmem_limit_bytes=VMEM_LIMIT)
    tail = pltpu.CompilerParams(vmem_limit_bytes=8 << 20)
    flags = jnp.transpose(wall_flags)
    gas_ring, north_main, south_main, core_pack, chip_pack, peak = pl.pallas_call(
        edges_kernel,
        out_shape=(
            shape(3, TILES + 1, RING, LANES),
            shape(4 * FIELDS, WIDE),
            shape(4 * FIELDS, WIDE),
            shape(ROWS, LANES),
            shape(ROWS, LANES),
            shape(ROWS, LANES),
        ),
        in_specs=[pl.BlockSpec(memory_space=pltpu.HBM)] * 4,
        out_specs=tuple(vmem(6)),
        scratch_shapes=[
            pltpu.VMEM((4, ROWS, COLS), jnp.float32),
            pltpu.VMEM((3, 4, ROWS, COLS), jnp.float32),
            pltpu.VMEM((ROWS, COLS), jnp.float32),
            pltpu.VMEM((TILES, ROWS), jnp.int32),
            pltpu.SemaphoreType.DMA((9,)),
        ],
        compiler_params=pltpu.CompilerParams(vmem_limit_bytes=VMEM_LIMIT),
        name="edges",
    )(*in_hbm(gas_state, flags, film_state, deposit))

    walls, gases = lax.axis_size("wall"), lax.axis_size("gas")
    partner = [(i, i ^ 1) for i in range(gases)]
    outer = [(i, (i + 1) % gases if i % 2 else (i - 1) % gases) for i in range(gases)]
    chip_side = lax.ppermute(chip_pack, "gas", outer)
    core_side = lax.ppermute(core_pack, "gas", partner)
    both = ("wall", "gas")
    peaks = lax.all_to_all(peak, both, split_axis=0, concat_axis=0, tiled=True)
    near, far = pl.pallas_call(
        corners_kernel,
        out_shape=(shape(4 * FIELDS, WIDE), shape(4 * FIELDS, WIDE)),
        in_specs=vmem(4),
        out_specs=tuple(vmem(2)),
        compiler_params=params,
        name="corners",
    )(core_side, chip_side, north_main, south_main)
    close = [(i, i ^ 1) for i in range(walls)]
    distant = [(i, (i + 1) % walls if i % 2 else (i - 1) % walls) for i in range(walls)]
    from_near = lax.ppermute(near, "wall", close)
    from_far = lax.ppermute(far, "wall", distant)

    ring_shape = (4, TILES + 1, RING, LANES)
    ring, spray, force = pl.pallas_call(
        inside_kernel,
        out_shape=(
            shape(*ring_shape),
            shape(TILES + 1, ROWS, LANES),
            shape(3, *ring_shape[1:]),
        ),
        in_specs=vmem(1) + [pl.BlockSpec(memory_space=pltpu.HBM)] * 3 + vmem(2),
        out_specs=tuple(vmem(3)),
        input_output_aliases={0: 2},
        scratch_shapes=[
            pltpu.VMEM(ring_shape[1:], jnp.float32),
            pltpu.VMEM((TILES, ROWS), jnp.int32),
            pltpu.SemaphoreType.DMA((6, TILES)),
        ],
        compiler_params=params,
        cost_estimate=pl.CostEstimate(
            flops=20 << 20, bytes_accessed=8 << 20, transcendentals=1 << 19
        ),
        name="inside",
    )(gas_ring, *in_hbm(film_state, flags, deposit), core_side, chip_side)
    pieces, _ = pl.pallas_call(
        film_kernel,
        out_shape=(shape(gases, 4 * TILES + 1, STRIP, LANES), shape(*ring_shape)),
        in_specs=[pl.BlockSpec(memory_space=pltpu.SMEM)] + vmem(8),
        out_specs=tuple(vmem(2)),
        input_output_aliases={1: 1},
        scratch_shapes=[
            pltpu.VMEM((5, TILES + 1, 24, LANES), jnp.float32),
            pltpu.VMEM(ring_shape, jnp.float32),
            pltpu.VMEM(ring_shape, jnp.float32),
            pltpu.VMEM(ring_shape, jnp.float32),
        ],
        compiler_params=params,
        name="film",
    )(
        owner_map,
        ring,
        spray,
        force,
        near,
        far,
        from_near,
        from_far,
        peaks,
    )
    pieces = lax.all_to_all(pieces, "gas", split_axis=0, concat_axis=0, tiled=True)
    band_peak = pl.pallas_call(
        band_peak_kernel,
        out_shape=shape(STRIP, LANES),
        in_specs=vmem(1),
        out_specs=vmem(1)[0],
        compiler_params=tail,
        name="band_peak",
    )(pieces)
    cfl = jnp.max(
        lax.all_to_all(band_peak, "wall", split_axis=0, concat_axis=0, tiled=True)
    )
    film_out = pl.pallas_call(
        strips_kernel,
        out_shape=shape(4, STRIP, gases * COLS),
        grid=(4,),
        in_specs=vmem(1),
        compiler_params=tail,
        out_specs=pl.BlockSpec((1, STRIP, gases * COLS), lambda i: (i, 0, 0)),
        cost_estimate=pl.CostEstimate(
            flops=0, bytes_accessed=2 << 20, transcendentals=0
        ),
        name="strips",
    )(pieces)
    return film_out, cfl


def solution(mesh):
    return jax.shard_map(
        coupling_step,
        mesh=mesh,
        in_specs=(
            P(None, None, "wall", "gas"),
            P("wall", "gas"),
            P(None, "wall", "gas"),
            P("wall", "gas"),
            P(),
        ),
        out_specs=(P(None, ("wall", "gas"), None), P()),
        check_vma=False,
    )
```

```python
import jax
import jax.numpy as jnp
from jax import lax
from jax.experimental import pallas as pl
from jax.experimental.pallas import tpu as pltpu
from jax.sharding import PartitionSpec as P


LAYER_WEIGHTS = (0.1, 0.2, 0.3, 0.4)
KAPPA = 0.41
HEIGHT_RATIO = 20.0
SPEED_FLOOR = 0.5
PRANDTL_TURB = 0.85
PRANDTL_JUMP = 3.0
LAMINAR_SHEAR = 0.3
LAMINAR_HEAT = 0.2
FILM_SPREAD = 0.24
FILM_FLOOR = 0.3
FRICTION = 0.5
COURANT = 6.0

ROWS = 128
COLS = 512
LANES = 128
TILES = COLS // LANES
FIELDS = 9
STRIP = 8
RING = ROWS + 16
WIDE = COLS + LANES
AHEAD = 8
VMEM_LIMIT = 24 << 20


def lane_iota(shape):
    return lax.broadcasted_iota(jnp.int32, shape, len(shape) - 1)


def film_speed(height, along, across):
    square = height * height + FILM_FLOOR * FILM_FLOOR
    inverse = lax.rsqrt(square)
    thickness = square * inverse
    moving = jnp.sqrt(along * along + across * across)
    return moving * inverse + thickness * lax.rsqrt(thickness)


def halo_tile(east, west, field):
    lane = lane_iota(east.shape)
    return jnp.where(
        lane < LANES // 2,
        pltpu.roll(east, (LANES - 4 * field) % LANES, 1),
        pltpu.roll(west, (LANES - 4 - 4 * field) % LANES, 1),
    )


def sides(core, chip):
    even = lax.rem(lax.axis_index("gas"), 2) == 0
    return jnp.where(even, core, chip), jnp.where(even, chip, core)


def sample(gas, field, rows, cols):
    value = LAYER_WEIGHTS[0] * gas[field, 0, rows, cols]
    for layer in range(1, 4):
        value = value + LAYER_WEIGHTS[layer] * gas[field, layer, rows, cols]
    return value


def flag_columns(flags_by_row):
    flags = flags_by_row.astype(jnp.float32)
    return jnp.transpose(jnp.concatenate([flags, flags], axis=0))


def attached_rows(columns, rows, tile):
    count = columns[rows, tile : tile + 1]
    lane = lane_iota((count.shape[0], LANES)).astype(jnp.float32)
    return jnp.where(lane < count, 1.0, 0.0)


def edges_kernel(
    gas_hbm,
    flags_hbm,
    film_hbm,
    deposit_hbm,
    gas_ring,
    to_north,
    to_south,
    core_pack,
    chip_pack,
    peak_hbm,
    film,
    gas,
    deposit,
    flags,
    peak,
    sems,
):
    pairs = [(flags_hbm, flags), (deposit_hbm, deposit)]
    pairs += [(film_hbm.at[field], film.at[field]) for field in range(4)]
    pairs += [(gas_hbm.at[field], gas.at[field]) for field in range(3)]
    copies = [
        pltpu.make_async_copy(source, target, sems.at[index])
        for index, (source, target) in enumerate(pairs)
    ]
    for copy in copies:
        copy.start()
    tiles = [slice(tile * LANES, (tile + 1) * LANES) for tile in range(TILES)]
    every = slice(0, ROWS)
    even = lax.rem(lax.axis_index("gas"), 2) == 0
    lane = lane_iota((ROWS, LANES))

    def send(field, value_of, fresh=False):
        target = slice(4 * field, 4 * field + 4)
        for tile, cols in enumerate(tiles):
            to_north[target, cols] = value_of(slice(0, 4), tile)
            to_south[target, cols] = value_of(slice(ROWS - 4, ROWS), tile)
        west = value_of(every, 0)
        if field:
            west = pltpu.roll(west, 4 * field, 1)
        east = pltpu.roll(value_of(every, TILES - 1), 4 * field + 4, 1)
        here = (lane >= 4 * field) & (lane < 4 * field + 4)
        for pack, value in (
            (core_pack, jnp.where(even, east, west)),
            (chip_pack, jnp.where(even, west, east)),
        ):
            old = jnp.zeros_like(value) if fresh else pack[...]
            pack[...] = jnp.where(here, value, old)

    copies[0].wait()
    columns = flag_columns(flags[...])
    send(8, lambda rows, tile: attached_rows(columns, rows, tile), True)
    copies[1].wait()
    send(7, lambda rows, tile: deposit[rows, tiles[tile]])
    for field in range(4):
        copies[2 + field].wait()
        send(field, lambda rows, tile, f=field: film[f, rows, tiles[tile]])
        if field == 2:
            best = jnp.zeros((STRIP, LANES), jnp.float32)
            for cols in tiles:
                speed = film_speed(film[0, :, cols], film[1, :, cols], film[2, :, cols])
                for row in range(0, ROWS, STRIP):
                    best = jnp.maximum(best, speed[row : row + STRIP])
            peak[...] = jnp.broadcast_to(jnp.max(best, keepdims=True), (ROWS, LANES))
            leaving = pltpu.make_async_copy(peak, peak_hbm, sems.at[9])
            leaving.start()
    for field in range(3):
        copies[6 + field].wait()
        for tile, cols in enumerate(tiles):
            gas_ring[field, tile, AHEAD : AHEAD + ROWS, :] = sample(
                gas, field, every, cols
            )
        send(
            4 + field,
            lambda rows, tile, f=field: gas_ring[
                f, tile, AHEAD + rows.start : AHEAD + rows.stop, :
            ],
        )
    leaving.wait()


def even_wall():
    return lax.rem(lax.axis_index("wall"), 2) == 0


def corners_kernel(core, chip, north_in, south_in, near, far):
    even = even_wall()
    north, south = north_in[:, 0:COLS], south_in[:, 0:COLS]
    near[:, 0:COLS] = jnp.where(even, south, north)
    far[:, 0:COLS] = jnp.where(even, north, south)
    top, bottom = slice(0, 8), slice(ROWS - 8, ROWS)
    upper = sides(core[top, :], chip[top, :])
    lower = sides(core[bottom, :], chip[bottom, :])
    for field in range(FIELDS):
        target = slice(4 * field, 4 * field + 4)
        north = halo_tile(*upper, field)[0:4]
        south = halo_tile(*lower, field)[4:8]
        near[target, COLS:WIDE] = jnp.where(even, south, north)
        far[target, COLS:WIDE] = jnp.where(even, north, south)


def shifted_lanes(tiles):
    lane = lane_iota(tiles[0].shape)
    plus = [pltpu.roll(t, 1, 1) for t in tiles]
    minus = [pltpu.roll(t, LANES - 1, 1) for t in tiles]
    count = len(tiles)
    west = [jnp.where(lane == 0, plus[i - 1], plus[i]) for i in range(count)]
    east = [
        jnp.where(lane == LANES - 1, minus[(i + 1) % count], minus[i])
        for i in range(count)
    ]
    return west, east


def wall_forcing(filtered, film_heat, attached):
    along, across, gas_heat = filtered
    contrast = gas_heat - film_heat
    on_wall = attached > 0.5
    square = along * along + across * across + SPEED_FLOOR * SPEED_FLOOR
    speed = square * lax.rsqrt(square)
    height = HEIGHT_RATIO * speed
    scaled = height * lax.rsqrt(height)
    uplus = jnp.log(1.0 + KAPPA * scaled) * (1.0 / KAPPA) + 7.8 * (
        1.0
        - jnp.exp(scaled * (-1.0 / 11.0))
        - scaled * (1.0 / 11.0) * jnp.exp(scaled * (-1.0 / 3.0))
    )
    factor = jnp.where(on_wall, speed / (uplus * uplus), LAMINAR_SHEAR)
    heat = jnp.where(
        on_wall, speed / (PRANDTL_TURB * uplus + PRANDTL_JUMP), LAMINAR_HEAT
    )
    return factor * along, factor * across, heat * contrast


def inside_kernel(
    gas_in,
    film_hbm,
    flags_hbm,
    deposit_hbm,
    core,
    chip,
    ring,
    spray,
    force,
    attached,
    flags,
    sems,
):
    del gas_in
    count = TILES + 1
    inner = slice(8, 8 + ROWS)
    flags_copy = pltpu.make_async_copy(flags_hbm, flags, sems.at[5, 0])
    flags_copy.start()
    arriving = {}
    for field in (3, 0, 1, 2, 4):
        arriving[field] = []
        for tile in range(TILES):
            cols = slice(tile * LANES, (tile + 1) * LANES)
            if field < 4:
                source, target = film_hbm.at[field, :, cols], ring.at[field, tile, inner]
            else:
                source, target = deposit_hbm.at[:, cols], spray.at[tile]
            copy = pltpu.make_async_copy(source, target, sems.at[field, tile])
            copy.start()
            arriving[field].append(copy)

    east, west = sides(core[...], chip[...])
    for field in range(4):
        ring[field, TILES, inner, :] = halo_tile(east, west, field)
    for field in range(3):
        force[field, TILES, AHEAD : AHEAD + ROWS, :] = halo_tile(east, west, 4 + field)
    spray[TILES] = halo_tile(east, west, 7)
    attached[TILES, 0:ROWS, :] = halo_tile(east, west, 8)
    flags_copy.wait()
    columns = flag_columns(flags[...])
    for tile in range(TILES):
        attached[tile, 0:ROWS, :] = attached_rows(columns, slice(0, ROWS), tile)
    for copy in arriving[3]:
        copy.wait()

    def forcing_rows(index, carry):
        row = 1 + 8 * index
        here = pl.ds(row, STRIP)
        filtered = []
        for field in range(3):
            summed = [
                force[field, t, pl.ds(row + AHEAD - 1, STRIP), :]
                + force[field, t, pl.ds(row + AHEAD, STRIP), :]
                + force[field, t, pl.ds(row + AHEAD + 1, STRIP), :]
                for t in range(count)
            ]
            west, east = shifted_lanes(summed)
            filtered.append(
                [(west[t] + summed[t] + east[t]) * (1.0 / 9.0) for t in range(count)]
            )
        for t in range(count):
            result = wall_forcing(
                [filtered[f][t] for f in range(3)],
                ring[3, t, pl.ds(row + 8, STRIP), :],
                attached[t, here, :],
            )
            for field in range(3):
                force[field, t, here, :] = result[field]
        return carry

    grouped(4, 16, forcing_rows, 0)
    for field in (0, 1, 2, 4):
        for copy in arriving[field]:
            copy.wait()


def film_kernel(
    owner_map,
    ring_in,
    spray,
    force_in,
    near_sent,
    far_sent,
    near,
    far,
    peaks,
    out,
    ring,
    stack,
    ring_a,
    ring_b,
    force,
):
    del ring_in
    count = TILES + 1
    wall = lax.axis_index("wall")
    step = COURANT / jnp.max(peaks[...])
    inner = slice(8, 8 + ROWS)
    above, below = slice(4, 8), slice(8 + ROWS, 12 + ROWS)

    even = even_wall()

    def pair(field, cols, close, distant):
        rows = slice(4 * field, 4 * field + 4)
        one, two = close[rows, cols], distant[rows, cols]
        return jnp.where(even, two, one), jnp.where(even, one, two)

    for tile in range(count):
        cols = slice(tile * LANES, (tile + 1) * LANES)
        arrived = [pair(field, cols, near, far) for field in range(FIELDS)]
        for field in range(4):
            ring[field, tile, above, :], ring[field, tile, below, :] = arrived[field]
        force[3, tile, above, :] = step * arrived[7][0]
        force[3, tile, inner, :] = step * spray[tile]
        force[3, tile, below, :] = step * arrived[7][1]
        for index, field in enumerate((4, 5, 6, 3, 8)):
            own = pair(field, cols, near_sent, far_sent)
            stack[index, tile, 0:4, :] = arrived[field][0]
            stack[index, tile, 4:8, :] = own[0]
            stack[index, tile, 8:12, :] = own[1]
            stack[index, tile, 12:16, :] = arrived[field][1]

    def scale_rows(index, carry):
        row = 1 + 8 * index
        for field in range(3):
            for t in range(count):
                force[field, t, pl.ds(row + 8, STRIP), :] = (
                    step * force_in[field, t, pl.ds(row, STRIP), :]
                )
        return carry

    grouped(4, 16, scale_rows, 0)
    for start, first, target in ((1, 0, 5), (8, 3, 135)):
        filtered = []
        for field in range(3):
            summed = [
                stack[field, t, start - 1 : start - 1 + STRIP, :]
                + stack[field, t, start : start + STRIP, :]
                + stack[field, t, start + 1 : start + 1 + STRIP, :]
                for t in range(count)
            ]
            west, east = shifted_lanes(summed)
            filtered.append(
                [(west[t] + summed[t] + east[t]) * (1.0 / 9.0) for t in range(count)]
            )
        for t in range(count):
            rows = slice(start, start + STRIP)
            result = wall_forcing(
                [filtered[f][t] for f in range(3)], stack[3, t, rows, :], stack[4, t, rows, :]
            )
            for field in range(3):
                force[field, t, target : target + 4, :] = (
                    step * result[field][first : first + 4]
                )

    half = 0.5 * step

    def advance(load, row):
        here = pl.ds(row, STRIP)
        centre, wests, easts, norths, souths = [], [], [], [], []
        for field in range(4):
            middle = [load(field, t, here) for t in range(count)]
            north = [load(field, t, pl.ds(row - 1, STRIP)) for t in range(count)]
            south = [load(field, t, pl.ds(row + 1, STRIP)) for t in range(count)]
            west, east = shifted_lanes(middle)
            centre.append(middle)
            wests.append(west)
            easts.append(east)
            norths.append(north)
            souths.append(south)
        news = []
        keep = 1.0 - 4.0 * FILM_SPREAD
        for t in range(count):
            mixed = [
                FILM_SPREAD
                * ((norths[f][t] + souths[f][t]) + (wests[f][t] + easts[f][t]))
                for f in range(4)
            ]
            height = centre[0][t]
            inverse = lax.rsqrt(height * height + FILM_FLOOR * FILM_FLOOR)
            keep_moving = keep - (FRICTION * step) * inverse
            slope = half * height
            height_new = (
                keep * height
                + mixed[0]
                + force[3, t, here, :]
                - half * ((easts[1][t] - wests[1][t]) + (souths[2][t] - norths[2][t]))
            )
            along_new = (
                keep_moving * centre[1][t]
                + mixed[1]
                + force[0, t, here, :]
                - slope * (easts[0][t] - wests[0][t])
            )
            across_new = (
                keep_moving * centre[2][t]
                + mixed[2]
                + force[1, t, here, :]
                - slope * (souths[0][t] - norths[0][t])
            )
            heat_new = (
                keep * centre[3][t] + mixed[3] + force[2, t, here, :] * inverse
            )
            news.append((height_new, along_new, across_new, heat_new))
        return news

    def middle_rows(source, target):
        def body(index, carry):
            row = 4 + 8 * index
            news = advance(source, row)
            for t in range(count):
                for field in range(4):
                    target[field, t, pl.ds(row, STRIP), :] = news[t][field]
            return carry

        grouped(17, 17, body, 0)

    def load_from(source):
        return lambda field, t, rows: source[field, t, rows, :]

    middle_rows(load_from(ring), ring_a)
    middle_rows(load_from(ring_a), ring_b)
    middle_rows(load_from(ring_b), ring_a)

    def last_rows(index, best):
        row = pl.multiple_of(8 + 8 * index, 8)
        news = advance(load_from(ring_a), row)
        place = owner_map[wall, index]
        for t in range(TILES):
            for field in range(4):
                out[place, field * TILES + t] = news[t][field]
            best = jnp.maximum(best, film_speed(*news[t][:3]))
        return best

    best = grouped(16, 16, last_rows, jnp.zeros((STRIP, LANES), jnp.float32))
    top = jnp.broadcast_to(step * jnp.max(best, keepdims=True), (STRIP, LANES))
    for owner in range(ROWS // STRIP):
        out[owner, 4 * TILES] = top


def band_peak_kernel(pieces, peak):
    best = pieces[0, 4 * TILES]
    for source in range(1, pieces.shape[0]):
        best = jnp.maximum(best, pieces[source, 4 * TILES])
    peak[...] = best


def strips_kernel(pieces, out):
    first = pl.program_id(0) * TILES
    for source in range(pieces.shape[0]):
        for t in range(TILES):
            start = source * COLS + t * LANES
            out[0, :, start : start + LANES] = pieces[source, first + t]


def grouped(unroll, total, body, carry):
    whole = total // unroll

    def many(index, carry):
        for k in range(unroll):
            carry = body(index * unroll + k, carry)
        return carry

    carry = lax.fori_loop(0, whole, many, carry)
    for index in range(whole * unroll, total):
        carry = body(index, carry)
    return carry


def in_hbm(*arrays):
    return [pltpu.with_memory_space_constraint(a, pltpu.HBM) for a in arrays]


def vmem(count):
    return [pl.BlockSpec(memory_space=pltpu.VMEM)] * count


def shape(*dims):
    return jax.ShapeDtypeStruct(dims, jnp.float32)


def coupling_step(gas_state, wall_flags, film_state, deposit, owner_map):
    params = pltpu.CompilerParams(vmem_limit_bytes=VMEM_LIMIT)
    tail = pltpu.CompilerParams(vmem_limit_bytes=8 << 20)
    flags = jnp.transpose(wall_flags)
    gas_ring, north_main, south_main, core_pack, chip_pack, peak = pl.pallas_call(
        edges_kernel,
        out_shape=(
            shape(3, TILES + 1, RING, LANES),
            shape(4 * FIELDS, WIDE),
            shape(4 * FIELDS, WIDE),
            shape(ROWS, LANES),
            shape(ROWS, LANES),
            shape(ROWS, LANES),
        ),
        in_specs=[pl.BlockSpec(memory_space=pltpu.HBM)] * 4,
        out_specs=(*vmem(5), pl.BlockSpec(memory_space=pltpu.HBM)),
        scratch_shapes=[
            pltpu.VMEM((4, ROWS, COLS), jnp.float32),
            pltpu.VMEM((3, 4, ROWS, COLS), jnp.float32),
            pltpu.VMEM((ROWS, COLS), jnp.float32),
            pltpu.VMEM((TILES, ROWS), jnp.int32),
            pltpu.VMEM((ROWS, LANES), jnp.float32),
            pltpu.SemaphoreType.DMA((10,)),
        ],
        compiler_params=pltpu.CompilerParams(vmem_limit_bytes=VMEM_LIMIT),
        name="edges",
    )(*in_hbm(gas_state, flags, film_state, deposit))

    walls, gases = lax.axis_size("wall"), lax.axis_size("gas")
    partner = [(i, i ^ 1) for i in range(gases)]
    outer = [(i, (i + 1) % gases if i % 2 else (i - 1) % gases) for i in range(gases)]
    chip_side = lax.ppermute(chip_pack, "gas", outer)
    core_side = lax.ppermute(core_pack, "gas", partner)
    both = ("wall", "gas")
    peaks = lax.all_to_all(peak, both, split_axis=0, concat_axis=0, tiled=True)
    near, far = pl.pallas_call(
        corners_kernel,
        out_shape=(shape(4 * FIELDS, WIDE), shape(4 * FIELDS, WIDE)),
        in_specs=vmem(4),
        out_specs=tuple(vmem(2)),
        compiler_params=params,
        name="corners",
    )(core_side, chip_side, north_main, south_main)
    close = [(i, i ^ 1) for i in range(walls)]
    distant = [(i, (i + 1) % walls if i % 2 else (i - 1) % walls) for i in range(walls)]
    from_near = lax.ppermute(near, "wall", close)
    from_far = lax.ppermute(far, "wall", distant)

    ring_shape = (4, TILES + 1, RING, LANES)
    ring, spray, force = pl.pallas_call(
        inside_kernel,
        out_shape=(
            shape(*ring_shape),
            shape(TILES + 1, ROWS, LANES),
            shape(3, *ring_shape[1:]),
        ),
        in_specs=vmem(1) + [pl.BlockSpec(memory_space=pltpu.HBM)] * 3 + vmem(2),
        out_specs=tuple(vmem(3)),
        input_output_aliases={0: 2},
        scratch_shapes=[
            pltpu.VMEM(ring_shape[1:], jnp.float32),
            pltpu.VMEM((TILES, ROWS), jnp.int32),
            pltpu.SemaphoreType.DMA((6, TILES)),
        ],
        compiler_params=params,
        cost_estimate=pl.CostEstimate(
            flops=20 << 20, bytes_accessed=8 << 20, transcendentals=1 << 19
        ),
        name="inside",
    )(gas_ring, *in_hbm(film_state, flags, deposit), core_side, chip_side)
    pieces, _ = pl.pallas_call(
        film_kernel,
        out_shape=(shape(gases, 4 * TILES + 1, STRIP, LANES), shape(*ring_shape)),
        in_specs=[pl.BlockSpec(memory_space=pltpu.SMEM)] + vmem(8),
        out_specs=tuple(vmem(2)),
        input_output_aliases={1: 1},
        scratch_shapes=[
            pltpu.VMEM((5, TILES + 1, 24, LANES), jnp.float32),
            pltpu.VMEM(ring_shape, jnp.float32),
            pltpu.VMEM(ring_shape, jnp.float32),
            pltpu.VMEM(ring_shape, jnp.float32),
        ],
        compiler_params=params,
        name="film",
    )(
        owner_map,
        ring,
        spray,
        force,
        near,
        far,
        from_near,
        from_far,
        peaks,
    )
    pieces = lax.all_to_all(pieces, "gas", split_axis=0, concat_axis=0, tiled=True)
    band_peak = pl.pallas_call(
        band_peak_kernel,
        out_shape=shape(STRIP, LANES),
        in_specs=vmem(1),
        out_specs=vmem(1)[0],
        compiler_params=tail,
        name="band_peak",
    )(pieces)
    cfl = jnp.max(
        lax.all_to_all(band_peak, "wall", split_axis=0, concat_axis=0, tiled=True)
    )
    film_out = pl.pallas_call(
        strips_kernel,
        out_shape=shape(4, STRIP, gases * COLS),
        grid=(4,),
        in_specs=vmem(1),
        compiler_params=tail,
        out_specs=pl.BlockSpec((1, STRIP, gases * COLS), lambda i: (i, 0, 0)),
        cost_estimate=pl.CostEstimate(
            flops=0, bytes_accessed=2 << 20, transcendentals=0
        ),
        name="strips",
    )(pieces)
    return film_out, cfl


def solution(mesh):
    return jax.shard_map(
        coupling_step,
        mesh=mesh,
        in_specs=(
            P(None, None, "wall", "gas"),
            P("wall", "gas"),
            P(None, "wall", "gas"),
            P("wall", "gas"),
            P(),
        ),
        out_specs=(P(None, ("wall", "gas"), None), P()),
        check_vma=False,
    )
```

```python
import jax
import jax.numpy as jnp
from jax import lax
from jax.experimental import pallas as pl
from jax.experimental.pallas import tpu as pltpu
from jax.sharding import PartitionSpec as P


LAYER_WEIGHTS = (0.1, 0.2, 0.3, 0.4)
KAPPA = 0.41
HEIGHT_RATIO = 20.0
SPEED_FLOOR = 0.5
PRANDTL_TURB = 0.85
PRANDTL_JUMP = 3.0
LAMINAR_SHEAR = 0.3
LAMINAR_HEAT = 0.2
FILM_SPREAD = 0.24
FILM_FLOOR = 0.3
FRICTION = 0.5
COURANT = 6.0

ROWS = 128
COLS = 512
LANES = 128
TILES = COLS // LANES
FIELDS = 9
STRIP = 8
RING = ROWS + 16
WIDE = COLS + LANES
AHEAD = 8
VMEM_LIMIT = 24 << 20


def lane_iota(shape):
    return lax.broadcasted_iota(jnp.int32, shape, len(shape) - 1)


def film_speed(height, along, across):
    square = height * height + FILM_FLOOR * FILM_FLOOR
    inverse = lax.rsqrt(square)
    thickness = square * inverse
    moving = jnp.sqrt(along * along + across * across)
    return moving * inverse + thickness * lax.rsqrt(thickness)


def halo_tile(east, west, field):
    lane = lane_iota(east.shape)
    return jnp.where(
        lane < LANES // 2,
        pltpu.roll(east, (LANES - 4 * field) % LANES, 1),
        pltpu.roll(west, (LANES - 4 - 4 * field) % LANES, 1),
    )


def sides(core, chip):
    even = lax.rem(lax.axis_index("gas"), 2) == 0
    return jnp.where(even, core, chip), jnp.where(even, chip, core)


def sample(gas, field, rows, cols):
    value = LAYER_WEIGHTS[0] * gas[field, 0, rows, cols]
    for layer in range(1, 4):
        value = value + LAYER_WEIGHTS[layer] * gas[field, layer, rows, cols]
    return value


def flag_columns(flags_by_row):
    flags = flags_by_row.astype(jnp.float32)
    return jnp.transpose(jnp.concatenate([flags, flags], axis=0))


def attached_rows(columns, rows, tile):
    count = columns[rows, tile : tile + 1]
    lane = lane_iota((count.shape[0], LANES)).astype(jnp.float32)
    return jnp.where(lane < count, 1.0, 0.0)


def edges_kernel(
    gas_hbm,
    flags_hbm,
    film_hbm,
    deposit_hbm,
    gas_ring,
    to_north,
    to_south,
    core_pack,
    chip_pack,
    peak_hbm,
    film,
    gas,
    deposit,
    flags,
    peak,
    sems,
):
    pairs = [(flags_hbm, flags), (deposit_hbm, deposit)]
    pairs += [(film_hbm.at[field], film.at[field]) for field in range(4)]
    pairs += [(gas_hbm.at[field], gas.at[field]) for field in range(3)]
    copies = [
        pltpu.make_async_copy(source, target, sems.at[index])
        for index, (source, target) in enumerate(pairs)
    ]
    for copy in copies:
        copy.start()
    tiles = [slice(tile * LANES, (tile + 1) * LANES) for tile in range(TILES)]
    every = slice(0, ROWS)
    even = lax.rem(lax.axis_index("gas"), 2) == 0
    lane = lane_iota((ROWS, LANES))

    def send(field, value_of, fresh=False):
        target = slice(4 * field, 4 * field + 4)
        for tile, cols in enumerate(tiles):
            to_north[target, cols] = value_of(slice(0, 4), tile)
            to_south[target, cols] = value_of(slice(ROWS - 4, ROWS), tile)
        west = value_of(every, 0)
        if field:
            west = pltpu.roll(west, 4 * field, 1)
        east = pltpu.roll(value_of(every, TILES - 1), 4 * field + 4, 1)
        here = (lane >= 4 * field) & (lane < 4 * field + 4)
        for pack, value in (
            (core_pack, jnp.where(even, east, west)),
            (chip_pack, jnp.where(even, west, east)),
        ):
            old = jnp.zeros_like(value) if fresh else pack[...]
            pack[...] = jnp.where(here, value, old)

    copies[0].wait()
    columns = flag_columns(flags[...])
    send(8, lambda rows, tile: attached_rows(columns, rows, tile), True)
    copies[1].wait()
    send(7, lambda rows, tile: deposit[rows, tiles[tile]])
    for field in range(4):
        copies[2 + field].wait()
        send(field, lambda rows, tile, f=field: film[f, rows, tiles[tile]])
        if field == 2:
            best = jnp.zeros((STRIP, LANES), jnp.float32)
            for cols in tiles:
                speed = film_speed(film[0, :, cols], film[1, :, cols], film[2, :, cols])
                for row in range(0, ROWS, STRIP):
                    best = jnp.maximum(best, speed[row : row + STRIP])
            peak[...] = jnp.broadcast_to(jnp.max(best, keepdims=True), (ROWS, LANES))
            leaving = pltpu.make_async_copy(peak, peak_hbm, sems.at[9])
            leaving.start()
    for field in range(3):
        copies[6 + field].wait()
        for tile, cols in enumerate(tiles):
            gas_ring[field, tile, AHEAD : AHEAD + ROWS, :] = sample(
                gas, field, every, cols
            )
        send(
            4 + field,
            lambda rows, tile, f=field: gas_ring[
                f, tile, AHEAD + rows.start : AHEAD + rows.stop, :
            ],
        )
    leaving.wait()


def even_wall():
    return lax.rem(lax.axis_index("wall"), 2) == 0


def corners_kernel(core, chip, north_in, south_in, near, far):
    even = even_wall()
    north, south = north_in[:, 0:COLS], south_in[:, 0:COLS]
    near[:, 0:COLS] = jnp.where(even, south, north)
    far[:, 0:COLS] = jnp.where(even, north, south)
    top, bottom = slice(0, 8), slice(ROWS - 8, ROWS)
    upper = sides(core[top, :], chip[top, :])
    lower = sides(core[bottom, :], chip[bottom, :])
    for field in range(FIELDS):
        target = slice(4 * field, 4 * field + 4)
        north = halo_tile(*upper, field)[0:4]
        south = halo_tile(*lower, field)[4:8]
        near[target, COLS:WIDE] = jnp.where(even, south, north)
        far[target, COLS:WIDE] = jnp.where(even, north, south)


def shifted_lanes(tiles):
    lane = lane_iota(tiles[0].shape)
    plus = [pltpu.roll(t, 1, 1) for t in tiles]
    minus = [pltpu.roll(t, LANES - 1, 1) for t in tiles]
    count = len(tiles)
    west = [jnp.where(lane == 0, plus[i - 1], plus[i]) for i in range(count)]
    east = [
        jnp.where(lane == LANES - 1, minus[(i + 1) % count], minus[i])
        for i in range(count)
    ]
    return west, east


def wall_forcing(filtered, film_heat, attached):
    along, across, gas_heat = filtered
    contrast = gas_heat - film_heat
    on_wall = attached > 0.5
    square = along * along + across * across + SPEED_FLOOR * SPEED_FLOOR
    speed = square * lax.rsqrt(square)
    height = HEIGHT_RATIO * speed
    scaled = height * lax.rsqrt(height)
    uplus = jnp.log(1.0 + KAPPA * scaled) * (1.0 / KAPPA) + 7.8 * (
        1.0
        - jnp.exp(scaled * (-1.0 / 11.0))
        - scaled * (1.0 / 11.0) * jnp.exp(scaled * (-1.0 / 3.0))
    )
    factor = jnp.where(on_wall, speed / (uplus * uplus), LAMINAR_SHEAR)
    heat = jnp.where(
        on_wall, speed / (PRANDTL_TURB * uplus + PRANDTL_JUMP), LAMINAR_HEAT
    )
    return factor * along, factor * across, heat * contrast


def inside_kernel(
    gas_in,
    film_hbm,
    flags_hbm,
    deposit_hbm,
    core,
    chip,
    ring,
    spray,
    force,
    attached,
    flags,
    sems,
):
    del gas_in
    count = TILES + 1
    inner = slice(8, 8 + ROWS)
    flags_copy = pltpu.make_async_copy(flags_hbm, flags, sems.at[5, 0])
    flags_copy.start()
    arriving = {}
    for field in (3, 0, 1, 2, 4):
        arriving[field] = []
        for tile in range(TILES):
            cols = slice(tile * LANES, (tile + 1) * LANES)
            if field < 4:
                source, target = film_hbm.at[field, :, cols], ring.at[field, tile, inner]
            else:
                source, target = deposit_hbm.at[:, cols], spray.at[tile]
            copy = pltpu.make_async_copy(source, target, sems.at[field, tile])
            copy.start()
            arriving[field].append(copy)

    east, west = sides(core[...], chip[...])
    for field in range(4):
        ring[field, TILES, inner, :] = halo_tile(east, west, field)
    for field in range(3):
        force[field, TILES, AHEAD : AHEAD + ROWS, :] = halo_tile(east, west, 4 + field)
    spray[TILES] = halo_tile(east, west, 7)
    attached[TILES, 0:ROWS, :] = halo_tile(east, west, 8)
    flags_copy.wait()
    columns = flag_columns(flags[...])
    for tile in range(TILES):
        attached[tile, 0:ROWS, :] = attached_rows(columns, slice(0, ROWS), tile)
    for copy in arriving[3]:
        copy.wait()

    def forcing_rows(index, carry):
        row = 1 + 8 * index
        here = pl.ds(row, STRIP)
        filtered = []
        for field in range(3):
            summed = [
                force[field, t, pl.ds(row + AHEAD - 1, STRIP), :]
                + force[field, t, pl.ds(row + AHEAD, STRIP), :]
                + force[field, t, pl.ds(row + AHEAD + 1, STRIP), :]
                for t in range(count)
            ]
            west, east = shifted_lanes(summed)
            filtered.append(
                [(west[t] + summed[t] + east[t]) * (1.0 / 9.0) for t in range(count)]
            )
        for t in range(count):
            result = wall_forcing(
                [filtered[f][t] for f in range(3)],
                ring[3, t, pl.ds(row + 8, STRIP), :],
                attached[t, here, :],
            )
            for field in range(3):
                force[field, t, here, :] = result[field]
        return carry

    grouped(16, 16, forcing_rows, 0)
    for field in (0, 1, 2, 4):
        for copy in arriving[field]:
            copy.wait()


def advance(load, force, step, row):
    count = TILES + 1
    half = 0.5 * step
    here = pl.ds(row, STRIP)
    centre, wests, easts, norths, souths = [], [], [], [], []
    for field in range(4):
        middle = [load(field, t, here) for t in range(count)]
        north = [load(field, t, pl.ds(row - 1, STRIP)) for t in range(count)]
        south = [load(field, t, pl.ds(row + 1, STRIP)) for t in range(count)]
        west, east = shifted_lanes(middle)
        centre.append(middle)
        wests.append(west)
        easts.append(east)
        norths.append(north)
        souths.append(south)
    news = []
    keep = 1.0 - 4.0 * FILM_SPREAD
    for t in range(count):
        mixed = [
            FILM_SPREAD
            * ((norths[f][t] + souths[f][t]) + (wests[f][t] + easts[f][t]))
            for f in range(4)
        ]
        height = centre[0][t]
        inverse = lax.rsqrt(height * height + FILM_FLOOR * FILM_FLOOR)
        keep_moving = keep - (FRICTION * step) * inverse
        slope = half * height
        height_new = (
            keep * height
            + mixed[0]
            + force[3, t, here, :]
            - half * ((easts[1][t] - wests[1][t]) + (souths[2][t] - norths[2][t]))
        )
        along_new = (
            keep_moving * centre[1][t]
            + mixed[1]
            + force[0, t, here, :]
            - slope * (easts[0][t] - wests[0][t])
        )
        across_new = (
            keep_moving * centre[2][t]
            + mixed[2]
            + force[1, t, here, :]
            - slope * (souths[0][t] - norths[0][t])
        )
        heat_new = (
            keep * centre[3][t] + mixed[3] + force[2, t, here, :] * inverse
        )
        news.append((height_new, along_new, across_new, heat_new))
    return news


def load_from(source):
    return lambda field, t, rows: source[field, t, rows, :]


def store_rows(target, row, news):
    for t, values in enumerate(news):
        for field in range(4):
            target[field, t, pl.ds(row, STRIP), :] = values[field]


def first_kernel(ring, spray, force_in, peaks, ring_a, force):
    count = TILES + 1
    step = COURANT / jnp.max(peaks[...])
    for tile in range(count):
        force[3, tile, 8 : 8 + ROWS, :] = step * spray[tile]

    def scale_rows(index, carry):
        row = 1 + 8 * index
        for field in range(3):
            for t in range(count):
                force[field, t, pl.ds(row + 8, STRIP), :] = (
                    step * force_in[field, t, pl.ds(row, STRIP), :]
                )
        return carry

    grouped(16, 16, scale_rows, 0)
    for row in range(12, 132, STRIP):
        store_rows(ring_a, row, advance(load_from(ring), force, step, row))


def film_kernel(
    owner_map,
    ring_in,
    ring_a_in,
    force_in,
    near_sent,
    far_sent,
    near,
    far,
    peaks,
    out,
    ring,
    ring_a,
    force,
    stack,
    ring_b,
):
    del ring_in, ring_a_in, force_in
    count = TILES + 1
    wall = lax.axis_index("wall")
    step = COURANT / jnp.max(peaks[...])
    above, below = slice(4, 8), slice(8 + ROWS, 12 + ROWS)

    even = even_wall()

    def pair(field, cols, close, distant):
        rows = slice(4 * field, 4 * field + 4)
        one, two = close[rows, cols], distant[rows, cols]
        return jnp.where(even, two, one), jnp.where(even, one, two)

    for tile in range(count):
        cols = slice(tile * LANES, (tile + 1) * LANES)
        arrived = [pair(field, cols, near, far) for field in range(FIELDS)]
        for field in range(4):
            ring[field, tile, above, :], ring[field, tile, below, :] = arrived[field]
        force[3, tile, above, :] = step * arrived[7][0]
        force[3, tile, below, :] = step * arrived[7][1]
        for index, field in enumerate((4, 5, 6, 3, 8)):
            own = pair(field, cols, near_sent, far_sent)
            stack[index, tile, 0:4, :] = arrived[field][0]
            stack[index, tile, 4:8, :] = own[0]
            stack[index, tile, 8:12, :] = own[1]
            stack[index, tile, 12:16, :] = arrived[field][1]

    filtered = []
    for field in range(3):
        for t in range(count):
            for start, place in ((0, 16), (10, 20)):
                stack[field, t, place : place + 4, :] = (
                    stack[field, t, start : start + 4, :]
                    + stack[field, t, start + 1 : start + 5, :]
                    + stack[field, t, start + 2 : start + 6, :]
                )
        summed = [stack[field, t, 16:24, :] for t in range(count)]
        west, east = shifted_lanes(summed)
        filtered.append(
            [(west[t] + summed[t] + east[t]) * (1.0 / 9.0) for t in range(count)]
        )
    for t in range(count):
        for index in (3, 4):
            for start, place in ((1, 16), (11, 20)):
                stack[index, t, place : place + 4, :] = stack[index, t, start : start + 4, :]
        result = wall_forcing(
            [filtered[f][t] for f in range(3)], stack[3, t, 16:24, :], stack[4, t, 16:24, :]
        )
        for field in range(3):
            value = step * result[field]
            force[field, t, 5:9, :] = value[0:4]
            force[field, t, 135:139, :] = value[4:8]

    for row in (4, 132):
        store_rows(ring_a, row, advance(load_from(ring), force, step, row))
    for source, target in ((ring_a, ring_b), (ring_b, ring_a)):
        for row in range(4, 140, STRIP):
            store_rows(target, row, advance(load_from(source), force, step, row))

    def last_rows(index, best):
        row = pl.multiple_of(8 + 8 * index, 8)
        news = advance(load_from(ring_a), force, step, row)
        place = owner_map[wall, index]
        for t in range(TILES):
            for field in range(4):
                out[place, field * TILES + t] = news[t][field]
            best = jnp.maximum(best, film_speed(*news[t][:3]))
        return best

    best = grouped(16, 16, last_rows, jnp.zeros((STRIP, LANES), jnp.float32))
    top = jnp.broadcast_to(step * jnp.max(best, keepdims=True), (STRIP, LANES))
    for owner in range(ROWS // STRIP):
        out[owner, 4 * TILES] = top


def band_peak_kernel(pieces, peak):
    best = pieces[0, 4 * TILES]
    for source in range(1, pieces.shape[0]):
        best = jnp.maximum(best, pieces[source, 4 * TILES])
    peak[...] = best


def strips_kernel(pieces, out):
    first = pl.program_id(0) * TILES
    for source in range(pieces.shape[0]):
        for t in range(TILES):
            start = source * COLS + t * LANES
            out[0, :, start : start + LANES] = pieces[source, first + t]


def grouped(unroll, total, body, carry):
    whole = total // unroll

    def many(index, carry):
        for k in range(unroll):
            carry = body(index * unroll + k, carry)
        return carry

    carry = lax.fori_loop(0, whole, many, carry)
    for index in range(whole * unroll, total):
        carry = body(index, carry)
    return carry


def in_hbm(*arrays):
    return [pltpu.with_memory_space_constraint(a, pltpu.HBM) for a in arrays]


def vmem(count):
    return [pl.BlockSpec(memory_space=pltpu.VMEM)] * count


def shape(*dims):
    return jax.ShapeDtypeStruct(dims, jnp.float32)


def coupling_step(gas_state, wall_flags, film_state, deposit, owner_map):
    params = pltpu.CompilerParams(vmem_limit_bytes=VMEM_LIMIT)
    tail = pltpu.CompilerParams(vmem_limit_bytes=8 << 20)
    flags = jnp.transpose(wall_flags)
    gas_ring, north_main, south_main, core_pack, chip_pack, peak = pl.pallas_call(
        edges_kernel,
        out_shape=(
            shape(3, TILES + 1, RING, LANES),
            shape(4 * FIELDS, WIDE),
            shape(4 * FIELDS, WIDE),
            shape(ROWS, LANES),
            shape(ROWS, LANES),
            shape(ROWS, LANES),
        ),
        in_specs=[pl.BlockSpec(memory_space=pltpu.HBM)] * 4,
        out_specs=(*vmem(5), pl.BlockSpec(memory_space=pltpu.HBM)),
        scratch_shapes=[
            pltpu.VMEM((4, ROWS, COLS), jnp.float32),
            pltpu.VMEM((3, 4, ROWS, COLS), jnp.float32),
            pltpu.VMEM((ROWS, COLS), jnp.float32),
            pltpu.VMEM((TILES, ROWS), jnp.int32),
            pltpu.VMEM((ROWS, LANES), jnp.float32),
            pltpu.SemaphoreType.DMA((10,)),
        ],
        compiler_params=pltpu.CompilerParams(vmem_limit_bytes=VMEM_LIMIT),
        name="edges",
    )(*in_hbm(gas_state, flags, film_state, deposit))

    walls, gases = lax.axis_size("wall"), lax.axis_size("gas")
    partner = [(i, i ^ 1) for i in range(gases)]
    outer = [(i, (i + 1) % gases if i % 2 else (i - 1) % gases) for i in range(gases)]
    chip_side = lax.ppermute(chip_pack, "gas", outer)
    core_side = lax.ppermute(core_pack, "gas", partner)
    both = ("wall", "gas")
    peaks = lax.all_to_all(peak, both, split_axis=0, concat_axis=0, tiled=True)
    near, far = pl.pallas_call(
        corners_kernel,
        out_shape=(shape(4 * FIELDS, WIDE), shape(4 * FIELDS, WIDE)),
        in_specs=vmem(4),
        out_specs=tuple(vmem(2)),
        compiler_params=params,
        name="corners",
    )(core_side, chip_side, north_main, south_main)
    close = [(i, i ^ 1) for i in range(walls)]
    distant = [(i, (i + 1) % walls if i % 2 else (i - 1) % walls) for i in range(walls)]
    from_near = lax.ppermute(near, "wall", close)
    from_far = lax.ppermute(far, "wall", distant)

    ring_shape = (4, TILES + 1, RING, LANES)
    ring, spray, force = pl.pallas_call(
        inside_kernel,
        out_shape=(
            shape(*ring_shape),
            shape(TILES + 1, ROWS, LANES),
            shape(3, *ring_shape[1:]),
        ),
        in_specs=vmem(1) + [pl.BlockSpec(memory_space=pltpu.HBM)] * 3 + vmem(2),
        out_specs=tuple(vmem(3)),
        input_output_aliases={0: 2},
        scratch_shapes=[
            pltpu.VMEM(ring_shape[1:], jnp.float32),
            pltpu.VMEM((TILES, ROWS), jnp.int32),
            pltpu.SemaphoreType.DMA((6, TILES)),
        ],
        compiler_params=params,
        cost_estimate=pl.CostEstimate(
            flops=20 << 20, bytes_accessed=8 << 20, transcendentals=1 << 19
        ),
        name="inside",
    )(gas_ring, *in_hbm(film_state, flags, deposit), core_side, chip_side)
    ring_a, force = pl.pallas_call(
        first_kernel,
        out_shape=(shape(*ring_shape), shape(*ring_shape)),
        in_specs=vmem(4),
        out_specs=tuple(vmem(2)),
        compiler_params=params,
        cost_estimate=pl.CostEstimate(
            flops=20 << 20, bytes_accessed=8 << 20, transcendentals=1 << 17
        ),
        name="first",
    )(ring, spray, force, peaks)
    pieces, *_ = pl.pallas_call(
        film_kernel,
        out_shape=(shape(gases, 4 * TILES + 1, STRIP, LANES),) + (shape(*ring_shape),) * 3,
        in_specs=[pl.BlockSpec(memory_space=pltpu.SMEM)] + vmem(8),
        out_specs=tuple(vmem(4)),
        input_output_aliases={1: 1, 2: 2, 3: 3},
        scratch_shapes=[
            pltpu.VMEM((5, TILES + 1, 24, LANES), jnp.float32),
            pltpu.VMEM(ring_shape, jnp.float32),
        ],
        compiler_params=params,
        name="film",
    )(owner_map, ring, ring_a, force, near, far, from_near, from_far, peaks)
    pieces = lax.all_to_all(pieces, "gas", split_axis=0, concat_axis=0, tiled=True)
    band_peak = pl.pallas_call(
        band_peak_kernel,
        out_shape=shape(STRIP, LANES),
        in_specs=vmem(1),
        out_specs=vmem(1)[0],
        compiler_params=tail,
        name="band_peak",
    )(pieces)
    cfl = jnp.max(
        lax.all_to_all(band_peak, "wall", split_axis=0, concat_axis=0, tiled=True)
    )
    film_out = pl.pallas_call(
        strips_kernel,
        out_shape=shape(4, STRIP, gases * COLS),
        grid=(4,),
        in_specs=vmem(1),
        compiler_params=tail,
        out_specs=pl.BlockSpec((1, STRIP, gases * COLS), lambda i: (i, 0, 0)),
        cost_estimate=pl.CostEstimate(
            flops=0, bytes_accessed=2 << 20, transcendentals=0
        ),
        name="strips",
    )(pieces)
    return film_out, cfl


def solution(mesh):
    return jax.shard_map(
        coupling_step,
        mesh=mesh,
        in_specs=(
            P(None, None, "wall", "gas"),
            P("wall", "gas"),
            P(None, "wall", "gas"),
            P("wall", "gas"),
            P(),
        ),
        out_specs=(P(None, ("wall", "gas"), None), P()),
        check_vma=False,
    )
```
